128 devices in a mesh: cand: 16 (over z_lo, y, core), rel: 8 (over z_hi, x).
Axes of the slice: x: 4, y: 4, z: 4 (z_hi: 2, z_lo: 2; z = z_hi * 2 + z_lo), core: 2. Of those that a mesh axis runs over, the one named last changes fastest.
Arguments:
- source_rows: bfloat16 [262144, 512], P(('cand', 'rel')), may hold values from -24 to 24
- rel_ids: int32 [262144, 1], P(('cand', 'rel')), may hold values from 0 to 15; in each aligned block of 2048 rows (0 to 2047, 2048 to 4095, ...) at most 256 rows name the same one
- relations: bfloat16 [16, 512, 512], P('rel'), may hold values from -0.25 to 0.25
- entities: float32 [32768, 512], P(('cand', 'rel')), may hold values from -0.3 to 0.3
- pos_slot: int32 [262144], P(('cand', 'rel')), may hold values from 0 to 2047
- negatives: int32 [8, 262144, 16], P(None, ('cand', 'rel')), may hold values from 0 to 255
Outputs:
- updated_entities: float32 [32768, 512], P(('cand', 'rel'))
- source_grad: bfloat16 [262144, 512], P(('cand', 'rel'))
- relation_grad: float32 [512, 16, 512], P('cand', 'rel')
The draws below stay inside these ranges and needn't reach their ends.
Inputs may be any that keep to these rules, and one draw needn't show every extreme that they name: `rel_ids`: in each aligned block of 2048 rows (the rows of one device) no relation is named by more than 256 rows, a bound that some block reaches.
All inputs are finite; a program needn't handle non-finite values.
Results may differ from the reference program's by a relative error of at most 0.019.
Values may be sent and summed in bfloat16 or wider, within the bound.
A program may use at most 128 MiB of HBM per device.

```python
import math
import jax
import jax.numpy as jnp
import numpy as np
from jax import lax

D = 512
PART = 256
SRC_DEV = 2048
REL_DEV = 2
STOPS = 8
NEG = 16
NREL = 16
MOST = 256
SOURCES = 262144
ENTITIES = 32768
N_CAND = 16
N_REL = 8


def set_ends(drawn, stream_key, least, top_value):
    extent = drawn.shape
    place = [jax.random.randint(jax.random.fold_in(stream_key, axis), (), 0, extent[axis]) for axis in range(len(extent))]
    drawn = drawn.at[tuple(place)].set(least)
    longest = extent.index(max(extent))
    place[longest] = (place[longest] + 1) % extent[longest]
    return drawn.at[tuple(place)].set(top_value)


def with_spikes(entries, stream_key, source, target, blocks, factor):
    owner, partner = [(jnp.arange(entries.shape[axis_at]) // (entries.shape[axis_at] // blocks)).reshape([-1 if axis == axis_at else 1 for axis in range(entries.ndim)]) for axis_at in (source, target)]
    chosen = jax.random.permutation(stream_key, blocks)[partner]
    strong = (owner == chosen) | (owner == (partner + blocks // 2) % blocks)
    return jnp.where(strong, factor * entries, entries)


def levels(key, extent, cuts, low, high):
    level, own = 1.0, jax.random.fold_in(key, 6)
    for position, shards_of in cuts:
        heights = jnp.exp(jax.random.uniform(jax.random.fold_in(own, position), (shards_of,), jnp.float32, low / len(cuts), high / len(cuts)))
        level = level * jnp.repeat(heights, extent[position] // shards_of).reshape([-1 if axis == position else 1 for axis in range(len(extent))])
    return level


def shared_out(own_key, own, number, rows, count, top, most, lean):
    ranking = jax.random.permutation(own_key, count)
    crowded, ordinary = portions_of(count, rows * top, most, lean, True), portions_of(count, rows * top, most, lean, False)
    places = jnp.arange(count)

    def named(tallies, rotation):
        used = int((tallies > 0).sum())
        fixed = max(1, used // 4)
        shifted = fixed + (places - fixed + rotation * (used - fixed)) % max(1, count - fixed)
        return jnp.zeros((count,), jnp.int32).at[ranking[jnp.where(places < fixed, places, shifted)]].set(jnp.asarray(tallies, jnp.int32))

    tallies = jnp.where(number % 4 == 0, named(crowded, number // 4), named(ordinary, number - number // 4 - 1))
    mixed = jax.random.permutation(jax.random.fold_in(own, 3), count)
    donor, receiver = mixed[0:count // 2 * 2:2], mixed[1:count // 2 * 2:2]
    slack = jnp.minimum(tallies[donor] - 1, most - tallies[receiver]) // 2
    slack = jnp.where((donor == ranking[0]) | (receiver == ranking[0]) | (tallies[receiver] == 0), 0, jnp.maximum(slack, 0))
    shifted = jax.random.randint(jax.random.fold_in(own, 4), (count // 2,), 0, 1 << 20) % (slack + 1)
    tallies = tallies.at[donor].add(-shifted).at[receiver].add(shifted)
    items = jnp.searchsorted(jnp.cumsum(tallies), jnp.arange(rows * top), side="right").astype(jnp.int32)
    grid = items.reshape(top, rows).T
    grid = grid[jax.random.permutation(jax.random.fold_in(own, 1), rows)]
    rotation = jax.random.randint(jax.random.fold_in(own, 2), (rows, 1), 0, top)
    return jnp.take_along_axis(grid, (jnp.arange(top)[None, :] + rotation) % top, axis=1)


def portions_of(number_of, total, reach, skew, full):
    weights = [(1 << 20) // math.isqrt(rank ** skew) + 1 for rank in range(1, number_of + 1)]
    largest = reach if full else min(reach, max(-(-total // number_of), total * weights[0] // sum(weights)))
    least = 1 if total - largest >= number_of - 1 else 0
    holding, rest = [largest] + [least] * (number_of - 1), total - largest - least * (number_of - 1)
    while rest > 0:
        movable = [i for i in range(1, number_of) if holding[i] < largest] or [i for i in range(1, number_of) if holding[i] < reach]
        pool, budget = sum([weights[i] for i in movable]), rest
        for i in movable:
            extra = min(reach - holding[i], max(1, budget * weights[i] // pool), rest)
            holding[i] = holding[i] + extra
            rest = rest - extra
    return np.array(holding)


def gaussian(rng, dims, deviation, reach, shards=(), kind=jnp.bfloat16):
    array = jax.random.normal(rng, dims, jnp.float32) * deviation
    if len(shards) > 0:
        array = levels(rng, dims, shards, -0.22, 0.18) * array
    return jnp.clip(array, min=-reach, max=reach).astype(kind)


def gaussian_with(key, shape, scale, most, pieces, heavy, kind=jnp.bfloat16):
    entries = scale * jax.random.normal(key, shape, jnp.float32)
    if pieces:
        entries = entries * levels(key, shape, pieces, -0.22, 0.18)
    return jnp.clip(with_spikes(entries, jax.random.fold_in(key, 3), *heavy), -most, most).astype(kind)


def setup_inputs(seed: int = 0) -> dict:
    seeds = jax.random.split(jax.random.key(seed), 7)
    source_rows = gaussian_with(seeds[0], (SOURCES, D), 1.0, 24.0, ((0, 128),), (0, 1, 128, 5.5))
    rel_ids_keys = jax.random.split(jax.random.fold_in(seeds[1], 1), SOURCES // SRC_DEV)
    rel_ids_turns = jax.random.permutation(jax.random.fold_in(seeds[1], 3), SOURCES // SRC_DEV)
    rel_ids = jax.vmap(lambda own, number: shared_out(jax.random.fold_in(seeds[1], 2), own, number, SRC_DEV, NREL, 1, MOST, 2))(rel_ids_keys, rel_ids_turns).reshape((SOURCES, 1))
    relations = gaussian(seeds[2], (NREL, D, D), D ** -0.5, 0.25, ((0, 8),))
    entities = gaussian(seeds[3], (ENTITIES, D), 0.05, 0.3, ((0, 128),), jnp.float32)
    pos_slot = set_ends(jax.random.randint(seeds[4], (SOURCES,), 0, STOPS * PART), jax.random.fold_in(seeds[4], 1), 0, (STOPS * PART) - 1).astype(jnp.int32)
    negatives = set_ends(jax.random.randint(seeds[5], (STOPS, SOURCES, NEG), 0, PART), jax.random.fold_in(seeds[5], 1), 0, PART - 1).astype(jnp.int32)
    return dict(source_rows=source_rows, rel_ids=rel_ids, relations=relations, entities=entities, pos_slot=pos_slot, negatives=negatives)


learn_rate = 0.005


def reference(source_rows, rel_ids, relations, entities, pos_slot, negatives):
    blocks = N_CAND * N_REL
    width = D
    nrel = REL_DEV * N_REL
    most = 2 * SRC_DEV // nrel
    ids = rel_ids[:, 0].reshape(blocks, SRC_DEV)
    onehot = (ids[:, :, None] == jnp.arange(nrel, dtype=jnp.int32)[None, None, :]).astype(jnp.int32)
    rank = jnp.cumsum(onehot, axis=1) - onehot
    slot = (ids * most + jnp.sum(rank * onehot, axis=2)).astype(jnp.int32)
    owner = jnp.broadcast_to(jnp.arange(blocks, dtype=jnp.int32)[:, None], slot.shape)
    rows = source_rows.reshape(blocks, SRC_DEV, width)
    sent = jnp.zeros((blocks, nrel * most, width), source_rows.dtype).at[owner, slot].set(rows)
    sent = sent.reshape(blocks, nrel, most, width)

    def forward(k):
        part_rows = sent[:, k].reshape(blocks * most, width)
        return jnp.dot(part_rows, relations[k], preferred_element_type=jnp.float32).astype(jnp.bfloat16)

    q_slots = lax.map(forward, jnp.arange(nrel))
    q_slots = jnp.transpose(q_slots.reshape(nrel, blocks, most, width), (1, 0, 2, 3)).reshape(blocks, nrel * most, width)
    queries = q_slots[owner, slot]
    queries = queries.reshape(N_CAND, N_REL, SRC_DEV, width)
    qf = queries.astype(jnp.float32)

    state = entities.reshape(N_CAND, N_REL, PART, width)
    acc = jnp.zeros((N_CAND, N_REL, SRC_DEV, width), jnp.float32)
    columns = jnp.arange(PART, dtype=jnp.int32)
    targets = pos_slot.reshape(N_CAND, N_REL, SRC_DEV)
    for stop in range(STOPS):
        if stop > 0:
            state = jnp.roll(state, 1, axis=0)
        wide = state.astype(jnp.bfloat16)
        wf = wide.astype(jnp.float32)
        logits = jnp.einsum('cnid,cnjd->cnij', qf, wf)
        picks = negatives[stop].reshape(N_CAND, N_REL, SRC_DEV, NEG)
        counts = jnp.zeros(logits.shape, jnp.float32)
        for sample in range(NEG):
            counts = counts + (picks[..., sample][..., None] == columns).astype(jnp.float32)
        hits = (targets[..., None] == stop * PART + columns).astype(jnp.float32)
        weight = (counts * jax.nn.sigmoid(logits) - hits * jax.nn.sigmoid(-logits)).astype(jnp.bfloat16)
        weightf = weight.astype(jnp.float32)
        acc = acc + jnp.einsum('cnij,cnjd->cnid', weightf, wf)
        state = state - learn_rate * jnp.einsum('cnij,cnid->cnjd', weightf, qf)
    updated_entities = state.reshape(blocks * PART, width)

    query_grad = acc.astype(jnp.bfloat16).reshape(blocks, SRC_DEV, width)
    gq = jnp.zeros((blocks, nrel * most, width), jnp.bfloat16).at[owner, slot].set(query_grad)
    gq = gq.reshape(blocks, nrel, most, width)

    def backward(k):
        gq_rows = gq[:, k].reshape(blocks * most, width)
        src = sent[:, k].reshape(blocks * most, width)
        back = jnp.dot(gq_rows, relations[k].T, preferred_element_type=jnp.float32).astype(jnp.bfloat16)
        dmat = jnp.dot(src.T, gq_rows, preferred_element_type=jnp.float32)
        return back, dmat

    back, dmats = lax.map(backward, jnp.arange(nrel))
    back = jnp.transpose(back.reshape(nrel, blocks, most, width), (1, 0, 2, 3)).reshape(blocks, nrel * most, width)
    source_grad = back[owner, slot].reshape(blocks * SRC_DEV, width)
    relation_grad = jnp.transpose(dmats, (1, 0, 2))
    return updated_entities, source_grad, relation_grad
```

```python
import functools

import jax
import jax.numpy as jnp
from jax import lax
from jax.experimental import pallas as pl
from jax.experimental.pallas import tpu as pltpu
from jax.sharding import PartitionSpec as P

MESH = pl.DeviceIdType.MESH
BF = jnp.bfloat16
F32 = jnp.float32


class Spot:
    def __init__(self):
        cand, rel = lax.axis_index("cand"), lax.axis_index("rel")
        self.core = lax.rem(cand, 2)
        self.y = lax.rem(cand // 2, 4)
        self.zl = cand // 8
        self.x = lax.rem(rel, 4)
        self.zh = rel // 4
        self.z = self.zh * 2 + self.zl
        self.rel = rel

    def device(self, x=None, y=None, z=None, core=None):
        x = self.x if x is None else x
        y = self.y if y is None else y
        z = self.z if z is None else z
        core = self.core if core is None else core
        return ((lax.rem(z, 2) * 4 + y) * 2 + core, (z // 2) * 4 + x)


def turn(i, by):
    return lax.rem(i + by, 4)


def greet(devices):
    barrier = pltpu.get_barrier_semaphore()
    for device in devices:
        pl.semaphore_signal(barrier, inc=1, device_id=device, device_id_type=MESH)
    pl.semaphore_wait(barrier, len(devices))


class Mail:
    def __init__(self, send_sem, recv_sem):
        self.send_sem, self.recv_sem, self.count, self.sent = send_sem, recv_sem, 0, []

    def send(self, src, dst, device):
        i = self.count
        self.count += 1
        copy = pltpu.make_async_remote_copy(
            src_ref=src,
            dst_ref=dst,
            send_sem=self.send_sem.at[i],
            recv_sem=self.recv_sem.at[i],
            device_id=device,
            device_id_type=MESH,
        )
        copy.start()
        self.sent.append(copy)
        return copy

    def drain(self):
        for copy in self.sent:
            copy.wait_send()


def gather_kernel(own, out, local_sem, send_sem, recv_sem):
    at = Spot()
    mail = Mail(send_sem, recv_sem)
    left, right = at.device(x=turn(at.x, 3)), at.device(x=turn(at.x, 1))
    across = at.device(z=3 - at.z)
    partner = at.device(core=1 - at.core)
    greet([left, right, across, partner])
    here = pltpu.make_async_copy(own, out.at[at.rel], local_sem)
    here.start()
    half = own.shape[1] // 2
    start = pl.multiple_of(at.core * half, half)
    mine = pl.ds(start, half)
    first = pl.ds(start, half // 2)
    second = pl.ds(pl.multiple_of(start + half // 2, half // 2), half // 2)
    me, far = at.zh * 4, (1 - at.zh) * 4
    x0, x1, x2, x3 = at.x, turn(at.x, 1), turn(at.x, 2), turn(at.x, 3)
    own_mine = own.at[:, mine]

    def block(base, x, rows):
        return out.at[base + x, :, rows]

    to_across = mail.send(own_mine, block(me, x0, mine), across)
    to_right = mail.send(own_mine, block(me, x0, mine), right)
    to_left = mail.send(own_mine, block(me, x0, mine), left)
    to_right.wait_recv()
    on_right = mail.send(block(me, x3, first), block(me, x3, first), right)
    share = [mail.send(block(me, x3, mine), block(me, x3, mine), partner)]
    to_left.wait_recv()
    on_left = mail.send(block(me, x1, second), block(me, x1, second), left)
    share.append(mail.send(block(me, x1, mine), block(me, x1, mine), partner))
    to_across.wait_recv()
    far_right = mail.send(block(far, x0, mine), block(far, x0, mine), right)
    far_left = mail.send(block(far, x0, mine), block(far, x0, mine), left)
    share.append(mail.send(block(far, x0, mine), block(far, x0, mine), partner))
    on_right.wait_recv()
    opposite_a = mail.send(block(me, x2, first), block(me, x2, first), across)
    on_left.wait_recv()
    opposite_b = mail.send(block(me, x2, second), block(me, x2, second), across)
    share.append(mail.send(block(me, x2, mine), block(me, x2, mine), partner))
    far_right.wait_recv()
    share.append(mail.send(block(far, x3, mine), block(far, x3, mine), partner))
    far_left.wait_recv()
    share.append(mail.send(block(far, x1, mine), block(far, x1, mine), partner))
    opposite_a.wait_recv()
    opposite_b.wait_recv()
    share.append(mail.send(block(far, x2, mine), block(far, x2, mine), partner))
    for copy in share:
        copy.wait_recv()
    mail.drain()
    here.wait()


def gather_relations(relations):
    per, width, _ = relations.shape
    owners = lax.axis_size("rel")
    out = pl.pallas_call(
        gather_kernel,
        out_shape=jax.ShapeDtypeStruct((owners, per, width, width), relations.dtype),
        in_specs=[pl.BlockSpec(memory_space=pltpu.VMEM)],
        out_specs=pl.BlockSpec(memory_space=pl.ANY),
        scratch_shapes=[
            pltpu.SemaphoreType.DMA,
            pltpu.SemaphoreType.DMA((20,)),
            pltpu.SemaphoreType.DMA((20,)),
        ],
        compiler_params=pltpu.CompilerParams(collective_id=0, has_side_effects=True),
        name="gather_relations",
    )(relations)
    return out.reshape(owners * per, width, width)


def add_into(dst, *others):
    lead = dst.shape[:-2]
    total = 1
    for n in lead:
        total *= n

    def body(i, carry):
        index, rest = [], i
        for n in reversed(lead):
            index.insert(0, lax.rem(rest, n))
            rest = rest // n
        value = dst[tuple(index)].astype(F32)
        for other in others:
            value = value + other[tuple(index)].astype(F32)
        dst[tuple(index)] = value.astype(dst.dtype)
        return carry

    lax.fori_loop(0, total, body, 0)


class Ring:
    def __init__(self, mail, place, ahead, behind, piece, halves, land_half, land_full):
        self.mail, self.place, self.ahead, self.behind = mail, place, ahead, behind
        self.piece, self.halves, self.land_half, self.land_full = piece, halves, land_half, land_full

    def one(self):
        far = turn(self.place, 2)
        self.h = [
            self.mail.send(self.halves(self.piece(far))[d], self.land_half[d], device)
            for d, device in enumerate((self.ahead, self.behind))
        ]

    def two(self):
        self.f = []
        for d, (step, device) in enumerate(((1, self.ahead), (3, self.behind))):
            self.h[d].wait_recv()
            target = self.piece(turn(self.place, step))
            add_into(self.halves(target)[d], self.land_half[d])
            self.f.append(self.mail.send(target, self.land_full[d], device))

    def three(self):
        for copy in self.f:
            copy.wait_recv()
        return self.piece(self.place), self.land_full


def scatter_kernel(
    terms, out, got, ax_h, ax_f, ay_h, ay_f, az_h, az_f, by_h, by_f, bx_h, bx_f, bz_h, bz_f, send_sem, recv_sem
):
    at = Spot()
    mail = Mail(send_sem, recv_sem)
    partner = at.device(core=1 - at.core)
    xs = at.device(x=turn(at.x, 1)), at.device(x=turn(at.x, 3))
    ys = at.device(y=turn(at.y, 1)), at.device(y=turn(at.y, 3))
    zs = at.device(z=turn(at.z, 1)), at.device(z=turn(at.z, 3))
    greet([partner, *xs, *ys, *zs])

    swap = [mail.send(terms.at[j, :, :, :, :, 1 - at.core], got.at[j], partner) for j in range(2)]

    def first_half(ref):
        return ref.at[0], ref.at[1]

    def row_halves(ref):
        rows = ref.shape[0] // 2
        return ref.at[pl.ds(0, rows)], ref.at[pl.ds(rows, rows)]

    def two(ref):
        return ref.at[0], ref.at[1]

    a, b = got.at[0], got.at[1]
    ax = Ring(mail, at.x, *xs, lambda t: a.at[:, t], first_half, two(ax_h), two(ax_f))
    a1 = lambda: a.at[:, at.x]
    ay = Ring(mail, at.y, *ys, lambda t: a1().at[:, :, t], first_half, two(ay_h), two(ay_f))
    a2 = lambda z: a.at[z // 2, at.x, lax.rem(z, 2), at.y]
    az = Ring(mail, at.z, *zs, a2, row_halves, two(az_h), two(az_f))
    by = Ring(mail, at.y, *ys, lambda t: b.at[:, :, :, t], first_half, two(by_h), two(by_f))
    bx = Ring(mail, at.x, *xs, lambda t: b.at[:, t, :, at.y], first_half, two(bx_h), two(bx_f))
    b2 = lambda z: b.at[z // 2, at.x, lax.rem(z, 2), at.y]
    bz = Ring(mail, at.z, *zs, b2, row_halves, two(bz_h), two(bz_f))

    for j, (ref, ring) in enumerate(((a, ax), (b, by))):
        swap[j].wait_recv()
        add_into(ref, terms.at[j, :, :, :, :, at.core])
        ring.one()
    ax.two()
    by.two()
    for ring, following in ((ax, ay), (by, bx)):
        piece, landed = ring.three()
        add_into(piece, *landed)
        following.one()
    ay.two()
    bx.two()
    for ring, following in ((ay, az), (bx, bz)):
        piece, landed = ring.three()
        add_into(piece, *landed)
        following.one()
    az.two()
    bz.two()
    for j, ring in enumerate((az, bz)):
        piece, landed = ring.three()
        out[:, j, :] = piece[...].astype(F32) + landed[0][...].astype(F32) + landed[1][...].astype(F32)
    mail.drain()


def scatter_terms(terms):
    nrel, width, _ = terms.shape
    rows = width // 16
    shaped = terms.reshape(2, 2, 4, 2, 4, 2, rows, width)
    v = lambda *lead: pltpu.VMEM((*lead, rows, width), BF)
    z = lambda r: pltpu.VMEM((2, r, width), BF)
    return pl.pallas_call(
        scatter_kernel,
        out_shape=jax.ShapeDtypeStruct((rows, 2, width), F32),
        in_specs=[pl.BlockSpec(memory_space=pltpu.VMEM)],
        out_specs=pl.BlockSpec(memory_space=pltpu.VMEM),
        scratch_shapes=[
            v(2, 2, 4, 2, 4),
            v(2, 2, 4), v(2, 2, 2, 4), v(2, 2), v(2, 2, 2), z(rows // 2), v(2),
            v(2, 4, 2), v(2, 2, 4, 2), v(2, 2), v(2, 2, 2), z(rows // 2), v(2),
            pltpu.SemaphoreType.DMA((26,)),
            pltpu.SemaphoreType.DMA((26,)),
        ],
        compiler_params=pltpu.CompilerParams(
            collective_id=1, has_side_effects=True, vmem_limit_bytes=60 << 20
        ),
        name="scatter_terms",
    )(shaped)

STOPS = 8
learn_rate = 0.005
LOW = 64


def stops_kernel(
    q, neg, pos, entities, state_out, grad_out,
    held, sent, wide, weights, acc, low, unit, packed, local_sem, send_sem, recv_sem,
):
    cand, rel = lax.axis_index("cand"), lax.axis_index("rel")
    n = lax.axis_size("cand")
    ahead, behind = (lax.rem(cand + 1, n), rel), (lax.rem(cand + n - 1, n), rel)
    greet([ahead, behind])
    part, width = entities.shape
    rows = q.shape[0]
    chunk = part // 2
    parts = part // LOW
    block = 256
    lanes = 128

    fetch = [
        pltpu.make_async_copy(entities.at[pl.ds(h * chunk, chunk)], held.at[h], local_sem.at[h])
        for h in range(2)
    ]
    for copy in fetch:
        copy.start()

    def tally(stop):
        picks = neg[stop]
        samples = picks.shape[0]
        low[0:samples, :] = lax.bitwise_and(picks, LOW - 1)
        unit[0:samples, :] = lax.shift_left(jnp.ones_like(picks), 8 * lax.shift_right_logical(picks, 6))
        place = pos[...] - stop * part
        inside = (place >= 0) & (place < part)
        place = jnp.where(inside, place, 0)
        low[samples : samples + 1, :] = lax.bitwise_and(place, LOW - 1)
        unit[samples : samples + 1, :] = jnp.where(
            inside, lax.shift_left(jnp.full_like(place, 32), 8 * lax.shift_right_logical(place, 6)), 0
        )

        def column(c, carry):
            here = pl.ds(pl.multiple_of(c * lanes, lanes), lanes)
            index = lax.broadcasted_iota(jnp.int32, (LOW, lanes), 0)
            total = jnp.zeros((LOW, lanes), jnp.int32)
            for k in range(samples + 1):
                match = jnp.broadcast_to(low[k : k + 1, here], (LOW, lanes)) == index
                total = total + jnp.where(match, jnp.broadcast_to(unit[k : k + 1, here], (LOW, lanes)), 0)
            packed[:, here] = total
            return carry

        lax.fori_loop(0, rows // lanes, column, 0)

    tally(0)
    acc[...] = jnp.zeros_like(acc)
    for copy in fetch:
        copy.wait()

    def hop(t):
        return pltpu.make_async_remote_copy(
            src_ref=sent.at[t],
            dst_ref=held.at[t + 2],
            send_sem=send_sem.at[t],
            recv_sem=recv_sem.at[t],
            device_id=ahead,
            device_id_type=MESH,
        )

    def step(t, carry):
        half = lax.rem(t, 2)
        base = half * chunk

        @pl.when(t >= 2)
        def _():
            hop(t - 2).wait_recv()

        state = held[t]
        rounded = state.astype(BF)
        wide[pl.ds(pl.multiple_of(base, chunk), chunk), :] = rounded
        pieces = []
        for i in range(rows // block):
            here = pl.ds(i * block, block)
            logits = lax.dot_general(
                rounded, q[here, :], (((1,), (1,)), ((), ())), preferred_element_type=F32
            )
            marks = packed[:, here]
            marks = jnp.concatenate(
                [
                    lax.bitwise_and(lax.shift_right_logical(marks, 16 * half + 8 * p), 63)
                    for p in range(chunk // LOW)
                ],
                axis=0,
            )
            count = lax.bitwise_and(marks, 31).astype(F32)
            small = jnp.exp(-jnp.abs(logits))
            big = 1.0 / (1.0 + small)
            small = small * big
            positive = logits >= 0
            up = count * jnp.where(positive, big, small)
            down = jnp.where(positive, small, big)
            pieces.append(jnp.where(marks >= 32, up - down, up).astype(BF))
        weight = jnp.concatenate(pieces, axis=1)
        weights[pl.ds(pl.multiple_of(base, chunk), chunk), :] = weight
        change = jnp.dot(weight, q[...], preferred_element_type=F32)
        sent[t] = state - learn_rate * change

        @pl.when(t < 2 * STOPS - 2)
        def _():
            hop(t).start()

        @pl.when(half == 1)
        def _():
            def gather(c, carry):
                here = pl.ds(pl.multiple_of(c * block, block), block)
                acc[:, here] += lax.dot_general(
                    wide[...], weights[:, here], (((0,), (0,)), ((), ())), preferred_element_type=F32
                )
                return carry

            lax.fori_loop(0, rows // block, gather, 0)

            @pl.when(t < 2 * STOPS - 1)
            def _():
                tally(t // 2 + 1)

        return carry

    lax.fori_loop(0, 2 * STOPS, step, 0)
    for h in range(2):
        state_out[pl.ds(h * chunk, chunk), :] = sent[2 * STOPS - 2 + h]

    def turned(c, carry):
        here = pl.ds(pl.multiple_of(c * block, block), block)
        grad_out[here, :] = acc[:, here].T.astype(BF)
        return carry

    lax.fori_loop(0, rows // block, turned, 0)

    def drained(t, carry):
        hop(t).wait_send()
        return carry

    lax.fori_loop(0, 2 * STOPS - 2, drained, 0)


def run_stops(queries, picks, pos, entities):
    rows, width = queries.shape
    part = entities.shape[0]
    chunk = part // 2
    vmem = pl.BlockSpec(memory_space=pltpu.VMEM)
    hops = 2 * STOPS
    return pl.pallas_call(
        stops_kernel,
        out_shape=(
            jax.ShapeDtypeStruct((part, width), F32),
            jax.ShapeDtypeStruct((rows, width), BF),
        ),
        in_specs=[vmem, vmem, vmem, pl.BlockSpec(memory_space=pl.ANY)],
        out_specs=(vmem, vmem),
        scratch_shapes=[
            pltpu.VMEM((hops, chunk, width), F32),
            pltpu.VMEM((hops, chunk, width), F32),
            pltpu.VMEM((part, width), BF),
            pltpu.VMEM((part, rows), BF),
            pltpu.VMEM((width, rows), F32),
            pltpu.VMEM((24, rows), jnp.int32),
            pltpu.VMEM((24, rows), jnp.int32),
            pltpu.VMEM((LOW, rows), jnp.int32),
            pltpu.SemaphoreType.DMA((2,)),
            pltpu.SemaphoreType.DMA((hops,)),
            pltpu.SemaphoreType.DMA((hops,)),
        ],
        compiler_params=pltpu.CompilerParams(
            collective_id=2, has_side_effects=True, vmem_limit_bytes=60 << 20
        ),
        name="run_stops",
    )(queries, picks, pos, entities)


def slot_index(rel_ids, nrel, most):
    ids = rel_ids[:, 0]
    onehot = (ids[:, None] == jnp.arange(nrel, dtype=jnp.int32)[None, :]).astype(jnp.int32)
    rank = jnp.cumsum(onehot, axis=0) - onehot
    return ids * most + jnp.sum(rank * onehot, axis=1)


def place_rows(rows, slot, total):
    return jnp.zeros((total, rows.shape[1]), rows.dtype).at[slot].set(rows)


def shards(source_rows, rel_ids, relations, entities, pos_slot, negatives):
    src_rows, width = source_rows.shape
    rel_dev = relations.shape[0]
    owners = lax.axis_size("rel")
    nrel = rel_dev * owners
    most = 2 * src_rows // nrel
    slot = slot_index(rel_ids, nrel, most)
    sent = place_rows(source_rows, slot, nrel * most).reshape(nrel, most, width)
    every_matrix = gather_relations(relations)
    q_slots = jnp.einsum(
        "kmd,kde->kme", sent, every_matrix, preferred_element_type=jnp.float32
    ).astype(jnp.bfloat16)
    queries = q_slots.reshape(nrel * most, width)[slot]
    state, query_grad = run_stops(
        queries, jnp.transpose(negatives, (0, 2, 1)), pos_slot.reshape(1, -1), entities
    )
    gq_slots = place_rows(query_grad, slot, nrel * most).reshape(nrel, most, width)
    back_slots = jnp.einsum(
        "kme,kde->kmd", gq_slots, every_matrix, preferred_element_type=jnp.float32
    ).astype(jnp.bfloat16)
    by_parity = lambda t: jnp.moveaxis(t.reshape(owners, rel_dev, most, width), 1, 0).reshape(nrel, most, width)
    terms = jnp.einsum(
        "kmd,kme->kde", by_parity(sent), by_parity(gq_slots), preferred_element_type=jnp.float32
    ).astype(jnp.bfloat16)
    source_grad = back_slots.reshape(nrel * most, width)[slot]
    relation_grad = scatter_terms(terms)
    return (state, source_grad, relation_grad)


def solution(mesh):
    placed = (
        P(("cand", "rel"), None),
        P(("cand", "rel"), None),
        P("rel", None, None),
        P(("cand", "rel"), None),
        P(("cand", "rel")),
        P(None, ("cand", "rel"), None),
    )
    return jax.shard_map(
        shards,
        mesh=mesh,
        in_specs=placed,
        out_specs=(P(("cand", "rel"), None), P(("cand", "rel"), None), P("cand", "rel", None)),
        check_vma=False,
    )
```

```python
import functools

import jax
import jax.numpy as jnp
from jax import lax
from jax.experimental import pallas as pl
from jax.experimental.pallas import tpu as pltpu
from jax.sharding import PartitionSpec as P

MESH = pl.DeviceIdType.MESH
BF = jnp.bfloat16
F32 = jnp.float32


class Spot:
    def __init__(self):
        cand, rel = lax.axis_index("cand"), lax.axis_index("rel")
        self.core = lax.rem(cand, 2)
        self.y = lax.rem(cand // 2, 4)
        self.zl = cand // 8
        self.x = lax.rem(rel, 4)
        self.zh = rel // 4
        self.z = self.zh * 2 + self.zl
        self.rel = rel

    def device(self, x=None, y=None, z=None, core=None):
        x = self.x if x is None else x
        y = self.y if y is None else y
        z = self.z if z is None else z
        core = self.core if core is None else core
        return ((lax.rem(z, 2) * 4 + y) * 2 + core, (z // 2) * 4 + x)


def turn(i, by):
    return lax.rem(i + by, 4)


def greet(devices):
    barrier = pltpu.get_barrier_semaphore()
    for device in devices:
        pl.semaphore_signal(barrier, inc=1, device_id=device, device_id_type=MESH)
    pl.semaphore_wait(barrier, len(devices))


class Mail:
    def __init__(self, send_sem, recv_sem):
        self.send_sem, self.recv_sem, self.count, self.sent = send_sem, recv_sem, 0, []

    def send(self, src, dst, device):
        i = self.count
        self.count += 1
        copy = pltpu.make_async_remote_copy(
            src_ref=src,
            dst_ref=dst,
            send_sem=self.send_sem.at[i],
            recv_sem=self.recv_sem.at[i],
            device_id=device,
            device_id_type=MESH,
        )
        copy.start()
        self.sent.append(copy)
        return copy

    def drain(self):
        for copy in self.sent:
            copy.wait_send()


WINDOW_PAD = 16


def sort_plan(ids, nrel):
    rows = ids.shape[1]
    block = 256
    named = (jnp.broadcast_to(ids, (nrel, rows)) == lax.broadcasted_iota(jnp.int32, (nrel, rows), 0)).astype(F32)
    before = (
        lax.broadcasted_iota(jnp.int32, (block, block), 0) < lax.broadcasted_iota(jnp.int32, (block, block), 1)
    ).astype(BF)
    running = jnp.zeros((nrel, 1), F32)
    ranks = []
    for b in range(rows // block):
        part = named[:, b * block : (b + 1) * block]
        ranks.append(jnp.dot(part.astype(BF), before, preferred_element_type=F32) + running)
        running = running + jnp.sum(part, axis=1, keepdims=True)
    rank = jnp.concatenate(ranks, axis=1)
    lower = (
        lax.broadcasted_iota(jnp.int32, (nrel, nrel), 1) < lax.broadcasted_iota(jnp.int32, (nrel, nrel), 0)
    ).astype(BF)
    starts = jnp.dot(lower, jnp.broadcast_to(running, (nrel, 128)).astype(BF), preferred_element_type=F32)
    place = jnp.sum(named * (rank + starts[:, 0:1]), axis=0, keepdims=True)
    return place, starts


def sort_rows(b, place, rows_ref, meta_ref, rows_out, picks_out, pos_out, part):
    rows = place.shape[1]
    block = 256
    here = pl.ds(b * block, block)
    spot = lax.broadcasted_iota(jnp.int32, (block, rows), 0) + b * block
    choose = (jnp.broadcast_to(place, (block, rows)) == spot).astype(F32).astype(BF)
    rows_out[here, :] = jnp.dot(choose, rows_ref[...], preferred_element_type=F32).astype(BF)
    meta = lax.dot_general(
        meta_ref[...], choose, (((1,), (1,)), ((), ())), preferred_element_type=F32
    ).astype(jnp.int32)
    named = picks_out.shape[0]
    picks_out[:, here] = meta[0:named]
    pos_out[:, here] = meta[named : named + 1] * part + meta[named + 1 : named + 2]


def group_queries(starts, rows_ref, matrix, out):
    k = pl.program_id(0)
    window = out_window(starts, k)
    rows = rows_ref[window[0], :]
    new = jnp.dot(rows, matrix[0], preferred_element_type=F32).astype(BF)
    out[window[0], :] = jnp.where(window[1], new, out[window[0], :])


def out_window(starts, k):
    size = 256 + WINDOW_PAD
    start, end = starts[k], starts[k + 1]
    base = pl.multiple_of(start // WINDOW_PAD * WINDOW_PAD, WINDOW_PAD)
    row = lax.broadcasted_iota(jnp.int32, (size, 512), 0) + base
    return pl.ds(base, size), (row >= start) & (row < end)


def make_queries(starts, rows, matrices):
    nrel, width, _ = matrices.shape
    return pl.pallas_call(
        group_queries,
        out_shape=jax.ShapeDtypeStruct(rows.shape, BF),
        grid_spec=pltpu.PrefetchScalarGridSpec(
            num_scalar_prefetch=1,
            grid=(nrel,),
            in_specs=[
                pl.BlockSpec(rows.shape, lambda k, s: (0, 0)),
                pl.BlockSpec((1, width, width), lambda k, s: (k, 0, 0)),
            ],
            out_specs=pl.BlockSpec(rows.shape, lambda k, s: (0, 0)),
        ),
        compiler_params=pltpu.CompilerParams(vmem_limit_bytes=40 << 20),
        name="make_queries",
    )(starts, rows, matrices)


def group_grads(starts, place, rows_ref, grads, matrix, terms, source_grad, back):
    step = pl.program_id(0)
    nrel = 16

    @pl.when(step < nrel)
    def _():
        window, inside = out_window(starts, step)
        grad = grads[window, :]
        new = lax.dot_general(grad, matrix[0], (((1,), (1,)), ((), ())), preferred_element_type=F32).astype(BF)
        back[window, :] = jnp.where(inside, new, back[window, :])
        rows = rows_ref[window, :]
        rows = jnp.where(inside, rows, jnp.zeros_like(rows))
        terms[0, 0] = lax.dot_general(
            rows, grad, (((0,), (0,)), ((), ())), preferred_element_type=F32
        ).astype(BF)

    @pl.when(step >= nrel)
    def _():
        lanes = 128
        b = step - nrel
        here = pl.ds(pl.multiple_of(b * lanes, lanes), lanes)
        mine = jnp.broadcast_to(place[:, here], (lanes, lanes)).T
        index = lax.broadcasted_iota(jnp.int32, (lanes, lanes), 1)
        total = place.shape[1]
        choose = jnp.concatenate(
            [(mine == index + t * lanes).astype(F32).astype(BF) for t in range(total // lanes)], axis=1
        )
        source_grad[...] = jnp.dot(choose, back[0:total, :], preferred_element_type=F32).astype(BF)


def make_grads(starts, place, rows, grads, matrices):
    nrel, width, _ = matrices.shape
    total = place.shape[1]
    blocks = total // 128
    last = lambda k: jnp.minimum(k, nrel - 1)
    whole = lambda a: pl.BlockSpec(a.shape, lambda k, s: (0, 0))
    return pl.pallas_call(
        group_grads,
        out_shape=(
            jax.ShapeDtypeStruct((2, nrel // 2, width, width), BF),
            jax.ShapeDtypeStruct((total, width), BF),
        ),
        grid_spec=pltpu.PrefetchScalarGridSpec(
            num_scalar_prefetch=1,
            grid=(nrel + blocks,),
            in_specs=[
                whole(place),
                whole(rows),
                whole(grads),
                pl.BlockSpec((1, width, width), lambda k, s: (last(k), 0, 0)),
            ],
            out_specs=(
                pl.BlockSpec((1, 1, width, width), lambda k, s: (lax.rem(last(k), 2), last(k) // 2, 0, 0)),
                pl.BlockSpec((128, width), lambda k, s: (jnp.maximum(k - nrel, 0), 0)),
            ),
            scratch_shapes=[pltpu.VMEM(rows.shape, BF)],
        ),
        compiler_params=pltpu.CompilerParams(vmem_limit_bytes=40 << 20),
        name="make_grads",
    )(starts, place, rows, grads, matrices)


def gather_kernel(
    own, ids, rows_ref, picks, target, out, rows_out, picks_out, target_out, place_out, starts_out, meta,
    local_sem, send_sem, recv_sem,
):
    at = Spot()
    mail = Mail(send_sem, recv_sem)
    left, right = at.device(x=turn(at.x, 3)), at.device(x=turn(at.x, 1))
    across = at.device(z=3 - at.z)
    partner = at.device(core=1 - at.core)
    greet([left, right, across, partner])
    here = pltpu.make_async_copy(own, out.at[at.rel], local_sem)
    here.start()
    half = own.shape[1] // 2
    start = pl.multiple_of(at.core * half, half)
    mine = pl.ds(start, half)
    first = pl.ds(start, half // 2)
    second = pl.ds(pl.multiple_of(start + half // 2, half // 2), half // 2)
    me, far = at.zh * 4, (1 - at.zh) * 4
    x0, x1, x2, x3 = at.x, turn(at.x, 1), turn(at.x, 2), turn(at.x, 3)
    own_mine = own.at[:, mine]

    def block(base, x, rows):
        return out.at[base + x, :, rows]

    to_across = mail.send(own_mine, block(me, x0, mine), across)
    to_right = mail.send(own_mine, block(me, x0, mine), right)
    to_left = mail.send(own_mine, block(me, x0, mine), left)

    stops, samples, total = picks.shape
    part = total // stops
    nrel = starts_out.shape[0]
    place, starts = sort_plan(ids[...], nrel)
    place = place.astype(jnp.int32)
    place_out[...] = place
    starts_out[...] = starts.astype(jnp.int32)
    for s in range(stops):
        meta[s * samples : (s + 1) * samples, :] = picks[s].astype(F32).astype(BF)
    goal = target[...]
    tail = lax.broadcasted_iota(jnp.int32, (16, total), 0)
    meta[stops * samples :, :] = jnp.where(
        tail == 0, jnp.broadcast_to(goal // part, (16, total)), jnp.broadcast_to(lax.rem(goal, part), (16, total))
    ).astype(F32).astype(BF)
    rows_out[total:, :] = jnp.zeros((rows_out.shape[0] - total, rows_out.shape[1]), BF)

    def work(b):
        sort_rows(b, place_out[...], rows_ref, meta, rows_out, picks_out, target_out, part)

    work(0)
    to_right.wait_recv()
    on_right = mail.send(block(me, x3, first), block(me, x3, first), right)
    share = [mail.send(block(me, x3, mine), block(me, x3, mine), partner)]
    to_left.wait_recv()
    on_left = mail.send(block(me, x1, second), block(me, x1, second), left)
    share.append(mail.send(block(me, x1, mine), block(me, x1, mine), partner))
    work(1)
    to_across.wait_recv()
    far_right = mail.send(block(far, x0, mine), block(far, x0, mine), right)
    far_left = mail.send(block(far, x0, mine), block(far, x0, mine), left)
    share.append(mail.send(block(far, x0, mine), block(far, x0, mine), partner))
    work(2)
    work(3)
    on_right.wait_recv()
    opposite_a = mail.send(block(me, x2, first), block(me, x2, first), across)
    on_left.wait_recv()
    opposite_b = mail.send(block(me, x2, second), block(me, x2, second), across)
    share.append(mail.send(block(me, x2, mine), block(me, x2, mine), partner))
    for b in range(4, 8):
        work(b)
    far_right.wait_recv()
    share.append(mail.send(block(far, x3, mine), block(far, x3, mine), partner))
    far_left.wait_recv()
    share.append(mail.send(block(far, x1, mine), block(far, x1, mine), partner))
    opposite_a.wait_recv()
    opposite_b.wait_recv()
    share.append(mail.send(block(far, x2, mine), block(far, x2, mine), partner))
    for copy in share:
        copy.wait_recv()
    mail.drain()
    here.wait()


def gather_relations(relations, ids, rows, picks, target):
    per, width, _ = relations.shape
    owners = lax.axis_size("rel")
    nrel = owners * per
    stops, samples, total = picks.shape
    vmem = pl.BlockSpec(memory_space=pltpu.VMEM)
    out = pl.pallas_call(
        gather_kernel,
        out_shape=(
            jax.ShapeDtypeStruct((owners, per, width, width), relations.dtype),
            jax.ShapeDtypeStruct((total + 256 + WINDOW_PAD, width), BF),
            jax.ShapeDtypeStruct((stops * samples, total), jnp.int32),
            jax.ShapeDtypeStruct((1, total), jnp.int32),
            jax.ShapeDtypeStruct((1, total), jnp.int32),
            jax.ShapeDtypeStruct((nrel, 128), jnp.int32),
        ),
        in_specs=[vmem] * 5,
        out_specs=(pl.BlockSpec(memory_space=pl.ANY), *[vmem] * 5),
        scratch_shapes=[
            pltpu.VMEM((stops * samples + 16, total), BF),
            pltpu.SemaphoreType.DMA,
            pltpu.SemaphoreType.DMA((20,)),
            pltpu.SemaphoreType.DMA((20,)),
        ],
        compiler_params=pltpu.CompilerParams(
            collective_id=0, has_side_effects=True, vmem_limit_bytes=40 << 20
        ),
        name="gather_relations",
    )(relations, ids, rows, picks, target)
    matrices, rows, picks, target, place, starts = out
    starts = jnp.concatenate([starts[:, 0], jnp.full((1,), total, jnp.int32)])
    return matrices.reshape(nrel, width, width), rows, picks.reshape(stops, samples, total), target, place, starts


STOPS = 8
learn_rate = 0.005
LOW = 64


def stops_kernel(
    q, neg, pos, entities, state_out, grad_out,
    held, sent, wide, weights, acc, low, unit, packed, local_sem, send_sem, recv_sem,
):
    cand, rel = lax.axis_index("cand"), lax.axis_index("rel")
    n = lax.axis_size("cand")
    ahead, behind = (lax.rem(cand + 1, n), rel), (lax.rem(cand + n - 1, n), rel)
    greet([ahead, behind])
    part, width = entities.shape
    rows = pos.shape[1]
    chunk = part // 2
    parts = part // LOW
    block = 256
    lanes = 128

    fetch = [
        pltpu.make_async_copy(entities.at[pl.ds(h * chunk, chunk)], held.at[h], local_sem.at[h])
        for h in range(2)
    ]
    for copy in fetch:
        copy.start()

    def tally(stop):
        picks = neg[stop]
        samples = picks.shape[0]
        low[0:samples, :] = lax.bitwise_and(picks, LOW - 1)
        unit[0:samples, :] = lax.shift_left(jnp.ones_like(picks), 8 * lax.shift_right_logical(picks, 6))
        place = pos[...] - stop * part
        inside = (place >= 0) & (place < part)
        place = jnp.where(inside, place, 0)
        low[samples : samples + 1, :] = lax.bitwise_and(place, LOW - 1)
        unit[samples : samples + 1, :] = jnp.where(
            inside, lax.shift_left(jnp.full_like(place, 32), 8 * lax.shift_right_logical(place, 6)), 0
        )

        def column(c, carry):
            here = pl.ds(pl.multiple_of(c * lanes, lanes), lanes)
            index = lax.broadcasted_iota(jnp.int32, (LOW, lanes), 0)
            total = jnp.zeros((LOW, lanes), jnp.int32)
            for k in range(samples + 1):
                match = jnp.broadcast_to(low[k : k + 1, here], (LOW, lanes)) == index
                total = total + jnp.where(match, jnp.broadcast_to(unit[k : k + 1, here], (LOW, lanes)), 0)
            packed[:, here] = total
            return carry

        lax.fori_loop(0, rows // lanes, column, 0)

    tally(0)
    acc[...] = jnp.zeros_like(acc)
    for copy in fetch:
        copy.wait()

    def hop(t):
        return pltpu.make_async_remote_copy(
            src_ref=sent.at[t],
            dst_ref=held.at[t + 2],
            send_sem=send_sem.at[t],
            recv_sem=recv_sem.at[t],
            device_id=ahead,
            device_id_type=MESH,
        )

    def step(t, carry):
        half = lax.rem(t, 2)
        base = half * chunk

        @pl.when(t >= 2)
        def _():
            hop(t - 2).wait_recv()

        state = held[t]
        rounded = state.astype(BF)
        wide[pl.ds(pl.multiple_of(base, chunk), chunk), :] = rounded
        pieces = []
        for i in range(rows // block):
            here = pl.ds(i * block, block)
            logits = lax.dot_general(
                rounded, q[here, :], (((1,), (1,)), ((), ())), preferred_element_type=F32
            )
            marks = packed[:, here]
            marks = jnp.concatenate(
                [
                    lax.bitwise_and(lax.shift_right_logical(marks, 16 * half + 8 * p), 63)
                    for p in range(chunk // LOW)
                ],
                axis=0,
            )
            count = lax.bitwise_and(marks, 31).astype(F32)
            small = jnp.exp(-jnp.abs(logits))
            big = 1.0 / (1.0 + small)
            small = small * big
            positive = logits >= 0
            up = count * jnp.where(positive, big, small)
            down = jnp.where(positive, small, big)
            pieces.append(jnp.where(marks >= 32, up - down, up).astype(BF))
        weight = jnp.concatenate(pieces, axis=1)
        weights[pl.ds(pl.multiple_of(base, chunk), chunk), :] = weight
        change = jnp.dot(weight, q[0:rows, :], preferred_element_type=F32)
        sent[t] = state - learn_rate * change

        @pl.when(t < 2 * STOPS - 2)
        def _():
            hop(t).start()

        @pl.when(half == 1)
        def _():
            def gather(c, carry):
                here = pl.ds(pl.multiple_of(c * block, block), block)
                acc[:, here] += lax.dot_general(
                    wide[...], weights[:, here], (((0,), (0,)), ((), ())), preferred_element_type=F32
                )
                return carry

            lax.fori_loop(0, rows // block, gather, 0)

            @pl.when(t < 2 * STOPS - 1)
            def _():
                tally(t // 2 + 1)

        return carry

    lax.fori_loop(0, 2 * STOPS, step, 0)
    for h in range(2):
        state_out[pl.ds(h * chunk, chunk), :] = sent[2 * STOPS - 2 + h]

    def turned(c, carry):
        here = pl.ds(pl.multiple_of(c * block, block), block)
        grad_out[here, :] = acc[:, here].T.astype(BF)
        return carry

    lax.fori_loop(0, rows // block, turned, 0)

    grad_out[rows:, :] = jnp.zeros((grad_out.shape[0] - rows, width), BF)

    def drained(t, carry):
        hop(t).wait_send()
        return carry

    lax.fori_loop(0, 2 * STOPS - 2, drained, 0)


def run_stops(queries, picks, pos, entities):
    padded, width = queries.shape
    rows = pos.shape[1]
    part = entities.shape[0]
    chunk = part // 2
    vmem = pl.BlockSpec(memory_space=pltpu.VMEM)
    hops = 2 * STOPS
    return pl.pallas_call(
        stops_kernel,
        out_shape=(
            jax.ShapeDtypeStruct((part, width), F32),
            jax.ShapeDtypeStruct((padded, width), BF),
        ),
        in_specs=[vmem, vmem, vmem, pl.BlockSpec(memory_space=pl.ANY)],
        out_specs=(vmem, vmem),
        scratch_shapes=[
            pltpu.VMEM((hops, chunk, width), F32),
            pltpu.VMEM((hops, chunk, width), F32),
            pltpu.VMEM((part, width), BF),
            pltpu.VMEM((part, rows), BF),
            pltpu.VMEM((width, rows), F32),
            pltpu.VMEM((24, rows), jnp.int32),
            pltpu.VMEM((24, rows), jnp.int32),
            pltpu.VMEM((LOW, rows), jnp.int32),
            pltpu.SemaphoreType.DMA((2,)),
            pltpu.SemaphoreType.DMA((hops,)),
            pltpu.SemaphoreType.DMA((hops,)),
        ],
        compiler_params=pltpu.CompilerParams(
            collective_id=2, has_side_effects=True, vmem_limit_bytes=60 << 20
        ),
        name="run_stops",
    )(queries, picks, pos, entities)


def add_into(dst, *others):
    lead = dst.shape[:-2]
    total = 1
    for n in lead:
        total *= n

    def body(i, carry):
        index, rest = [], i
        for n in reversed(lead):
            index.insert(0, lax.rem(rest, n))
            rest = rest // n
        value = dst[tuple(index)].astype(F32)
        for other in others:
            value = value + other[tuple(index)].astype(F32)
        dst[tuple(index)] = value.astype(dst.dtype)
        return carry

    lax.fori_loop(0, total, body, 0)


class Ring:
    def __init__(self, mail, place, ahead, behind, piece, halves, land_half, land_full):
        self.mail, self.place, self.ahead, self.behind = mail, place, ahead, behind
        self.piece, self.halves, self.land_half, self.land_full = piece, halves, land_half, land_full

    def one(self):
        far = turn(self.place, 2)
        self.h = [
            self.mail.send(self.halves(self.piece(far))[d], self.land_half[d], device)
            for d, device in enumerate((self.ahead, self.behind))
        ]

    def two(self):
        self.f = []
        for d, (step, device) in enumerate(((1, self.ahead), (3, self.behind))):
            self.h[d].wait_recv()
            target = self.piece(turn(self.place, step))
            add_into(self.halves(target)[d], self.land_half[d])
            self.f.append(self.mail.send(target, self.land_full[d], device))

    def three(self):
        for copy in self.f:
            copy.wait_recv()
        return self.piece(self.place), self.land_full


def scatter_kernel(
    terms, out, got, ax_h, ax_f, ay_h, ay_f, az_h, az_f, by_h, by_f, bx_h, bx_f, bz_h, bz_f, send_sem, recv_sem
):
    at = Spot()
    mail = Mail(send_sem, recv_sem)
    partner = at.device(core=1 - at.core)
    xs = at.device(x=turn(at.x, 1)), at.device(x=turn(at.x, 3))
    ys = at.device(y=turn(at.y, 1)), at.device(y=turn(at.y, 3))
    zs = at.device(z=turn(at.z, 1)), at.device(z=turn(at.z, 3))
    greet([partner, *xs, *ys, *zs])

    swap = [mail.send(terms.at[j, :, :, :, :, 1 - at.core], got.at[j], partner) for j in range(2)]

    def first_half(ref):
        return ref.at[0], ref.at[1]

    def row_halves(ref):
        rows = ref.shape[0] // 2
        return ref.at[pl.ds(0, rows)], ref.at[pl.ds(rows, rows)]

    def two(ref):
        return ref.at[0], ref.at[1]

    a, b = got.at[0], got.at[1]
    ax = Ring(mail, at.x, *xs, lambda t: a.at[:, t], first_half, two(ax_h), two(ax_f))
    a1 = lambda: a.at[:, at.x]
    ay = Ring(mail, at.y, *ys, lambda t: a1().at[:, :, t], first_half, two(ay_h), two(ay_f))
    a2 = lambda z: a.at[z // 2, at.x, lax.rem(z, 2), at.y]
    az = Ring(mail, at.z, *zs, a2, row_halves, two(az_h), two(az_f))
    by = Ring(mail, at.y, *ys, lambda t: b.at[:, :, :, t], first_half, two(by_h), two(by_f))
    bx = Ring(mail, at.x, *xs, lambda t: b.at[:, t, :, at.y], first_half, two(bx_h), two(bx_f))
    b2 = lambda z: b.at[z // 2, at.x, lax.rem(z, 2), at.y]
    bz = Ring(mail, at.z, *zs, b2, row_halves, two(bz_h), two(bz_f))

    for j, (ref, ring) in enumerate(((a, ax), (b, by))):
        swap[j].wait_recv()
        add_into(ref, terms.at[j, :, :, :, :, at.core])
        ring.one()
    ax.two()
    by.two()
    for ring, following in ((ax, ay), (by, bx)):
        piece, landed = ring.three()
        add_into(piece, *landed)
        following.one()
    ay.two()
    bx.two()
    for ring, following in ((ay, az), (bx, bz)):
        piece, landed = ring.three()
        add_into(piece, *landed)
        following.one()
    az.two()
    bz.two()
    for j, ring in enumerate((az, bz)):
        piece, landed = ring.three()
        out[:, j, :] = piece[...].astype(F32) + landed[0][...].astype(F32) + landed[1][...].astype(F32)
    mail.drain()


def scatter_terms(terms):
    width = terms.shape[-1]
    rows = width // 16
    shaped = terms.reshape(2, 2, 4, 2, 4, 2, rows, width)
    v = lambda *lead: pltpu.VMEM((*lead, rows, width), BF)
    z = lambda r: pltpu.VMEM((2, r, width), BF)
    return pl.pallas_call(
        scatter_kernel,
        out_shape=jax.ShapeDtypeStruct((rows, 2, width), F32),
        in_specs=[pl.BlockSpec(memory_space=pltpu.VMEM)],
        out_specs=pl.BlockSpec(memory_space=pltpu.VMEM),
        scratch_shapes=[
            v(2, 2, 4, 2, 4),
            v(2, 2, 4), v(2, 2, 2, 4), v(2, 2), v(2, 2, 2), z(rows // 2), v(2),
            v(2, 4, 2), v(2, 2, 4, 2), v(2, 2), v(2, 2, 2), z(rows // 2), v(2),
            pltpu.SemaphoreType.DMA((26,)),
            pltpu.SemaphoreType.DMA((26,)),
        ],
        compiler_params=pltpu.CompilerParams(
            collective_id=1, has_side_effects=True, vmem_limit_bytes=60 << 20
        ),
        name="scatter_terms",
    )(shaped)


def shards(source_rows, rel_ids, relations, entities, pos_slot, negatives):
    rows = source_rows.shape[0]
    matrices, sorted_rows, picks, target, place, starts = gather_relations(
        relations,
        rel_ids.reshape(1, rows),
        source_rows,
        jnp.transpose(negatives, (0, 2, 1)),
        pos_slot.reshape(1, rows),
    )
    queries = make_queries(starts, sorted_rows, matrices)
    state, query_grad = run_stops(queries, picks, target, entities)
    terms, source_grad = make_grads(starts, place, sorted_rows, query_grad, matrices)
    relation_grad = scatter_terms(terms)
    return (state, source_grad, relation_grad)


def solution(mesh):
    placed = (
        P(("cand", "rel"), None),
        P(("cand", "rel"), None),
        P("rel", None, None),
        P(("cand", "rel"), None),
        P(("cand", "rel")),
        P(None, ("cand", "rel"), None),
    )
    return jax.shard_map(
        shards,
        mesh=mesh,
        in_specs=placed,
        out_specs=(P(("cand", "rel"), None), P(("cand", "rel"), None), P("cand", "rel", None)),
        check_vma=False,
    )
```

```python
import functools

import jax
import jax.numpy as jnp
from jax import lax
from jax.experimental import pallas as pl
from jax.experimental.pallas import tpu as pltpu
from jax.sharding import PartitionSpec as P

MESH = pl.DeviceIdType.MESH
BF = jnp.bfloat16
F32 = jnp.float32


class Spot:
    def __init__(self):
        cand, rel = lax.axis_index("cand"), lax.axis_index("rel")
        self.core = lax.rem(cand, 2)
        self.y = lax.rem(cand // 2, 4)
        self.zl = cand // 8
        self.x = lax.rem(rel, 4)
        self.zh = rel // 4
        self.z = self.zh * 2 + self.zl
        self.rel = rel

    def device(self, x=None, y=None, z=None, core=None):
        x = self.x if x is None else x
        y = self.y if y is None else y
        z = self.z if z is None else z
        core = self.core if core is None else core
        return ((lax.rem(z, 2) * 4 + y) * 2 + core, (z // 2) * 4 + x)


def turn(i, by):
    return lax.rem(i + by, 4)


def greet(devices):
    barrier = pltpu.get_barrier_semaphore()
    for device in devices:
        pl.semaphore_signal(barrier, inc=1, device_id=device, device_id_type=MESH)
    pl.semaphore_wait(barrier, len(devices))


class Mail:
    def __init__(self, send_sem, recv_sem):
        self.send_sem, self.recv_sem, self.count, self.sent = send_sem, recv_sem, 0, []

    def send(self, src, dst, device):
        i = self.count
        self.count += 1
        copy = pltpu.make_async_remote_copy(
            src_ref=src,
            dst_ref=dst,
            send_sem=self.send_sem.at[i],
            recv_sem=self.recv_sem.at[i],
            device_id=device,
            device_id_type=MESH,
        )
        copy.start()
        self.sent.append(copy)
        return copy

    def drain(self):
        for copy in self.sent:
            copy.wait_send()


WINDOW_PAD = 16


def sort_plan(ids, nrel):
    rows = ids.shape[1]
    block = 256
    named = (jnp.broadcast_to(ids, (nrel, rows)) == lax.broadcasted_iota(jnp.int32, (nrel, rows), 0)).astype(F32)
    before = (
        lax.broadcasted_iota(jnp.int32, (block, block), 0) < lax.broadcasted_iota(jnp.int32, (block, block), 1)
    ).astype(BF)
    running = jnp.zeros((nrel, 1), F32)
    ranks = []
    for b in range(rows // block):
        part = named[:, b * block : (b + 1) * block]
        ranks.append(jnp.dot(part.astype(BF), before, preferred_element_type=F32) + running)
        running = running + jnp.sum(part, axis=1, keepdims=True)
    rank = jnp.concatenate(ranks, axis=1)
    lower = (
        lax.broadcasted_iota(jnp.int32, (nrel, nrel), 1) < lax.broadcasted_iota(jnp.int32, (nrel, nrel), 0)
    ).astype(BF)
    starts = jnp.dot(lower, jnp.broadcast_to(running, (nrel, 128)).astype(BF), preferred_element_type=F32)
    place = jnp.sum(named * (rank + starts[:, 0:1]), axis=0, keepdims=True)
    return place, starts


def sort_rows(b, place, rows_ref, meta_ref, rows_out, picks_out, pos_out, part):
    rows = place.shape[1]
    block = 256
    here = pl.ds(b * block, block)
    spot = lax.broadcasted_iota(jnp.int32, (block, rows), 0) + b * block
    choose = (jnp.broadcast_to(place, (block, rows)) == spot).astype(F32).astype(BF)
    rows_out[here, :] = jnp.dot(choose, rows_ref[...], preferred_element_type=F32).astype(BF)
    meta = lax.dot_general(
        meta_ref[...], choose, (((1,), (1,)), ((), ())), preferred_element_type=F32
    ).astype(jnp.int32)
    named = picks_out.shape[0]
    picks_out[:, here] = meta[0:named]
    pos_out[:, here] = meta[named : named + 1] * part + meta[named + 1 : named + 2]


def group_queries(starts, rows_ref, matrix, out):
    k = pl.program_id(0)
    window = out_window(starts, k)
    rows = rows_ref[window[0], :]
    new = jnp.dot(rows, matrix[0], preferred_element_type=F32).astype(BF)
    out[window[0], :] = jnp.where(window[1], new, out[window[0], :])


def out_window(starts, k):
    size = 256 + WINDOW_PAD
    start, end = starts[k], starts[k + 1]
    base = pl.multiple_of(start // WINDOW_PAD * WINDOW_PAD, WINDOW_PAD)
    row = lax.broadcasted_iota(jnp.int32, (size, 512), 0) + base
    return pl.ds(base, size), (row >= start) & (row < end)


def make_queries(starts, rows, matrices):
    nrel, width, _ = matrices.shape
    return pl.pallas_call(
        group_queries,
        out_shape=jax.ShapeDtypeStruct(rows.shape, BF),
        grid_spec=pltpu.PrefetchScalarGridSpec(
            num_scalar_prefetch=1,
            grid=(nrel,),
            in_specs=[
                pl.BlockSpec(rows.shape, lambda k, s: (0, 0)),
                pl.BlockSpec((1, width, width), lambda k, s: (k, 0, 0)),
            ],
            out_specs=pl.BlockSpec(rows.shape, lambda k, s: (0, 0)),
        ),
        compiler_params=pltpu.CompilerParams(vmem_limit_bytes=20 << 20),
        name="make_queries",
    )(starts, rows, matrices)


def group_grads(starts, rows_ref, grads, matrix, back, terms):
    window, inside = out_window(starts, pl.program_id(0))
    grad = grads[window, :]
    new = lax.dot_general(grad, matrix[0], (((1,), (1,)), ((), ())), preferred_element_type=F32).astype(BF)
    back[window, :] = jnp.where(inside, new, back[window, :])
    rows = rows_ref[window, :]
    rows = jnp.where(inside, rows, jnp.zeros_like(rows))
    terms[0, 0] = lax.dot_general(rows, grad, (((0,), (0,)), ((), ())), preferred_element_type=F32).astype(BF)


def make_grads(starts, rows, grads, matrices):
    nrel, width, _ = matrices.shape
    whole = pl.BlockSpec(grads.shape, lambda k, s: (0, 0))
    return pl.pallas_call(
        group_grads,
        out_shape=(
            jax.ShapeDtypeStruct(grads.shape, BF),
            jax.ShapeDtypeStruct((2, nrel // 2, width, width), BF),
        ),
        grid_spec=pltpu.PrefetchScalarGridSpec(
            num_scalar_prefetch=1,
            grid=(nrel,),
            in_specs=[whole, whole, pl.BlockSpec((1, width, width), lambda k, s: (k, 0, 0))],
            out_specs=(
                whole,
                pl.BlockSpec((1, 1, width, width), lambda k, s: (lax.rem(k, 2), k // 2, 0, 0)),
            ),
        ),
        compiler_params=pltpu.CompilerParams(vmem_limit_bytes=20 << 20),
        name="make_grads",
    )(starts, rows, grads, matrices)


LOW = 64


def tally(stop, part, picks, pos, low, unit, packed):
    samples = 16
    rows = pos.shape[1]
    lanes = 128
    names = picks[pl.ds(pl.multiple_of(stop * samples, samples), samples), :]
    low[0:samples, :] = lax.bitwise_and(names, LOW - 1)
    unit[0:samples, :] = lax.shift_left(jnp.ones_like(names), 8 * lax.shift_right_logical(names, 6))
    place = pos[...] - stop * part
    inside = (place >= 0) & (place < part)
    place = jnp.where(inside, place, 0)
    low[samples : samples + 1, :] = lax.bitwise_and(place, LOW - 1)
    unit[samples : samples + 1, :] = jnp.where(
        inside, lax.shift_left(jnp.full_like(place, 33), 8 * lax.shift_right_logical(place, 6)), 0
    )

    def column(c, carry):
        here = pl.ds(pl.multiple_of(c * lanes, lanes), lanes)
        index = lax.broadcasted_iota(jnp.int32, (LOW, lanes), 0)
        total = jnp.zeros((LOW, lanes), jnp.int32)
        for k in range(samples + 1):
            match = jnp.broadcast_to(low[k : k + 1, here], (LOW, lanes)) == index
            total = total + jnp.where(match, jnp.broadcast_to(unit[k : k + 1, here], (LOW, lanes)), 0)
        packed[stop, :, here] = total
        return carry

    lax.fori_loop(0, rows // lanes, column, 0)


def gather_kernel(
    own, ids, rows_ref, picks, target, out, rows_out, packed, place_out, starts_out,
    meta, sorted_picks, sorted_target, low, unit, local_sem, send_sem, recv_sem,
):
    at = Spot()
    mail = Mail(send_sem, recv_sem)
    left, right = at.device(x=turn(at.x, 3)), at.device(x=turn(at.x, 1))
    down, up = at.device(y=turn(at.y, 3)), at.device(y=turn(at.y, 1))
    across = at.device(z=3 - at.z)
    partner = at.device(core=1 - at.core)
    greet([left, right, down, up, across, partner])
    half = own.shape[1] // 2
    share = half // 4

    def rows(start, size, step):
        return pl.ds(pl.multiple_of(start, step), size)

    start = at.core * half
    mine, first, second = rows(start, half, half), rows(start, half // 2, half), rows(start + half // 2, half // 2, half // 2)

    def quarter(y):
        return rows(start + y * share, share, share)

    def quarter_halves(y):
        return (
            rows(start + y * share, share // 2, share),
            rows(start + y * share + share // 2, share // 2, share // 2),
        )

    me, far = at.zh * 4, (1 - at.zh) * 4
    x0, x1, x2, x3 = at.x, turn(at.x, 1), turn(at.x, 2), turn(at.x, 3)
    y0, y1, y2, y3 = at.y, turn(at.y, 1), turn(at.y, 2), turn(at.y, 3)
    here = [
        pltpu.make_async_copy(own.at[0], out.at[at.rel, 0], local_sem.at[0]),
        pltpu.make_async_copy(own.at[1, quarter(y0)], out.at[at.rel, 1, quarter(y0)], local_sem.at[1]),
    ]
    for copy in here:
        copy.start()

    def same(ref, device):
        return mail.send(ref, ref, device)

    def a(base, x, rows):
        return out.at[base + x, 0, rows]

    def b(base, x, rows):
        return out.at[base + x, 1, rows]

    def b4(base, rows):
        return out.at[pl.ds(base, 4), 1, rows]

    own_a, own_b = own.at[0, mine], own.at[1, quarter(y0)]
    b_across = mail.send(own_b, b(me, x0, quarter(y0)), across)
    b_right = mail.send(own_b, b(me, x0, quarter(y0)), right)
    b_left = mail.send(own_b, b(me, x0, quarter(y0)), left)
    a_across = mail.send(own_a, a(me, x0, mine), across)
    a_right = mail.send(own_a, a(me, x0, mine), right)
    a_left = mail.send(own_a, a(me, x0, mine), left)

    stops, samples, total = picks.shape
    part = total // stops
    nrel = starts_out.shape[0]
    place, starts = sort_plan(ids[...], nrel)
    place = place.astype(jnp.int32)
    place_out[...] = place
    starts_out[...] = starts.astype(jnp.int32)
    for s in range(stops):
        meta[s * samples : (s + 1) * samples, :] = picks[s].astype(F32).astype(BF)
    goal = target[...]
    tail = lax.broadcasted_iota(jnp.int32, (16, total), 0)
    meta[stops * samples :, :] = jnp.where(
        tail == 0, jnp.broadcast_to(goal // part, (16, total)), jnp.broadcast_to(lax.rem(goal, part), (16, total))
    ).astype(F32).astype(BF)
    rows_out[total:, :] = jnp.zeros((rows_out.shape[0] - total, rows_out.shape[1]), BF)

    def work(b):
        sort_rows(b, place_out[...], rows_ref, meta, rows_out, sorted_picks, sorted_target, part)

    def count(s):
        tally(s, part, sorted_picks, sorted_target, low, unit, packed)

    work(0)
    h0, h1 = quarter_halves(y0)
    b_right.wait_recv()
    b_on_right = same(b(me, x3, h0), right)
    b_left.wait_recv()
    b_on_left = same(b(me, x1, h1), left)
    b_across.wait_recv()
    b_far_right = same(b(far, x0, quarter(y0)), right)
    b_far_left = same(b(far, x0, quarter(y0)), left)
    work(1)
    a_right.wait_recv()
    a_on_right = same(a(me, x3, first), right)
    gifts = [same(a(me, x3, mine), partner)]
    a_left.wait_recv()
    a_on_left = same(a(me, x1, second), left)
    gifts.append(same(a(me, x1, mine), partner))
    work(2)
    b_on_right.wait_recv()
    b_on_left.wait_recv()
    here[1].wait()
    me_up, me_down = same(b4(me, quarter(y0)), up), same(b4(me, quarter(y0)), down)
    b_far_right.wait_recv()
    b_far_on_right = same(b(far, x3, h0), right)
    b_far_left.wait_recv()
    b_far_on_left = same(b(far, x1, h1), left)
    work(3)
    a_across.wait_recv()
    a_far_right = same(a(far, x0, mine), right)
    a_far_left = same(a(far, x0, mine), left)
    gifts.append(same(a(far, x0, mine), partner))
    work(4)
    b_far_on_right.wait_recv()
    b_far_on_left.wait_recv()
    far_up, far_down = same(b4(far, quarter(y0)), up), same(b4(far, quarter(y0)), down)
    a_on_right.wait_recv()
    a_opposite = [same(a(me, x2, first), across)]
    a_on_left.wait_recv()
    a_opposite.append(same(a(me, x2, second), across))
    gifts.append(same(a(me, x2, mine), partner))
    work(5)
    me_up.wait_recv()
    me_on_up = same(b4(me, quarter_halves(y3)[0]), up)
    me_down.wait_recv()
    me_on_down = same(b4(me, quarter_halves(y1)[1]), down)
    work(6)
    work(7)
    count(0)
    far_up.wait_recv()
    far_on_up = same(b4(far, quarter_halves(y3)[0]), up)
    far_down.wait_recv()
    far_on_down = same(b4(far, quarter_halves(y1)[1]), down)
    count(1)
    a_far_right.wait_recv()
    gifts.append(same(a(far, x3, mine), partner))
    a_far_left.wait_recv()
    gifts.append(same(a(far, x1, mine), partner))
    count(2)
    me_on_up.wait_recv()
    me_on_down.wait_recv()
    gifts.append(same(b4(me, mine), partner))
    for copy in a_opposite:
        copy.wait_recv()
    gifts.append(same(a(far, x2, mine), partner))
    count(3)
    count(4)
    far_on_up.wait_recv()
    far_on_down.wait_recv()
    gifts.append(same(b4(far, mine), partner))

    def later(s, carry):
        count(s)
        return carry

    lax.fori_loop(5, stops, later, 0)
    for copy in gifts:
        copy.wait_recv()
    mail.drain()
    here[0].wait()


def gather_relations(relations, ids, rows, picks, target):
    per, width, _ = relations.shape
    owners = lax.axis_size("rel")
    nrel = owners * per
    stops, samples, total = picks.shape
    vmem = pl.BlockSpec(memory_space=pltpu.VMEM)
    out = pl.pallas_call(
        gather_kernel,
        out_shape=(
            jax.ShapeDtypeStruct((owners, per, width, width), relations.dtype),
            jax.ShapeDtypeStruct((total + 256 + WINDOW_PAD, width), BF),
            jax.ShapeDtypeStruct((stops, LOW, total), jnp.int32),
            jax.ShapeDtypeStruct((1, total), jnp.int32),
            jax.ShapeDtypeStruct((nrel, 128), jnp.int32),
        ),
        in_specs=[vmem] * 5,
        out_specs=(pl.BlockSpec(memory_space=pl.ANY), *[vmem] * 4),
        scratch_shapes=[
            pltpu.VMEM((stops * samples + 16, total), BF),
            pltpu.VMEM((stops * samples, total), jnp.int32),
            pltpu.VMEM((1, total), jnp.int32),
            pltpu.VMEM((24, total), jnp.int32),
            pltpu.VMEM((24, total), jnp.int32),
            pltpu.SemaphoreType.DMA((2,)),
            pltpu.SemaphoreType.DMA((36,)),
            pltpu.SemaphoreType.DMA((36,)),
        ],
        compiler_params=pltpu.CompilerParams(
            collective_id=0, has_side_effects=True, vmem_limit_bytes=24 << 20
        ),
        name="gather_relations",
    )(relations, ids, rows, picks, target)
    matrices, rows, packed, place, starts = out
    starts = jnp.concatenate([starts[:, 0], jnp.full((1,), total, jnp.int32)])
    return matrices.reshape(nrel, width, width), rows, packed, place, starts


STOPS = 8
learn_rate = 0.005


def stops_kernel(
    q, packed, entities, state_out, grad_out, held, sent, wide, turned_wide, weights, acc, local_sem, send_sem, recv_sem
):
    cand, rel = lax.axis_index("cand"), lax.axis_index("rel")
    n = lax.axis_size("cand")
    ahead, behind = (lax.rem(cand + 1, n), rel), (lax.rem(cand + n - 1, n), rel)
    greet([ahead, behind])
    part, width = entities.shape
    rows = packed.shape[2]
    chunk = part // 2
    block = 256

    fetch = [
        pltpu.make_async_copy(entities.at[pl.ds(h * chunk, chunk)], held.at[h], local_sem.at[h])
        for h in range(2)
    ]
    for copy in fetch:
        copy.start()
    acc[...] = jnp.zeros_like(acc)
    for copy in fetch:
        copy.wait()

    def hop(t):
        return pltpu.make_async_remote_copy(
            src_ref=sent.at[t],
            dst_ref=held.at[t + 2],
            send_sem=send_sem.at[t],
            recv_sem=recv_sem.at[t],
            device_id=ahead,
            device_id_type=MESH,
        )

    def step(t, carry):
        half = lax.rem(t, 2)
        stop = t // 2
        here_rows = pl.ds(pl.multiple_of(half * chunk, chunk), chunk)

        @pl.when(t >= 2)
        def _():
            hop(t - 2).wait_recv()

        state = held[t]
        rounded = state.astype(BF)
        wide[here_rows, :] = rounded
        pieces = []
        for i in range(rows // block):
            here = pl.ds(i * block, block)
            logits = lax.dot_general(
                rounded, q[here, :], (((1,), (1,)), ((), ())), preferred_element_type=F32
            )
            marks = packed[stop, :, here]
            marks = jnp.concatenate(
                [lax.shift_right_logical(marks, 16 * half + 8 * p) for p in range(chunk // LOW)], axis=0
            )
            named = lax.bitwise_and(marks, 31).astype(F32)
            chance = 1.0 / (1.0 + jnp.exp(-logits))
            product = named * chance
            pieces.append(jnp.where(lax.bitwise_and(marks, 32) != 0, product - 1.0, product).astype(BF))
        weight = jnp.concatenate(pieces, axis=1)
        weights[here_rows, :] = weight
        change = jnp.dot(weight, q[0:rows, :], preferred_element_type=F32)
        sent[t] = state - learn_rate * change

        @pl.when(t < 2 * STOPS - 2)
        def _():
            hop(t).start()

        @pl.when(half == 1)
        def _():
            turned_wide[...] = wide[...].astype(F32).T.astype(BF)
            big = 512

            def gather(c, carry):
                here = pl.ds(pl.multiple_of(c * big, big), big)
                acc[:, here] += jnp.dot(turned_wide[...], weights[:, here], preferred_element_type=F32)
                return carry

            lax.fori_loop(0, rows // big, gather, 0)

        return carry

    lax.fori_loop(0, 2 * STOPS, step, 0)
    for h in range(2):
        state_out[pl.ds(h * chunk, chunk), :] = sent[2 * STOPS - 2 + h]

    def turned(c, carry):
        here = pl.ds(pl.multiple_of(c * block, block), block)
        grad_out[here, :] = acc[:, here].T.astype(BF)
        return carry

    lax.fori_loop(0, rows // block, turned, 0)
    grad_out[rows:, :] = jnp.zeros((grad_out.shape[0] - rows, width), BF)

    def drained(t, carry):
        hop(t).wait_send()
        return carry

    lax.fori_loop(0, 2 * STOPS - 2, drained, 0)


def run_stops(queries, packed, entities):
    padded, width = queries.shape
    rows = packed.shape[2]
    part = entities.shape[0]
    chunk = part // 2
    vmem = pl.BlockSpec(memory_space=pltpu.VMEM)
    hops = 2 * STOPS
    return pl.pallas_call(
        stops_kernel,
        out_shape=(
            jax.ShapeDtypeStruct((part, width), F32),
            jax.ShapeDtypeStruct((padded, width), BF),
        ),
        in_specs=[vmem, vmem, pl.BlockSpec(memory_space=pl.ANY)],
        out_specs=(vmem, vmem),
        scratch_shapes=[
            pltpu.VMEM((hops, chunk, width), F32),
            pltpu.VMEM((hops, chunk, width), F32),
            pltpu.VMEM((part, width), BF),
            pltpu.VMEM((width, part), BF),
            pltpu.VMEM((part, rows), BF),
            pltpu.VMEM((width, rows), F32),
            pltpu.SemaphoreType.DMA((2,)),
            pltpu.SemaphoreType.DMA((hops,)),
            pltpu.SemaphoreType.DMA((hops,)),
        ],
        compiler_params=pltpu.CompilerParams(
            collective_id=2, has_side_effects=True, vmem_limit_bytes=28 << 20
        ),
        name="run_stops",
    )(queries, packed, entities)


def add_into(dst, *others):
    lead = dst.shape[:-2]
    total = 1
    for n in lead:
        total *= n

    def body(i, carry):
        index, rest = [], i
        for n in reversed(lead):
            index.insert(0, lax.rem(rest, n))
            rest = rest // n
        value = dst[tuple(index)].astype(F32)
        for other in others:
            value = value + other[tuple(index)].astype(F32)
        dst[tuple(index)] = value.astype(dst.dtype)
        return carry

    lax.fori_loop(0, total, body, 0)


class Ring:
    def __init__(self, mail, place, ahead, behind, piece, halves, land_half, land_full):
        self.mail, self.place, self.ahead, self.behind = mail, place, ahead, behind
        self.piece, self.halves, self.land_half, self.land_full = piece, halves, land_half, land_full

    def one(self):
        far = turn(self.place, 2)
        self.h = [
            self.mail.send(self.halves(self.piece(far))[d], self.land_half[d], device)
            for d, device in enumerate((self.ahead, self.behind))
        ]

    def two(self):
        self.f = []
        for d, (step, device) in enumerate(((1, self.ahead), (3, self.behind))):
            self.h[d].wait_recv()
            target = self.piece(turn(self.place, step))
            add_into(self.halves(target)[d], self.land_half[d])
            self.f.append(self.mail.send(target, self.land_full[d], device))

    def three(self):
        for copy in self.f:
            copy.wait_recv()
        return self.piece(self.place), self.land_full


def scatter_kernel(
    place, terms, back, out, source_grad, got,
    ax_h, ax_f, ay_h, ay_f, az_h, az_f, by_h, by_f, bx_h, bx_f, bz_h, bz_f, swap_send, swap_recv, send_sem, recv_sem
):
    at = Spot()
    mail = Mail(send_sem, recv_sem)
    partner = at.device(core=1 - at.core)
    xs = at.device(x=turn(at.x, 1)), at.device(x=turn(at.x, 3))
    ys = at.device(y=turn(at.y, 1)), at.device(y=turn(at.y, 3))
    zs = at.device(z=turn(at.z, 1)), at.device(z=turn(at.z, 3))
    greet([partner, *xs, *ys, *zs])

    def swap(j, r):
        zh, x = r // 4, lax.rem(r, 4)
        return pltpu.make_async_remote_copy(
            src_ref=terms.at[j, zh, x, :, :, 1 - at.core],
            dst_ref=got.at[j, zh, x],
            send_sem=swap_send.at[j, r],
            recv_sem=swap_recv.at[j, r],
            device_id=partner,
            device_id_type=MESH,
        )

    def offer(i, carry):
        swap(i // 8, lax.rem(i, 8)).start()
        return carry

    lax.fori_loop(0, 16, offer, 0)

    def joined(j):
        def one(r, carry):
            swap(j, r).wait_recv()
            zh, x = r // 4, lax.rem(r, 4)
            add_into(got.at[j, zh, x], terms.at[j, zh, x, :, :, at.core])
            return carry

        lax.fori_loop(0, 8, one, 0)

    def unsort(begin, end):
        lanes = 128
        total = place.shape[1]

        def one(b, carry):
            here = pl.ds(pl.multiple_of(b * lanes, lanes), lanes)
            mine = jnp.broadcast_to(place[:, here], (lanes, lanes)).T
            index = lax.broadcasted_iota(jnp.int32, (lanes, lanes), 1)
            choose = jnp.concatenate(
                [(mine == index + t * lanes).astype(F32).astype(BF) for t in range(total // lanes)], axis=1
            )
            source_grad[here, :] = jnp.dot(choose, back[0:total, :], preferred_element_type=F32).astype(BF)
            return carry

        lax.fori_loop(begin, end, one, 0)


    def first_half(ref):
        return ref.at[0], ref.at[1]

    def row_halves(ref):
        rows = ref.shape[0] // 2
        return ref.at[pl.ds(0, rows)], ref.at[pl.ds(rows, rows)]

    def two(ref):
        return ref.at[0], ref.at[1]

    a, b = got.at[0], got.at[1]
    ax = Ring(mail, at.x, *xs, lambda t: a.at[:, t], first_half, two(ax_h), two(ax_f))
    a1 = lambda: a.at[:, at.x]
    ay = Ring(mail, at.y, *ys, lambda t: a1().at[:, :, t], first_half, two(ay_h), two(ay_f))
    a2 = lambda z: a.at[z // 2, at.x, lax.rem(z, 2), at.y]
    az = Ring(mail, at.z, *zs, a2, row_halves, two(az_h), two(az_f))
    by = Ring(mail, at.y, *ys, lambda t: b.at[:, :, :, t], first_half, two(by_h), two(by_f))
    bx = Ring(mail, at.x, *xs, lambda t: b.at[:, t, :, at.y], first_half, two(bx_h), two(bx_f))
    b2 = lambda z: b.at[z // 2, at.x, lax.rem(z, 2), at.y]
    bz = Ring(mail, at.z, *zs, b2, row_halves, two(bz_h), two(bz_f))

    for j, ring in enumerate((ax, by)):
        joined(j)
        ring.one()
    unsort(0, 4)
    ax.two()
    by.two()
    unsort(4, 12)
    for ring, following in ((ax, ay), (by, bx)):
        piece, landed = ring.three()
        add_into(piece, *landed)
        following.one()
    unsort(12, 14)
    ay.two()
    bx.two()
    unsort(14, 16)
    for ring, following in ((ay, az), (bx, bz)):
        piece, landed = ring.three()
        add_into(piece, *landed)
        following.one()
    az.two()
    bz.two()
    for j, ring in enumerate((az, bz)):
        piece, landed = ring.three()
        out[:, j, :] = piece[...].astype(F32) + landed[0][...].astype(F32) + landed[1][...].astype(F32)

    def sent(i, carry):
        swap(i // 8, lax.rem(i, 8)).wait_send()
        return carry

    lax.fori_loop(0, 16, sent, 0)
    mail.drain()


def scatter_grads(place, terms, back):
    width = back.shape[1]
    total = place.shape[1]
    rows = width // 16
    terms = terms.reshape(2, 2, 4, 2, 4, 2, rows, width)
    v = lambda *lead: pltpu.VMEM((*lead, rows, width), BF)
    z = lambda r: pltpu.VMEM((2, r, width), BF)
    vmem = pl.BlockSpec(memory_space=pltpu.VMEM)
    return pl.pallas_call(
        scatter_kernel,
        out_shape=(jax.ShapeDtypeStruct((rows, 2, width), F32), jax.ShapeDtypeStruct((total, width), BF)),
        in_specs=[vmem, vmem, vmem],
        out_specs=(vmem, vmem),
        scratch_shapes=[
            v(2, 2, 4, 2, 4),
            v(2, 2, 4), v(2, 2, 2, 4), v(2, 2), v(2, 2, 2), z(rows // 2), v(2),
            v(2, 4, 2), v(2, 2, 4, 2), v(2, 2), v(2, 2, 2), z(rows // 2), v(2),
            pltpu.SemaphoreType.DMA((2, 8)),
            pltpu.SemaphoreType.DMA((2, 8)),
            pltpu.SemaphoreType.DMA((24,)),
            pltpu.SemaphoreType.DMA((24,)),
        ],
        compiler_params=pltpu.CompilerParams(
            collective_id=1, has_side_effects=True, vmem_limit_bytes=30 << 20
        ),
        name="scatter_grads",
    )(place, terms, back)


def shards(source_rows, rel_ids, relations, entities, pos_slot, negatives):
    rows = source_rows.shape[0]
    matrices, sorted_rows, packed, place, starts = gather_relations(
        relations,
        rel_ids.reshape(1, rows),
        source_rows,
        jnp.transpose(negatives, (0, 2, 1)),
        pos_slot.reshape(1, rows),
    )
    queries = make_queries(starts, sorted_rows, matrices)
    state, query_grad = run_stops(queries, packed, entities)
    back, terms = make_grads(starts, sorted_rows, query_grad, matrices)
    relation_grad, source_grad = scatter_grads(place, terms, back)
    return (state, source_grad, relation_grad)


def solution(mesh):
    placed = (
        P(("cand", "rel"), None),
        P(("cand", "rel"), None),
        P("rel", None, None),
        P(("cand", "rel"), None),
        P(("cand", "rel")),
        P(None, ("cand", "rel"), None),
    )
    return jax.shard_map(
        shards,
        mesh=mesh,
        in_specs=placed,
        out_specs=(P(("cand", "rel"), None), P(("cand", "rel"), None), P("cand", "rel", None)),
        check_vma=False,
    )
```

```python
import functools

import jax
import jax.numpy as jnp
from jax import lax
from jax.experimental import pallas as pl
from jax.experimental.pallas import tpu as pltpu
from jax.sharding import PartitionSpec as P

MESH = pl.DeviceIdType.MESH
BF = jnp.bfloat16
F32 = jnp.float32


class Spot:
    def __init__(self):
        cand, rel = lax.axis_index("cand"), lax.axis_index("rel")
        self.core = lax.rem(cand, 2)
        self.y = lax.rem(cand // 2, 4)
        self.zl = cand // 8
        self.x = lax.rem(rel, 4)
        self.zh = rel // 4
        self.z = self.zh * 2 + self.zl
        self.rel = rel

    def device(self, x=None, y=None, z=None, core=None):
        x = self.x if x is None else x
        y = self.y if y is None else y
        z = self.z if z is None else z
        core = self.core if core is None else core
        return ((lax.rem(z, 2) * 4 + y) * 2 + core, (z // 2) * 4 + x)


def turn(i, by):
    return lax.rem(i + by, 4)


def greet(devices):
    barrier = pltpu.get_barrier_semaphore()
    for device in devices:
        pl.semaphore_signal(barrier, inc=1, device_id=device, device_id_type=MESH)
    pl.semaphore_wait(barrier, len(devices))


class Mail:
    def __init__(self, send_sem, recv_sem):
        self.send_sem, self.recv_sem, self.count, self.sent = send_sem, recv_sem, 0, []

    def send(self, src, dst, device):
        i = self.count
        self.count += 1
        copy = pltpu.make_async_remote_copy(
            src_ref=src,
            dst_ref=dst,
            send_sem=self.send_sem.at[i],
            recv_sem=self.recv_sem.at[i],
            device_id=device,
            device_id_type=MESH,
        )
        copy.start()
        self.sent.append(copy)
        return copy

    def drain(self):
        for copy in self.sent:
            copy.wait_send()


WINDOW_PAD = 16


def sort_plan(ids, nrel):
    rows = ids.shape[1]
    block = 256
    named = (jnp.broadcast_to(ids, (nrel, rows)) == lax.broadcasted_iota(jnp.int32, (nrel, rows), 0)).astype(F32)
    before = (
        lax.broadcasted_iota(jnp.int32, (block, block), 0) < lax.broadcasted_iota(jnp.int32, (block, block), 1)
    ).astype(BF)
    running = jnp.zeros((nrel, 1), F32)
    ranks = []
    for b in range(rows // block):
        part = named[:, b * block : (b + 1) * block]
        ranks.append(jnp.dot(part.astype(BF), before, preferred_element_type=F32) + running)
        running = running + jnp.sum(part, axis=1, keepdims=True)
    rank = jnp.concatenate(ranks, axis=1)
    lower = (
        lax.broadcasted_iota(jnp.int32, (nrel, nrel), 1) < lax.broadcasted_iota(jnp.int32, (nrel, nrel), 0)
    ).astype(BF)
    starts = jnp.dot(lower, jnp.broadcast_to(running, (nrel, 128)).astype(BF), preferred_element_type=F32)
    place = jnp.sum(named * (rank + starts[:, 0:1]), axis=0, keepdims=True)
    return place, starts


def sort_rows(b, place, rows_ref, meta_ref, rows_out, picks_out, pos_out, part):
    rows = place.shape[1]
    block = 256
    here = pl.ds(b * block, block)
    spot = lax.broadcasted_iota(jnp.int32, (block, rows), 0) + b * block
    choose = (jnp.broadcast_to(place, (block, rows)) == spot).astype(F32).astype(BF)
    rows_out[here, :] = jnp.dot(choose, rows_ref[...], preferred_element_type=F32).astype(BF)
    meta = lax.dot_general(
        meta_ref[...], choose, (((1,), (1,)), ((), ())), preferred_element_type=F32
    ).astype(jnp.int32)
    named = picks_out.shape[0]
    picks_out[:, here] = meta[0:named]
    pos_out[:, here] = meta[named : named + 1] * part + meta[named + 1 : named + 2]


def group_queries(starts, rows_ref, matrix, out):
    k = pl.program_id(0)
    window = out_window(starts, k)
    rows = rows_ref[window[0], :]
    new = jnp.dot(rows, matrix[0], preferred_element_type=F32).astype(BF)
    out[window[0], :] = jnp.where(window[1], new, out[window[0], :])


def out_window(starts, k):
    size = 256 + WINDOW_PAD
    start, end = starts[k], starts[k + 1]
    base = pl.multiple_of(start // WINDOW_PAD * WINDOW_PAD, WINDOW_PAD)
    row = lax.broadcasted_iota(jnp.int32, (size, 512), 0) + base
    return pl.ds(base, size), (row >= start) & (row < end)


def make_queries(starts, rows, matrices):
    nrel, width, _ = matrices.shape
    return pl.pallas_call(
        group_queries,
        out_shape=jax.ShapeDtypeStruct(rows.shape, BF),
        grid_spec=pltpu.PrefetchScalarGridSpec(
            num_scalar_prefetch=1,
            grid=(nrel,),
            in_specs=[
                pl.BlockSpec(rows.shape, lambda k, s: (0, 0)),
                pl.BlockSpec((1, width, width), lambda k, s: (k, 0, 0)),
            ],
            out_specs=pl.BlockSpec(rows.shape, lambda k, s: (0, 0)),
        ),
        compiler_params=pltpu.CompilerParams(vmem_limit_bytes=20 << 20),
        name="make_queries",
    )(starts, rows, matrices)


def group_grads(starts, rows_ref, grads, matrix, back, terms):
    window, inside = out_window(starts, pl.program_id(0))
    grad = grads[window, :]
    new = lax.dot_general(grad, matrix[0], (((1,), (1,)), ((), ())), preferred_element_type=F32).astype(BF)
    back[window, :] = jnp.where(inside, new, back[window, :])
    rows = rows_ref[window, :]
    rows = jnp.where(inside, rows, jnp.zeros_like(rows))
    terms[0, 0] = lax.dot_general(rows, grad, (((0,), (0,)), ((), ())), preferred_element_type=F32).astype(BF)


def make_grads(starts, rows, grads, matrices):
    nrel, width, _ = matrices.shape
    whole = pl.BlockSpec(grads.shape, lambda k, s: (0, 0))
    return pl.pallas_call(
        group_grads,
        out_shape=(
            jax.ShapeDtypeStruct(grads.shape, BF),
            jax.ShapeDtypeStruct((2, nrel // 2, width, width), BF),
        ),
        grid_spec=pltpu.PrefetchScalarGridSpec(
            num_scalar_prefetch=1,
            grid=(nrel,),
            in_specs=[whole, whole, pl.BlockSpec((1, width, width), lambda k, s: (k, 0, 0))],
            out_specs=(
                whole,
                pl.BlockSpec((1, 1, width, width), lambda k, s: (lax.rem(k, 2), k // 2, 0, 0)),
            ),
        ),
        compiler_params=pltpu.CompilerParams(vmem_limit_bytes=20 << 20),
        name="make_grads",
    )(starts, rows, grads, matrices)


LOW = 64


def tally(stop, part, picks, pos, low, unit, packed):
    samples = 16
    rows = pos.shape[1]
    lanes = 128
    names = picks[pl.ds(pl.multiple_of(stop * samples, samples), samples), :]
    low[0:samples, :] = lax.bitwise_and(names, LOW - 1)
    unit[0:samples, :] = lax.shift_left(jnp.ones_like(names), 8 * lax.shift_right_logical(names, 6))
    place = pos[...] - stop * part
    inside = (place >= 0) & (place < part)
    place = jnp.where(inside, place, 0)
    low[samples : samples + 1, :] = lax.bitwise_and(place, LOW - 1)
    unit[samples : samples + 1, :] = jnp.where(
        inside, lax.shift_left(jnp.full_like(place, 33), 8 * lax.shift_right_logical(place, 6)), 0
    )

    def column(c, carry):
        here = pl.ds(pl.multiple_of(c * lanes, lanes), lanes)
        index = lax.broadcasted_iota(jnp.int32, (LOW, lanes), 0)
        total = jnp.zeros((LOW, lanes), jnp.int32)
        for k in range(samples + 1):
            match = jnp.broadcast_to(low[k : k + 1, here], (LOW, lanes)) == index
            total = total + jnp.where(match, jnp.broadcast_to(unit[k : k + 1, here], (LOW, lanes)), 0)
        packed[stop, :, here] = total
        return carry

    lax.fori_loop(0, rows // lanes, column, 0)


def gather_kernel(
    own_in, ids_in, rows_in, picks_in, target_in, out, rows_out, packed, place_out, starts_out,
    own, ids, rows_ref, picks, target,
    meta, sorted_picks, sorted_target, low, unit, local_sem, fetch_sem, send_sem, recv_sem,
):
    at = Spot()
    mail = Mail(send_sem, recv_sem)
    left, right = at.device(x=turn(at.x, 3)), at.device(x=turn(at.x, 1))
    down, up = at.device(y=turn(at.y, 3)), at.device(y=turn(at.y, 1))
    across = at.device(z=3 - at.z)
    partner = at.device(core=1 - at.core)
    fetch = [
        pltpu.make_async_copy(source, landing, fetch_sem.at[i])
        for i, (source, landing) in enumerate(
            ((own_in, own), (ids_in, ids), (target_in, target), (picks_in, picks), (rows_in, rows_ref))
        )
    ]
    for copy in fetch:
        copy.start()
    greet([left, right, down, up, across, partner])
    fetch[0].wait()
    half = own.shape[1] // 2
    share = half // 4

    def rows(start, size, step):
        return pl.ds(pl.multiple_of(start, step), size)

    start = at.core * half
    mine, first, second = rows(start, half, half), rows(start, half // 2, half), rows(start + half // 2, half // 2, half // 2)

    def quarter(y):
        return rows(start + y * share, share, share)

    def quarter_halves(y):
        return (
            rows(start + y * share, share // 2, share),
            rows(start + y * share + share // 2, share // 2, share // 2),
        )

    me, far = at.zh * 4, (1 - at.zh) * 4
    x0, x1, x2, x3 = at.x, turn(at.x, 1), turn(at.x, 2), turn(at.x, 3)
    y0, y1, y2, y3 = at.y, turn(at.y, 1), turn(at.y, 2), turn(at.y, 3)
    here = [
        pltpu.make_async_copy(own.at[0], out.at[at.rel, 0], local_sem.at[0]),
        pltpu.make_async_copy(own.at[1, quarter(y0)], out.at[at.rel, 1, quarter(y0)], local_sem.at[1]),
    ]
    for copy in here:
        copy.start()

    def same(ref, device):
        return mail.send(ref, ref, device)

    def a(base, x, rows):
        return out.at[base + x, 0, rows]

    def b(base, x, rows):
        return out.at[base + x, 1, rows]

    def b4(base, rows):
        return out.at[pl.ds(base, 4), 1, rows]

    own_a, own_b = own.at[0, mine], own.at[1, quarter(y0)]
    b_across = mail.send(own_b, b(me, x0, quarter(y0)), across)
    b_right = mail.send(own_b, b(me, x0, quarter(y0)), right)
    b_left = mail.send(own_b, b(me, x0, quarter(y0)), left)
    a_across = mail.send(own_a, a(me, x0, mine), across)
    a_right = mail.send(own_a, a(me, x0, mine), right)
    a_left = mail.send(own_a, a(me, x0, mine), left)

    stops, samples, total = picks.shape
    part = total // stops
    nrel = starts_out.shape[0]
    for copy in fetch[1:]:
        copy.wait()
    place, starts = sort_plan(ids[...], nrel)
    place = place.astype(jnp.int32)
    place_out[...] = place
    starts_out[...] = starts.astype(jnp.int32)
    for s in range(stops):
        meta[s * samples : (s + 1) * samples, :] = picks[s].astype(F32).astype(BF)
    goal = target[...]
    tail = lax.broadcasted_iota(jnp.int32, (16, total), 0)
    meta[stops * samples :, :] = jnp.where(
        tail == 0, jnp.broadcast_to(goal // part, (16, total)), jnp.broadcast_to(lax.rem(goal, part), (16, total))
    ).astype(F32).astype(BF)
    rows_out[total:, :] = jnp.zeros((rows_out.shape[0] - total, rows_out.shape[1]), BF)

    def work(b):
        sort_rows(b, place_out[...], rows_ref, meta, rows_out, sorted_picks, sorted_target, part)

    def count(s):
        tally(s, part, sorted_picks, sorted_target, low, unit, packed)

    work(0)
    h0, h1 = quarter_halves(y0)
    b_right.wait_recv()
    b_on_right = same(b(me, x3, h0), right)
    b_left.wait_recv()
    b_on_left = same(b(me, x1, h1), left)
    b_across.wait_recv()
    b_far_right = same(b(far, x0, quarter(y0)), right)
    b_far_left = same(b(far, x0, quarter(y0)), left)
    work(1)
    a_right.wait_recv()
    a_on_right = same(a(me, x3, first), right)
    gifts = [same(a(me, x3, mine), partner)]
    a_left.wait_recv()
    a_on_left = same(a(me, x1, second), left)
    gifts.append(same(a(me, x1, mine), partner))
    work(2)
    b_on_right.wait_recv()
    b_on_left.wait_recv()
    here[1].wait()
    me_up, me_down = same(b4(me, quarter(y0)), up), same(b4(me, quarter(y0)), down)
    b_far_right.wait_recv()
    b_far_on_right = same(b(far, x3, h0), right)
    b_far_left.wait_recv()
    b_far_on_left = same(b(far, x1, h1), left)
    work(3)
    a_across.wait_recv()
    a_far_right = same(a(far, x0, mine), right)
    a_far_left = same(a(far, x0, mine), left)
    gifts.append(same(a(far, x0, mine), partner))
    work(4)
    b_far_on_right.wait_recv()
    b_far_on_left.wait_recv()
    far_up, far_down = same(b4(far, quarter(y0)), up), same(b4(far, quarter(y0)), down)
    a_on_right.wait_recv()
    a_opposite = [same(a(me, x2, first), across)]
    a_on_left.wait_recv()
    a_opposite.append(same(a(me, x2, second), across))
    gifts.append(same(a(me, x2, mine), partner))
    work(5)
    me_up.wait_recv()
    me_on_up = same(b4(me, quarter_halves(y3)[0]), up)
    me_down.wait_recv()
    me_on_down = same(b4(me, quarter_halves(y1)[1]), down)
    work(6)
    work(7)
    count(0)
    far_up.wait_recv()
    far_on_up = same(b4(far, quarter_halves(y3)[0]), up)
    far_down.wait_recv()
    far_on_down = same(b4(far, quarter_halves(y1)[1]), down)
    count(1)
    a_far_right.wait_recv()
    gifts.append(same(a(far, x3, mine), partner))
    a_far_left.wait_recv()
    gifts.append(same(a(far, x1, mine), partner))
    count(2)
    me_on_up.wait_recv()
    me_on_down.wait_recv()
    gifts.append(same(b4(me, mine), partner))
    for copy in a_opposite:
        copy.wait_recv()
    gifts.append(same(a(far, x2, mine), partner))
    count(3)
    count(4)
    far_on_up.wait_recv()
    far_on_down.wait_recv()
    gifts.append(same(b4(far, mine), partner))

    def later(s, carry):
        count(s)
        return carry

    lax.fori_loop(5, stops, later, 0)
    for copy in gifts:
        copy.wait_recv()
    mail.drain()
    here[0].wait()


def gather_relations(relations, ids, rows, picks, target):
    per, width, _ = relations.shape
    owners = lax.axis_size("rel")
    nrel = owners * per
    stops, samples, total = picks.shape
    vmem = pl.BlockSpec(memory_space=pltpu.VMEM)
    out = pl.pallas_call(
        gather_kernel,
        out_shape=(
            jax.ShapeDtypeStruct((owners, per, width, width), relations.dtype),
            jax.ShapeDtypeStruct((total + 256 + WINDOW_PAD, width), BF),
            jax.ShapeDtypeStruct((stops, LOW, total), jnp.int32),
            jax.ShapeDtypeStruct((1, total), jnp.int32),
            jax.ShapeDtypeStruct((nrel, 128), jnp.int32),
        ),
        in_specs=[pl.BlockSpec(memory_space=pltpu.HBM)] * 5,
        out_specs=(pl.BlockSpec(memory_space=pl.ANY), *[vmem] * 4),
        scratch_shapes=[
            *(pltpu.VMEM(a.shape, a.dtype) for a in (relations, ids, rows, picks, target)),
            pltpu.VMEM((stops * samples + 16, total), BF),
            pltpu.VMEM((stops * samples, total), jnp.int32),
            pltpu.VMEM((1, total), jnp.int32),
            pltpu.VMEM((24, total), jnp.int32),
            pltpu.VMEM((24, total), jnp.int32),
            pltpu.SemaphoreType.DMA((2,)),
            pltpu.SemaphoreType.DMA((5,)),
            pltpu.SemaphoreType.DMA((36,)),
            pltpu.SemaphoreType.DMA((36,)),
        ],
        compiler_params=pltpu.CompilerParams(
            collective_id=0, has_side_effects=True, vmem_limit_bytes=24 << 20
        ),
        name="gather_relations",
    )(relations, ids, rows, picks, target)
    matrices, rows, packed, place, starts = out
    starts = jnp.concatenate([starts[:, 0], jnp.full((1,), total, jnp.int32)])
    return matrices.reshape(nrel, width, width), rows, packed, place, starts


STOPS = 8
learn_rate = 0.005
LOG2E = 1.4426950408889634


def stops_kernel(
    q, packed, entities, state_out, grad_out, held, sent, held_short, sent_short, now, wide, turned_wide, weights, acc,
    local_sem, send_sem, recv_sem,
):
    cand, rel = lax.axis_index("cand"), lax.axis_index("rel")
    n = lax.axis_size("cand")
    ahead, behind = (lax.rem(cand + 1, n), rel), (lax.rem(cand + n - 1, n), rel)
    greet([ahead, behind])
    part, width = entities.shape
    rows = packed.shape[2]
    chunk = part // 2
    block = 256

    fetch = [
        pltpu.make_async_copy(entities.at[pl.ds(h * chunk, chunk)], held.at[h], local_sem.at[h])
        for h in range(2)
    ]
    for copy in fetch:
        copy.start()
    acc[...] = jnp.zeros_like(acc)
    for copy in fetch:
        copy.wait()

    def copier(kind, source, landing):
        return lambda t: pltpu.make_async_remote_copy(
            src_ref=source.at[t],
            dst_ref=landing.at[t + 2],
            send_sem=send_sem.at[kind, t],
            recv_sem=recv_sem.at[kind, t],
            device_id=ahead,
            device_id_type=MESH,
        )

    core = lax.rem(cand, 2)
    hop, hop_short = copier(0, sent, held), copier(1, sent_short, held_short)

    def step(t, carry):
        half = lax.rem(t, 2)
        stop = t // 2
        here_rows = pl.ds(pl.multiple_of(half * chunk, chunk), chunk)

        @pl.when(t < 2)
        def _():
            now[...] = held[t]

        @pl.when((t >= 2) & (core == 1))
        def _():
            hop(t - 2).wait_recv()
            now[...] = held[t]

        @pl.when((t >= 2) & (core == 0))
        def _():
            hop_short(t - 2).wait_recv()
            now[...] = held_short[t].astype(F32)

        rounded = now[...].astype(BF)
        wide[here_rows, :] = rounded
        pieces = []
        for i in range(rows // block):
            here = pl.ds(i * block, block)
            logits = lax.dot_general(
                rounded, q[here, :], (((1,), (1,)), ((), ())), preferred_element_type=F32
            )
            marks = packed[stop, :, here]
            marks = jnp.concatenate(
                [lax.shift_right_logical(marks, 16 * half + 8 * p) for p in range(chunk // LOW)], axis=0
            )
            named = lax.bitwise_and(marks, 31).astype(F32)
            chance = 1.0 / (1.0 + jnp.exp2(logits * -LOG2E))
            product = named * chance
            pieces.append(jnp.where(lax.bitwise_and(marks, 32) != 0, product - 1.0, product).astype(BF))
        weight = jnp.concatenate(pieces, axis=1)
        weights[here_rows, :] = weight
        change = jnp.dot(weight, q[0:rows, :], preferred_element_type=F32)
        moved = now[...] - learn_rate * change
        sent[t] = moved
        sent_short[t] = moved.astype(BF)

        @pl.when((t < 2 * STOPS - 2) & (core == 0))
        def _():
            hop(t).start()

        @pl.when((t < 2 * STOPS - 2) & (core == 1))
        def _():
            hop_short(t).start()

        @pl.when(half == 1)
        def _():
            turned_wide[...] = wide[...].astype(F32).T.astype(BF)
            big = 512

            def gather(c, carry):
                here = pl.ds(pl.multiple_of(c * big, big), big)
                acc[:, here] += jnp.dot(turned_wide[...], weights[:, here], preferred_element_type=F32)
                return carry

            lax.fori_loop(0, rows // big, gather, 0, unroll=True)

        return carry

    lax.fori_loop(0, 2 * STOPS, step, 0)
    for h in range(2):
        state_out[pl.ds(h * chunk, chunk), :] = sent[2 * STOPS - 2 + h]

    def turned(c, carry):
        here = pl.ds(pl.multiple_of(c * block, block), block)
        grad_out[here, :] = acc[:, here].T.astype(BF)
        return carry

    lax.fori_loop(0, rows // block, turned, 0)
    grad_out[rows:, :] = jnp.zeros((grad_out.shape[0] - rows, width), BF)

    def drained(t, carry):
        @pl.when(core == 0)
        def _():
            hop(t).wait_send()

        @pl.when(core == 1)
        def _():
            hop_short(t).wait_send()

        return carry

    lax.fori_loop(0, 2 * STOPS - 2, drained, 0)


def run_stops(queries, packed, entities):
    padded, width = queries.shape
    rows = packed.shape[2]
    part = entities.shape[0]
    chunk = part // 2
    vmem = pl.BlockSpec(memory_space=pltpu.VMEM)
    hops = 2 * STOPS
    return pl.pallas_call(
        stops_kernel,
        out_shape=(
            jax.ShapeDtypeStruct((part, width), F32),
            jax.ShapeDtypeStruct((padded, width), BF),
        ),
        in_specs=[vmem, vmem, pl.BlockSpec(memory_space=pltpu.HBM)],
        out_specs=(vmem, vmem),
        scratch_shapes=[
            pltpu.VMEM((hops, chunk, width), F32),
            pltpu.VMEM((hops, chunk, width), F32),
            pltpu.VMEM((hops, chunk, width), BF),
            pltpu.VMEM((hops, chunk, width), BF),
            pltpu.VMEM((chunk, width), F32),
            pltpu.VMEM((part, width), BF),
            pltpu.VMEM((width, part), BF),
            pltpu.VMEM((part, rows), BF),
            pltpu.VMEM((width, rows), F32),
            pltpu.SemaphoreType.DMA((2,)),
            pltpu.SemaphoreType.DMA((2, hops)),
            pltpu.SemaphoreType.DMA((2, hops)),
        ],
        compiler_params=pltpu.CompilerParams(
            collective_id=2, has_side_effects=True, vmem_limit_bytes=28 << 20
        ),
        name="run_stops",
    )(queries, packed, entities)


def add_into(dst, *others):
    lead = dst.shape[:-2]
    total = 1
    for n in lead:
        total *= n

    def body(i, carry):
        index, rest = [], i
        for n in reversed(lead):
            index.insert(0, lax.rem(rest, n))
            rest = rest // n
        value = dst[tuple(index)].astype(F32)
        for other in others:
            value = value + other[tuple(index)].astype(F32)
        dst[tuple(index)] = value.astype(dst.dtype)
        return carry

    lax.fori_loop(0, total, body, 0)


class Ring:
    def __init__(self, mail, place, ahead, behind, piece, halves, land_half, land_full):
        self.mail, self.place, self.ahead, self.behind = mail, place, ahead, behind
        self.piece, self.halves, self.land_half, self.land_full = piece, halves, land_half, land_full

    def one(self):
        far = turn(self.place, 2)
        self.h = [
            self.mail.send(self.halves(self.piece(far))[d], self.land_half[d], device)
            for d, device in enumerate((self.ahead, self.behind))
        ]

    def two(self):
        self.f = []
        for d, (step, device) in enumerate(((1, self.ahead), (3, self.behind))):
            self.h[d].wait_recv()
            target = self.piece(turn(self.place, step))
            add_into(self.halves(target)[d], self.land_half[d])
            self.f.append(self.mail.send(target, self.land_full[d], device))

    def three(self):
        for copy in self.f:
            copy.wait_recv()
        return self.piece(self.place), self.land_full


def scatter_kernel(
    place, terms, back, out, source_grad, got,
    ax_h, ax_f, ay_h, ay_f, az_h, az_f, by_h, by_f, bx_h, bx_f, bz_h, bz_f, swap_send, swap_recv, send_sem, recv_sem
):
    at = Spot()
    mail = Mail(send_sem, recv_sem)
    partner = at.device(core=1 - at.core)
    xs = at.device(x=turn(at.x, 1)), at.device(x=turn(at.x, 3))
    ys = at.device(y=turn(at.y, 1)), at.device(y=turn(at.y, 3))
    zs = at.device(z=turn(at.z, 1)), at.device(z=turn(at.z, 3))
    greet([partner, *xs, *ys, *zs])

    def swap(j, r):
        zh, x = r // 4, lax.rem(r, 4)
        return pltpu.make_async_remote_copy(
            src_ref=terms.at[j, zh, x, :, :, 1 - at.core],
            dst_ref=got.at[j, zh, x],
            send_sem=swap_send.at[j, r],
            recv_sem=swap_recv.at[j, r],
            device_id=partner,
            device_id_type=MESH,
        )

    def offer(i, carry):
        swap(i // 8, lax.rem(i, 8)).start()
        return carry

    lax.fori_loop(0, 16, offer, 0)

    def joined(j):
        def one(r, carry):
            swap(j, r).wait_recv()
            zh, x = r // 4, lax.rem(r, 4)
            add_into(got.at[j, zh, x], terms.at[j, zh, x, :, :, at.core])
            return carry

        lax.fori_loop(0, 8, one, 0)

    def unsort(begin, end):
        lanes = 128
        total = place.shape[1]

        def one(b, carry):
            here = pl.ds(pl.multiple_of(b * lanes, lanes), lanes)
            mine = jnp.broadcast_to(place[:, here], (lanes, lanes)).T
            index = lax.broadcasted_iota(jnp.int32, (lanes, lanes), 1)
            choose = jnp.concatenate(
                [(mine == index + t * lanes).astype(F32).astype(BF) for t in range(total // lanes)], axis=1
            )
            source_grad[here, :] = jnp.dot(choose, back[0:total, :], preferred_element_type=F32).astype(BF)
            return carry

        lax.fori_loop(begin, end, one, 0)


    def first_half(ref):
        return ref.at[0], ref.at[1]

    def row_halves(ref):
        rows = ref.shape[0] // 2
        return ref.at[pl.ds(0, rows)], ref.at[pl.ds(rows, rows)]

    def two(ref):
        return ref.at[0], ref.at[1]

    a, b = got.at[0], got.at[1]
    ax = Ring(mail, at.x, *xs, lambda t: a.at[:, t], first_half, two(ax_h), two(ax_f))
    a1 = lambda: a.at[:, at.x]
    ay = Ring(mail, at.y, *ys, lambda t: a1().at[:, :, t], first_half, two(ay_h), two(ay_f))
    a2 = lambda z: a.at[z // 2, at.x, lax.rem(z, 2), at.y]
    az = Ring(mail, at.z, *zs, a2, row_halves, two(az_h), two(az_f))
    by = Ring(mail, at.y, *ys, lambda t: b.at[:, :, :, t], first_half, two(by_h), two(by_f))
    bx = Ring(mail, at.x, *xs, lambda t: b.at[:, t, :, at.y], first_half, two(bx_h), two(bx_f))
    b2 = lambda z: b.at[z // 2, at.x, lax.rem(z, 2), at.y]
    bz = Ring(mail, at.z, *zs, b2, row_halves, two(bz_h), two(bz_f))

    for j, ring in enumerate((ax, by)):
        joined(j)
        ring.one()
    unsort(0, 4)
    ax.two()
    by.two()
    unsort(4, 12)
    for ring, following in ((ax, ay), (by, bx)):
        piece, landed = ring.three()
        add_into(piece, *landed)
        following.one()
    unsort(12, 14)
    ay.two()
    bx.two()
    unsort(14, 16)
    for ring, following in ((ay, az), (bx, bz)):
        piece, landed = ring.three()
        add_into(piece, *landed)
        following.one()
    az.two()
    bz.two()
    for j, ring in enumerate((az, bz)):
        piece, landed = ring.three()
        out[:, j, :] = piece[...].astype(F32) + landed[0][...].astype(F32) + landed[1][...].astype(F32)

    def sent(i, carry):
        swap(i // 8, lax.rem(i, 8)).wait_send()
        return carry

    lax.fori_loop(0, 16, sent, 0)
    mail.drain()


def scatter_grads(place, terms, back):
    width = back.shape[1]
    total = place.shape[1]
    rows = width // 16
    terms = terms.reshape(2, 2, 4, 2, 4, 2, rows, width)
    v = lambda *lead: pltpu.VMEM((*lead, rows, width), BF)
    z = lambda r: pltpu.VMEM((2, r, width), BF)
    vmem = pl.BlockSpec(memory_space=pltpu.VMEM)
    return pl.pallas_call(
        scatter_kernel,
        out_shape=(jax.ShapeDtypeStruct((rows, 2, width), F32), jax.ShapeDtypeStruct((total, width), BF)),
        in_specs=[vmem, vmem, vmem],
        out_specs=(vmem, vmem),
        scratch_shapes=[
            v(2, 2, 4, 2, 4),
            v(2, 2, 4), v(2, 2, 2, 4), v(2, 2), v(2, 2, 2), z(rows // 2), v(2),
            v(2, 4, 2), v(2, 2, 4, 2), v(2, 2), v(2, 2, 2), z(rows // 2), v(2),
            pltpu.SemaphoreType.DMA((2, 8)),
            pltpu.SemaphoreType.DMA((2, 8)),
            pltpu.SemaphoreType.DMA((24,)),
            pltpu.SemaphoreType.DMA((24,)),
        ],
        compiler_params=pltpu.CompilerParams(
            collective_id=1, has_side_effects=True, vmem_limit_bytes=30 << 20
        ),
        name="scatter_grads",
    )(place, terms, back)


def shards(source_rows, rel_ids, relations, entities, pos_slot, negatives):
    rows = source_rows.shape[0]
    matrices, sorted_rows, packed, place, starts = gather_relations(
        relations,
        rel_ids.reshape(1, rows),
        source_rows,
        jnp.transpose(negatives, (0, 2, 1)),
        pos_slot.reshape(1, rows),
    )
    queries = make_queries(starts, sorted_rows, matrices)
    state, query_grad = run_stops(queries, packed, entities)
    back, terms = make_grads(starts, sorted_rows, query_grad, matrices)
    relation_grad, source_grad = scatter_grads(place, terms, back)
    return (state, source_grad, relation_grad)


def solution(mesh):
    placed = (
        P(("cand", "rel"), None),
        P(("cand", "rel"), None),
        P("rel", None, None),
        P(("cand", "rel"), None),
        P(("cand", "rel")),
        P(None, ("cand", "rel"), None),
    )
    return jax.shard_map(
        shards,
        mesh=mesh,
        in_specs=placed,
        out_specs=(P(("cand", "rel"), None), P(("cand", "rel"), None), P("cand", "rel", None)),
        check_vma=False,
    )
```

```python
import functools

import jax
import jax.numpy as jnp
from jax import lax
from jax.experimental import pallas as pl
from jax.experimental.pallas import tpu as pltpu
from jax.sharding import PartitionSpec as P

MESH = pl.DeviceIdType.MESH
BF = jnp.bfloat16
F32 = jnp.float32


class Spot:
    def __init__(self):
        cand, rel = lax.axis_index("cand"), lax.axis_index("rel")
        self.core = lax.rem(cand, 2)
        self.y = lax.rem(cand // 2, 4)
        self.zl = cand // 8
        self.x = lax.rem(rel, 4)
        self.zh = rel // 4
        self.z = self.zh * 2 + self.zl
        self.rel = rel

    def device(self, x=None, y=None, z=None, core=None):
        x = self.x if x is None else x
        y = self.y if y is None else y
        z = self.z if z is None else z
        core = self.core if core is None else core
        return ((lax.rem(z, 2) * 4 + y) * 2 + core, (z // 2) * 4 + x)


def turn(i, by):
    return lax.rem(i + by, 4)


def greet(devices):
    barrier = pltpu.get_barrier_semaphore()
    for device in devices:
        pl.semaphore_signal(barrier, inc=1, device_id=device, device_id_type=MESH)
    pl.semaphore_wait(barrier, len(devices))


class Mail:
    def __init__(self, send_sem, recv_sem):
        self.send_sem, self.recv_sem, self.count, self.sent = send_sem, recv_sem, 0, []

    def send(self, src, dst, device):
        i = self.count
        self.count += 1
        copy = pltpu.make_async_remote_copy(
            src_ref=src,
            dst_ref=dst,
            send_sem=self.send_sem.at[i],
            recv_sem=self.recv_sem.at[i],
            device_id=device,
            device_id_type=MESH,
        )
        copy.start()
        self.sent.append(copy)
        return copy

    def drain(self):
        for copy in self.sent:
            copy.wait_send()


WINDOW_PAD = 16


def sort_plan(ids, nrel):
    rows = ids.shape[1]
    block = 256
    named = (jnp.broadcast_to(ids, (nrel, rows)) == lax.broadcasted_iota(jnp.int32, (nrel, rows), 0)).astype(F32)
    before = (
        lax.broadcasted_iota(jnp.int32, (block, block), 0) < lax.broadcasted_iota(jnp.int32, (block, block), 1)
    ).astype(BF)
    running = jnp.zeros((nrel, 1), F32)
    ranks = []
    for b in range(rows // block):
        part = named[:, b * block : (b + 1) * block]
        ranks.append(jnp.dot(part.astype(BF), before, preferred_element_type=F32) + running)
        running = running + jnp.sum(part, axis=1, keepdims=True)
    rank = jnp.concatenate(ranks, axis=1)
    lower = (
        lax.broadcasted_iota(jnp.int32, (nrel, nrel), 1) < lax.broadcasted_iota(jnp.int32, (nrel, nrel), 0)
    ).astype(BF)
    starts = jnp.dot(lower, jnp.broadcast_to(running, (nrel, 128)).astype(BF), preferred_element_type=F32)
    place = jnp.sum(named * (rank + starts[:, 0:1]), axis=0, keepdims=True)
    return place, starts


def sort_rows(b, place, rows_ref, meta_ref, rows_out, picks_out, pos_out, part):
    rows = place.shape[1]
    block = 256
    here = pl.ds(b * block, block)
    spot = lax.broadcasted_iota(jnp.int32, (block, rows), 0) + b * block
    choose = (jnp.broadcast_to(place, (block, rows)) == spot).astype(F32).astype(BF)
    rows_out[here, :] = jnp.dot(choose, rows_ref[...], preferred_element_type=F32).astype(BF)
    meta = lax.dot_general(
        meta_ref[...], choose, (((1,), (1,)), ((), ())), preferred_element_type=F32
    ).astype(jnp.int32)
    named = picks_out.shape[0]
    picks_out[:, here] = meta[0:named]
    pos_out[:, here] = meta[named : named + 1] * part + meta[named + 1 : named + 2]


def group_queries(starts, rows_ref, matrix, out):
    k = pl.program_id(0)
    window = out_window(starts, k)
    rows = rows_ref[window[0], :]
    new = jnp.dot(rows, matrix[0], preferred_element_type=F32).astype(BF)
    out[window[0], :] = jnp.where(window[1], new, out[window[0], :])


def out_window(starts, k):
    size = 256 + WINDOW_PAD
    start, end = starts[k], starts[k + 1]
    base = pl.multiple_of(start // WINDOW_PAD * WINDOW_PAD, WINDOW_PAD)
    row = lax.broadcasted_iota(jnp.int32, (size, 512), 0) + base
    return pl.ds(base, size), (row >= start) & (row < end)


def make_queries(starts, rows, matrices):
    nrel, width, _ = matrices.shape
    return pl.pallas_call(
        group_queries,
        out_shape=jax.ShapeDtypeStruct(rows.shape, BF),
        grid_spec=pltpu.PrefetchScalarGridSpec(
            num_scalar_prefetch=1,
            grid=(nrel,),
            in_specs=[
                pl.BlockSpec(rows.shape, lambda k, s: (0, 0)),
                pl.BlockSpec((1, width, width), lambda k, s: (k, 0, 0)),
            ],
            out_specs=pl.BlockSpec(rows.shape, lambda k, s: (0, 0)),
        ),
        compiler_params=pltpu.CompilerParams(vmem_limit_bytes=20 << 20),
        name="make_queries",
    )(starts, rows, matrices)


def group_grads(starts, rows_ref, grads, matrix, back, terms):
    window, inside = out_window(starts, pl.program_id(0))
    grad = grads[window, :]
    new = lax.dot_general(grad, matrix[0], (((1,), (1,)), ((), ())), preferred_element_type=F32).astype(BF)
    back[window, :] = jnp.where(inside, new, back[window, :])
    rows = rows_ref[window, :]
    rows = jnp.where(inside, rows, jnp.zeros_like(rows))
    terms[0, 0] = lax.dot_general(rows, grad, (((0,), (0,)), ((), ())), preferred_element_type=F32).astype(BF)


def make_grads(starts, rows, grads, matrices):
    nrel, width, _ = matrices.shape
    whole = pl.BlockSpec(grads.shape, lambda k, s: (0, 0))
    return pl.pallas_call(
        group_grads,
        out_shape=(
            jax.ShapeDtypeStruct(grads.shape, BF),
            jax.ShapeDtypeStruct((2, nrel // 2, width, width), BF),
        ),
        grid_spec=pltpu.PrefetchScalarGridSpec(
            num_scalar_prefetch=1,
            grid=(nrel,),
            in_specs=[whole, whole, pl.BlockSpec((1, width, width), lambda k, s: (k, 0, 0))],
            out_specs=(
                whole,
                pl.BlockSpec((1, 1, width, width), lambda k, s: (lax.rem(k, 2), k // 2, 0, 0)),
            ),
        ),
        compiler_params=pltpu.CompilerParams(vmem_limit_bytes=20 << 20),
        name="make_grads",
    )(starts, rows, grads, matrices)


LOW = 64


def tally(stop, part, picks, pos, low, unit, packed):
    samples = 16
    rows = pos.shape[1]
    lanes = 128
    names = picks[pl.ds(pl.multiple_of(stop * samples, samples), samples), :]
    low[0:samples, :] = lax.bitwise_and(names, LOW - 1)
    unit[0:samples, :] = lax.shift_left(jnp.ones_like(names), 8 * lax.shift_right_logical(names, 6))
    place = pos[...] - stop * part
    inside = (place >= 0) & (place < part)
    place = jnp.where(inside, place, 0)
    low[samples : samples + 1, :] = lax.bitwise_and(place, LOW - 1)
    unit[samples : samples + 1, :] = jnp.where(
        inside, lax.shift_left(jnp.full_like(place, 33), 8 * lax.shift_right_logical(place, 6)), 0
    )

    def column(c, carry):
        here = pl.ds(pl.multiple_of(c * lanes, lanes), lanes)
        index = lax.broadcasted_iota(jnp.int32, (LOW, lanes), 0)
        total = jnp.zeros((LOW, lanes), jnp.int32)
        for k in range(samples + 1):
            match = jnp.broadcast_to(low[k : k + 1, here], (LOW, lanes)) == index
            total = total + jnp.where(match, jnp.broadcast_to(unit[k : k + 1, here], (LOW, lanes)), 0)
        packed[stop, :, here] = total
        return carry

    lax.fori_loop(0, rows // lanes, column, 0)


def gather_kernel(
    own_in, ids_in, rows_in, picks_in, target_in, out, rows_out, packed, place_out, starts_out,
    own, ids, rows_ref, picks, target,
    meta, sorted_picks, sorted_target, low, unit, local_sem, fetch_sem, send_sem, recv_sem,
):
    at = Spot()
    mail = Mail(send_sem, recv_sem)
    left, right = at.device(x=turn(at.x, 3)), at.device(x=turn(at.x, 1))
    down, up = at.device(y=turn(at.y, 3)), at.device(y=turn(at.y, 1))
    across = at.device(z=3 - at.z)
    partner = at.device(core=1 - at.core)
    fetch = [
        pltpu.make_async_copy(source, landing, fetch_sem.at[i])
        for i, (source, landing) in enumerate(
            ((own_in, own), (ids_in, ids), (target_in, target), (picks_in, picks), (rows_in, rows_ref))
        )
    ]
    for copy in fetch:
        copy.start()
    greet([left, right, down, up, across, partner])
    fetch[0].wait()
    half = own.shape[1] // 2
    share = half // 4

    def rows(start, size, step):
        return pl.ds(pl.multiple_of(start, step), size)

    start = at.core * half
    mine, first, second = rows(start, half, half), rows(start, half // 2, half), rows(start + half // 2, half // 2, half // 2)

    def quarter(y):
        return rows(start + y * share, share, share)

    def quarter_halves(y):
        return (
            rows(start + y * share, share // 2, share),
            rows(start + y * share + share // 2, share // 2, share // 2),
        )

    me, far = at.zh * 4, (1 - at.zh) * 4
    x0, x1, x2, x3 = at.x, turn(at.x, 1), turn(at.x, 2), turn(at.x, 3)
    y0, y1, y2, y3 = at.y, turn(at.y, 1), turn(at.y, 2), turn(at.y, 3)
    here = pltpu.make_async_copy(own, out.at[at.rel], local_sem)
    here.start()

    def same(ref, device):
        return mail.send(ref, ref, device)

    def a(base, x, rows):
        return out.at[base + x, 0, rows]

    def b(base, x, rows):
        return out.at[base + x, 1, rows]

    gifts = []

    class Quarter:
        def __init__(self, base, x):
            self.base, self.x = base, x
            self.sent = [same(b(base, x, quarter(y0)), device) for device in (up, down)]

        def on(self):
            self.sent[0].wait_recv()
            first = same(b(self.base, self.x, quarter_halves(y3)[0]), up)
            self.sent[1].wait_recv()
            self.sent = [first, same(b(self.base, self.x, quarter_halves(y1)[1]), down)]

        def done(self):
            for copy in self.sent:
                copy.wait_recv()
            gifts.append(same(b(self.base, self.x, mine), partner))

    own_a, own_b = own.at[0, mine], own.at[1, quarter(y0)]
    b_across = mail.send(own_b, b(me, x0, quarter(y0)), across)
    b_right = mail.send(own_b, b(me, x0, quarter(y0)), right)
    b_left = mail.send(own_b, b(me, x0, quarter(y0)), left)
    a_across = mail.send(own_a, a(me, x0, mine), across)
    a_right = mail.send(own_a, a(me, x0, mine), right)
    a_left = mail.send(own_a, a(me, x0, mine), left)

    stops, samples, total = picks.shape
    part = total // stops
    nrel = starts_out.shape[0]
    for copy in fetch[1:]:
        copy.wait()
    place, starts = sort_plan(ids[...], nrel)
    place = place.astype(jnp.int32)
    place_out[...] = place
    starts_out[...] = starts.astype(jnp.int32)
    for s in range(stops):
        meta[s * samples : (s + 1) * samples, :] = picks[s].astype(F32).astype(BF)
    goal = target[...]
    tail = lax.broadcasted_iota(jnp.int32, (16, total), 0)
    meta[stops * samples :, :] = jnp.where(
        tail == 0, jnp.broadcast_to(goal // part, (16, total)), jnp.broadcast_to(lax.rem(goal, part), (16, total))
    ).astype(F32).astype(BF)
    rows_out[total:, :] = jnp.zeros((rows_out.shape[0] - total, rows_out.shape[1]), BF)

    def work(b):
        sort_rows(b, place_out[...], rows_ref, meta, rows_out, sorted_picks, sorted_target, part)

    def count(s):
        tally(s, part, sorted_picks, sorted_target, low, unit, packed)

    h0, h1 = quarter_halves(y0)
    work(0)
    b_right.wait_recv()
    b_on_right = same(b(me, x3, h0), right)
    q_me3 = Quarter(me, x3)
    b_left.wait_recv()
    b_on_left = same(b(me, x1, h1), left)
    q_me1 = Quarter(me, x1)
    b_across.wait_recv()
    b_far_right = same(b(far, x0, quarter(y0)), right)
    b_far_left = same(b(far, x0, quarter(y0)), left)
    q_far0 = Quarter(far, x0)
    work(1)
    a_right.wait_recv()
    a_on_right = same(a(me, x3, first), right)
    gifts.append(same(a(me, x3, mine), partner))
    a_left.wait_recv()
    a_on_left = same(a(me, x1, second), left)
    gifts.append(same(a(me, x1, mine), partner))
    b_on_right.wait_recv()
    b_on_left.wait_recv()
    q_me2 = Quarter(me, x2)
    work(2)
    b_far_right.wait_recv()
    b_far_on_right = same(b(far, x3, h0), right)
    q_far3 = Quarter(far, x3)
    b_far_left.wait_recv()
    b_far_on_left = same(b(far, x1, h1), left)
    q_far1 = Quarter(far, x1)
    a_across.wait_recv()
    a_far_right = same(a(far, x0, mine), right)
    a_far_left = same(a(far, x0, mine), left)
    gifts.append(same(a(far, x0, mine), partner))
    work(3)
    q_me3.on()
    q_me1.on()
    work(4)
    q_far0.on()
    a_on_right.wait_recv()
    a_opposite = [same(a(me, x2, first), across)]
    a_on_left.wait_recv()
    a_opposite.append(same(a(me, x2, second), across))
    gifts.append(same(a(me, x2, mine), partner))
    b_far_on_right.wait_recv()
    b_far_on_left.wait_recv()
    q_far2 = Quarter(far, x2)
    work(5)
    q_me2.on()
    q_me3.done()
    work(6)
    q_far3.on()
    q_me1.done()
    work(7)
    q_far1.on()
    q_far0.done()
    count(0)
    q_far2.on()
    q_me2.done()
    count(1)
    a_far_right.wait_recv()
    gifts.append(same(a(far, x3, mine), partner))
    a_far_left.wait_recv()
    gifts.append(same(a(far, x1, mine), partner))
    q_far3.done()
    count(2)
    for copy in a_opposite:
        copy.wait_recv()
    gifts.append(same(a(far, x2, mine), partner))
    q_far1.done()
    q_far2.done()
    count(3)
    count(4)

    def later(s, carry):
        count(s)
        return carry

    lax.fori_loop(5, stops, later, 0)
    for copy in gifts:
        copy.wait_recv()
    mail.drain()
    here.wait()


def gather_relations(relations, ids, rows, picks, target):
    per, width, _ = relations.shape
    owners = lax.axis_size("rel")
    nrel = owners * per
    stops, samples, total = picks.shape
    vmem = pl.BlockSpec(memory_space=pltpu.VMEM)
    out = pl.pallas_call(
        gather_kernel,
        out_shape=(
            jax.ShapeDtypeStruct((owners, per, width, width), relations.dtype),
            jax.ShapeDtypeStruct((total + 256 + WINDOW_PAD, width), BF),
            jax.ShapeDtypeStruct((stops, LOW, total), jnp.int32),
            jax.ShapeDtypeStruct((1, total), jnp.int32),
            jax.ShapeDtypeStruct((nrel, 128), jnp.int32),
        ),
        in_specs=[pl.BlockSpec(memory_space=pltpu.HBM)] * 5,
        out_specs=(pl.BlockSpec(memory_space=pl.ANY), *[vmem] * 4),
        scratch_shapes=[
            *(pltpu.VMEM(a.shape, a.dtype) for a in (relations, ids, rows, picks, target)),
            pltpu.VMEM((stops * samples + 16, total), BF),
            pltpu.VMEM((stops * samples, total), jnp.int32),
            pltpu.VMEM((1, total), jnp.int32),
            pltpu.VMEM((24, total), jnp.int32),
            pltpu.VMEM((24, total), jnp.int32),
            pltpu.SemaphoreType.DMA,
            pltpu.SemaphoreType.DMA((5,)),
            pltpu.SemaphoreType.DMA((60,)),
            pltpu.SemaphoreType.DMA((60,)),
        ],
        compiler_params=pltpu.CompilerParams(
            collective_id=0, has_side_effects=True, vmem_limit_bytes=24 << 20
        ),
        name="gather_relations",
    )(relations, ids, rows, picks, target)
    matrices, rows, packed, place, starts = out
    starts = jnp.concatenate([starts[:, 0], jnp.full((1,), total, jnp.int32)])
    return matrices.reshape(nrel, width, width), rows, packed, place, starts


STOPS = 8
learn_rate = 0.005
LOG2E = 1.4426950408889634


def stops_kernel(
    q, packed, entities, state_out, grad_out, held, sent, held_short, sent_short, now, wide, turned_wide, weights, acc,
    local_sem, send_sem, recv_sem,
):
    cand, rel = lax.axis_index("cand"), lax.axis_index("rel")
    n = lax.axis_size("cand")
    ahead, behind = (lax.rem(cand + 1, n), rel), (lax.rem(cand + n - 1, n), rel)
    greet([ahead, behind])
    part, width = entities.shape
    rows = packed.shape[2]
    chunk = part // 2
    block = 256

    fetch = [
        pltpu.make_async_copy(entities.at[pl.ds(h * chunk, chunk)], held.at[h], local_sem.at[h])
        for h in range(2)
    ]
    for copy in fetch:
        copy.start()
    acc[...] = jnp.zeros_like(acc)
    for copy in fetch:
        copy.wait()

    def copier(kind, source, landing):
        return lambda t: pltpu.make_async_remote_copy(
            src_ref=source.at[t],
            dst_ref=landing.at[t + 2],
            send_sem=send_sem.at[kind, t],
            recv_sem=recv_sem.at[kind, t],
            device_id=ahead,
            device_id_type=MESH,
        )

    core = lax.rem(cand, 2)
    hop, hop_short = copier(0, sent, held), copier(1, sent_short, held_short)

    def step(t, carry):
        half = lax.rem(t, 2)
        stop = t // 2
        here_rows = pl.ds(pl.multiple_of(half * chunk, chunk), chunk)

        @pl.when(t < 2)
        def _():
            now[...] = held[t]

        @pl.when((t >= 2) & (core == 1))
        def _():
            hop(t - 2).wait_recv()
            now[...] = held[t]

        @pl.when((t >= 2) & (core == 0))
        def _():
            hop_short(t - 2).wait_recv()
            now[...] = held_short[t].astype(F32)

        rounded = now[...].astype(BF)
        wide[here_rows, :] = rounded
        pieces = []
        for i in range(rows // block):
            here = pl.ds(i * block, block)
            logits = lax.dot_general(
                rounded, q[here, :], (((1,), (1,)), ((), ())), preferred_element_type=F32
            )
            marks = packed[stop, :, here]
            marks = jnp.concatenate(
                [lax.shift_right_logical(marks, 16 * half + 8 * p) for p in range(chunk // LOW)], axis=0
            )
            named = lax.bitwise_and(marks, 31).astype(F32)
            chance = 1.0 / (1.0 + jnp.exp2(logits * -LOG2E))
            product = named * chance
            pieces.append(jnp.where(lax.bitwise_and(marks, 32) != 0, product - 1.0, product).astype(BF))
        weight = jnp.concatenate(pieces, axis=1)
        weights[here_rows, :] = weight
        change = jnp.dot(weight, q[0:rows, :], preferred_element_type=F32)
        moved = now[...] - learn_rate * change
        sent[t] = moved
        sent_short[t] = moved.astype(BF)

        @pl.when((t < 2 * STOPS - 2) & (core == 0))
        def _():
            hop(t).start()

        @pl.when((t < 2 * STOPS - 2) & (core == 1))
        def _():
            hop_short(t).start()

        @pl.when(half == 1)
        def _():
            turned_wide[...] = wide[...].astype(F32).T.astype(BF)
            big = 512

            def gather(c, carry):
                here = pl.ds(pl.multiple_of(c * big, big), big)
                acc[:, here] += jnp.dot(turned_wide[...], weights[:, here], preferred_element_type=F32)
                return carry

            lax.fori_loop(0, rows // big, gather, 0, unroll=True)

        return carry

    lax.fori_loop(0, 2 * STOPS, step, 0)
    for h in range(2):
        state_out[pl.ds(h * chunk, chunk), :] = sent[2 * STOPS - 2 + h]

    def turned(c, carry):
        here = pl.ds(pl.multiple_of(c * block, block), block)
        grad_out[here, :] = acc[:, here].T.astype(BF)
        return carry

    lax.fori_loop(0, rows // block, turned, 0)
    grad_out[rows:, :] = jnp.zeros((grad_out.shape[0] - rows, width), BF)

    def drained(t, carry):
        @pl.when(core == 0)
        def _():
            hop(t).wait_send()

        @pl.when(core == 1)
        def _():
            hop_short(t).wait_send()

        return carry

    lax.fori_loop(0, 2 * STOPS - 2, drained, 0)


def run_stops(queries, packed, entities):
    padded, width = queries.shape
    rows = packed.shape[2]
    part = entities.shape[0]
    chunk = part // 2
    vmem = pl.BlockSpec(memory_space=pltpu.VMEM)
    hops = 2 * STOPS
    return pl.pallas_call(
        stops_kernel,
        out_shape=(
            jax.ShapeDtypeStruct((part, width), F32),
            jax.ShapeDtypeStruct((padded, width), BF),
        ),
        in_specs=[vmem, vmem, pl.BlockSpec(memory_space=pltpu.HBM)],
        out_specs=(vmem, vmem),
        scratch_shapes=[
            pltpu.VMEM((hops, chunk, width), F32),
            pltpu.VMEM((hops, chunk, width), F32),
            pltpu.VMEM((hops, chunk, width), BF),
            pltpu.VMEM((hops, chunk, width), BF),
            pltpu.VMEM((chunk, width), F32),
            pltpu.VMEM((part, width), BF),
            pltpu.VMEM((width, part), BF),
            pltpu.VMEM((part, rows), BF),
            pltpu.VMEM((width, rows), F32),
            pltpu.SemaphoreType.DMA((2,)),
            pltpu.SemaphoreType.DMA((2, hops)),
            pltpu.SemaphoreType.DMA((2, hops)),
        ],
        compiler_params=pltpu.CompilerParams(
            collective_id=2, has_side_effects=True, vmem_limit_bytes=28 << 20
        ),
        name="run_stops",
    )(queries, packed, entities)


def add_into(dst, *others):
    lead, size = [], dst.size
    for n in dst.shape[:-2]:
        if size <= 1 << 15:
            break
        lead.append(n)
        size //= n
    total = 1
    for n in lead:
        total *= n

    def body(i, carry):
        index, rest = [], i
        for n in reversed(lead):
            index.insert(0, lax.rem(rest, n))
            rest = rest // n
        index = tuple(index) if index else ...
        value = dst[index].astype(F32)
        for other in others:
            value = value + other[index].astype(F32)
        dst[index] = value.astype(dst.dtype)
        return carry

    if total == 1:
        body(0, 0)
    else:
        lax.fori_loop(0, total, body, 0)


ORDERS = (("xyz", "yxz", "zxy", "xyz"), ("yxz", "xyz", "zyx", "yxz"))
SIZES = {"zh": 2, "x": 4, "zl": 2, "y": 4}
OF_AXIS = {"x": ("x",), "y": ("y",), "z": ("zh", "zl")}


def piece_shape(order, phase, rows, columns):
    gone = [name for axis in order[: phase + 1] for name in OF_AXIS[axis]]
    free = [n for name, n in SIZES.items() if name not in gone]
    if free:
        return (free[0] // 2, *free[1:], rows, columns), (*free, rows, columns)
    return (rows, columns // 2), (rows, columns)


def landing_shapes(order, rows, columns):
    shapes = []
    for phase in range(3):
        half, whole = piece_shape(order, phase, rows, columns)
        shapes += [(2, *half), (2, *whole)]
    return shapes


class Eighth:
    def __init__(self, mail, at, base, row, column, order, landings, ways):
        self.mail, self.at, self.base, self.order, self.landings, self.ways = mail, at, base, order, landings, ways
        self.row, self.column = row, column
        self.fixed, self.phase = {}, 0

    def view(self, fixed, cut=None):
        index = []
        free = [name for name in SIZES if name not in fixed]
        for name, n in SIZES.items():
            if name in fixed:
                index.append(fixed[name])
            elif cut is not None and name == free[0]:
                index.append(pl.ds(cut * (n // 2), n // 2))
            else:
                index.append(slice(None))
        start, size = self.column
        if cut is not None and not free:
            start, size = start + cut * (size // 2), size // 2
        return self.base.at[(*index, pl.ds(*self.row), pl.ds(start, size))]

    def spot(self, by):
        axis = self.order[self.phase]
        t = turn(getattr(self.at, axis), by)
        return {**self.fixed, **({"zh": t // 2, "zl": lax.rem(t, 2)} if axis == "z" else {axis: t})}

    def one(self):
        self.half, self.whole = self.landings[2 * self.phase : 2 * self.phase + 2]
        self.devices = self.ways[self.order[self.phase]]
        self.h = [
            self.mail.send(self.view(self.spot(2), d), self.half.at[d], device)
            for d, device in enumerate(self.devices)
        ]

    def two(self):
        self.f = []
        for d, device in enumerate(self.devices):
            self.h[d].wait_recv()
            target = self.spot((1, 3)[d])
            add_into(self.view(target, d), self.half.at[d])
            self.f.append(self.mail.send(self.view(target), self.whole.at[d], device))

    def three(self):
        for copy in self.f:
            copy.wait_recv()
        self.fixed = self.spot(0)
        self.phase += 1
        if self.phase < 3:
            add_into(self.view(self.fixed), self.whole.at[0], self.whole.at[1])
            self.one()

    def result(self):
        own = self.view(self.fixed)[...].astype(F32)
        return own + self.whole[0].astype(F32) + self.whole[1].astype(F32)


def scatter_kernel(place, terms, back, out, source_grad, got, *rest):
    swap_send, swap_recv, send_sem, recv_sem = rest[-4:]
    landings = rest[:-4]
    at = Spot()
    mail = Mail(send_sem, recv_sem)
    partner = at.device(core=1 - at.core)
    ways = {
        "x": (at.device(x=turn(at.x, 1)), at.device(x=turn(at.x, 3))),
        "y": (at.device(y=turn(at.y, 1)), at.device(y=turn(at.y, 3))),
        "z": (at.device(z=turn(at.z, 1)), at.device(z=turn(at.z, 3))),
    }
    greet([partner, *ways["x"], *ways["y"], *ways["z"]])

    def swap(j, r):
        zh, x = r // 4, lax.rem(r, 4)
        return pltpu.make_async_remote_copy(
            src_ref=terms.at[j, zh, x, :, :, 1 - at.core],
            dst_ref=got.at[j, zh, x],
            send_sem=swap_send.at[j, r],
            recv_sem=swap_recv.at[j, r],
            device_id=partner,
            device_id_type=MESH,
        )

    def offer(i, carry):
        swap(i // 8, lax.rem(i, 8)).start()
        return carry

    lax.fori_loop(0, 16, offer, 0)

    def joined(j):
        def one(r, carry):
            swap(j, r).wait_recv()
            zh, x = r // 4, lax.rem(r, 4)
            add_into(got.at[j, zh, x], terms.at[j, zh, x, :, :, at.core])
            return carry

        lax.fori_loop(0, 8, one, 0)

    def unsort(begin, end):
        lanes = 128
        total = place.shape[1]

        def one(b, carry):
            here = pl.ds(pl.multiple_of(b * lanes, lanes), lanes)
            mine = jnp.broadcast_to(place[:, here], (lanes, lanes)).T
            index = lax.broadcasted_iota(jnp.int32, (lanes, lanes), 1)
            choose = jnp.concatenate(
                [(mine == index + t * lanes).astype(F32).astype(BF) for t in range(total // lanes)], axis=1
            )
            source_grad[here, :] = jnp.dot(choose, back[0:total, :], preferred_element_type=F32).astype(BF)
            return carry

        lax.fori_loop(begin, end, one, 0)


    rows, columns = got.shape[-2] // 2, got.shape[-1] // 2
    units = [
        [
            Eighth(
                mail, at, got.at[j], (u // 2 * rows, rows), (u % 2 * columns, columns), ORDERS[j][u],
                landings[(4 * j + u) * 6 : (4 * j + u) * 6 + 6], ways,
            )
            for u in range(4)
        ]
        for j in range(2)
    ]
    every = [unit for group in units for unit in group]
    for j in range(2):
        joined(j)
        for unit in units[j]:
            unit.one()
    unsort(0, 3)
    for phase in range(3):
        for unit in every:
            unit.two()
        unsort(3 + 4 * phase, 5 + 4 * phase)
        for unit in every:
            unit.three()
        unsort(5 + 4 * phase, 7 + 4 * phase)
    unsort(15, 16)
    for j in range(2):
        for u, unit in enumerate(units[j]):
            out[unit.row[0] : unit.row[0] + rows, j, unit.column[0] : unit.column[0] + columns] = unit.result()

    def sent(i, carry):
        swap(i // 8, lax.rem(i, 8)).wait_send()
        return carry

    lax.fori_loop(0, 16, sent, 0)
    mail.drain()


def scatter_grads(place, terms, back):
    width = back.shape[1]
    total = place.shape[1]
    rows = width // 16
    terms = terms.reshape(2, 2, 4, 2, 4, 2, rows, width)
    v = lambda *lead: pltpu.VMEM((*lead, rows, width), BF)
    vmem = pl.BlockSpec(memory_space=pltpu.VMEM)
    return pl.pallas_call(
        scatter_kernel,
        out_shape=(jax.ShapeDtypeStruct((rows, 2, width), F32), jax.ShapeDtypeStruct((total, width), BF)),
        in_specs=[vmem, vmem, vmem],
        out_specs=(vmem, vmem),
        scratch_shapes=[
            v(2, 2, 4, 2, 4),
            *(
                pltpu.VMEM(shape, BF)
                for group in ORDERS
                for order in group
                for shape in landing_shapes(order, rows // 2, width // 2)
            ),
            pltpu.SemaphoreType.DMA((2, 8)),
            pltpu.SemaphoreType.DMA((2, 8)),
            pltpu.SemaphoreType.DMA((96,)),
            pltpu.SemaphoreType.DMA((96,)),
        ],
        compiler_params=pltpu.CompilerParams(
            collective_id=1, has_side_effects=True, vmem_limit_bytes=30 << 20
        ),
        name="scatter_grads",
    )(place, terms, back)


def shards(source_rows, rel_ids, relations, entities, pos_slot, negatives):
    rows = source_rows.shape[0]
    matrices, sorted_rows, packed, place, starts = gather_relations(
        relations,
        rel_ids.reshape(1, rows),
        source_rows,
        jnp.transpose(negatives, (0, 2, 1)),
        pos_slot.reshape(1, rows),
    )
    queries = make_queries(starts, sorted_rows, matrices)
    state, query_grad = run_stops(queries, packed, entities)
    back, terms = make_grads(starts, sorted_rows, query_grad, matrices)
    relation_grad, source_grad = scatter_grads(place, terms, back)
    return (state, source_grad, relation_grad)


def solution(mesh):
    placed = (
        P(("cand", "rel"), None),
        P(("cand", "rel"), None),
        P("rel", None, None),
        P(("cand", "rel"), None),
        P(("cand", "rel")),
        P(None, ("cand", "rel"), None),
    )
    return jax.shard_map(
        shards,
        mesh=mesh,
        in_specs=placed,
        out_specs=(P(("cand", "rel"), None), P(("cand", "rel"), None), P("cand", "rel", None)),
        check_vma=False,
    )
```

```python
import functools

import jax
import jax.numpy as jnp
from jax import lax
from jax.experimental import pallas as pl
from jax.experimental.pallas import tpu as pltpu
from jax.sharding import PartitionSpec as P

MESH = pl.DeviceIdType.MESH
BF = jnp.bfloat16
F32 = jnp.float32


class Spot:
    def __init__(self):
        cand, rel = lax.axis_index("cand"), lax.axis_index("rel")
        self.core = lax.rem(cand, 2)
        self.y = lax.rem(cand // 2, 4)
        self.zl = cand // 8
        self.x = lax.rem(rel, 4)
        self.zh = rel // 4
        self.z = self.zh * 2 + self.zl
        self.rel = rel

    def device(self, x=None, y=None, z=None, core=None):
        x = self.x if x is None else x
        y = self.y if y is None else y
        z = self.z if z is None else z
        core = self.core if core is None else core
        return ((lax.rem(z, 2) * 4 + y) * 2 + core, (z // 2) * 4 + x)


def turn(i, by):
    return lax.rem(i + by, 4)


def greet(devices):
    barrier = pltpu.get_barrier_semaphore()
    for device in devices:
        pl.semaphore_signal(barrier, inc=1, device_id=device, device_id_type=MESH)
    pl.semaphore_wait(barrier, len(devices))


class Mail:
    def __init__(self, send_sem, recv_sem):
        self.send_sem, self.recv_sem, self.count, self.sent = send_sem, recv_sem, 0, []

    def send(self, src, dst, device):
        i = self.count
        self.count += 1
        copy = pltpu.make_async_remote_copy(
            src_ref=src,
            dst_ref=dst,
            send_sem=self.send_sem.at[i],
            recv_sem=self.recv_sem.at[i],
            device_id=device,
            device_id_type=MESH,
        )
        copy.start()
        self.sent.append(copy)
        return copy

    def drain(self):
        for copy in self.sent:
            copy.wait_send()


WINDOW_PAD = 16


def sort_plan(ids, nrel):
    rows = ids.shape[1]
    block = 256
    named = (jnp.broadcast_to(ids, (nrel, rows)) == lax.broadcasted_iota(jnp.int32, (nrel, rows), 0)).astype(F32)
    before = (
        lax.broadcasted_iota(jnp.int32, (block, block), 0) < lax.broadcasted_iota(jnp.int32, (block, block), 1)
    ).astype(BF)
    running = jnp.zeros((nrel, 1), F32)
    ranks = []
    for b in range(rows // block):
        part = named[:, b * block : (b + 1) * block]
        ranks.append(jnp.dot(part.astype(BF), before, preferred_element_type=F32) + running)
        running = running + jnp.sum(part, axis=1, keepdims=True)
    rank = jnp.concatenate(ranks, axis=1)
    lower = (
        lax.broadcasted_iota(jnp.int32, (nrel, nrel), 1) < lax.broadcasted_iota(jnp.int32, (nrel, nrel), 0)
    ).astype(BF)
    starts = jnp.dot(lower, jnp.broadcast_to(running, (nrel, 128)).astype(BF), preferred_element_type=F32)
    place = jnp.sum(named * (rank + starts[:, 0:1]), axis=0, keepdims=True)
    return place, starts


def sort_rows(b, place, rows_ref, meta_ref, rows_out, picks_out, pos_out, part):
    rows = place.shape[1]
    block = 256
    here = pl.ds(b * block, block)
    spot = lax.broadcasted_iota(jnp.int32, (block, rows), 0) + b * block
    choose = (jnp.broadcast_to(place, (block, rows)) == spot).astype(F32).astype(BF)
    rows_out[here, :] = jnp.dot(choose, rows_ref[...], preferred_element_type=F32).astype(BF)
    meta = lax.dot_general(
        meta_ref[...], choose, (((1,), (1,)), ((), ())), preferred_element_type=F32
    ).astype(jnp.int32)
    named = picks_out.shape[0]
    picks_out[:, here] = meta[0:named]
    pos_out[:, here] = meta[named : named + 1] * part + meta[named + 1 : named + 2]


TOGETHER = 4


def group_queries(starts, rows_ref, matrix, out):
    for r in range(TOGETHER):
        window, inside = out_window(starts, TOGETHER * pl.program_id(0) + r)
        new = jnp.dot(rows_ref[window, :], matrix[r], preferred_element_type=F32).astype(BF)
        out[window, :] = jnp.where(inside, new, out[window, :])


def out_window(starts, k):
    size = 256 + WINDOW_PAD
    start, end = starts[k], starts[k + 1]
    base = pl.multiple_of(start // WINDOW_PAD * WINDOW_PAD, WINDOW_PAD)
    row = lax.broadcasted_iota(jnp.int32, (size, 512), 0) + base
    return pl.ds(base, size), (row >= start) & (row < end)


def make_queries(starts, rows, matrices):
    nrel, width, _ = matrices.shape
    return pl.pallas_call(
        group_queries,
        out_shape=jax.ShapeDtypeStruct(rows.shape, BF),
        grid_spec=pltpu.PrefetchScalarGridSpec(
            num_scalar_prefetch=1,
            grid=(nrel // TOGETHER,),
            in_specs=[
                pl.BlockSpec(rows.shape, lambda k, s: (0, 0)),
                pl.BlockSpec((TOGETHER, width, width), lambda k, s: (k, 0, 0)),
            ],
            out_specs=pl.BlockSpec(rows.shape, lambda k, s: (0, 0)),
        ),
        compiler_params=pltpu.CompilerParams(vmem_limit_bytes=16 << 20),
        name="make_queries",
    )(starts, rows, matrices)


def group_grads(starts, rows_ref, grads, matrix, state, back, terms, state_out, sem):
    step = pl.program_id(0)
    keep = pltpu.make_async_copy(state, state_out, sem)

    @pl.when(step == 0)
    def _():
        keep.start()

    window, inside = out_window(starts, step)
    grad = grads[window, :]
    new = lax.dot_general(grad, matrix[0], (((1,), (1,)), ((), ())), preferred_element_type=F32).astype(BF)
    back[window, :] = jnp.where(inside, new, back[window, :])
    rows = rows_ref[window, :]
    rows = jnp.where(inside, rows, jnp.zeros_like(rows))
    terms[0, 0] = lax.dot_general(rows, grad, (((0,), (0,)), ((), ())), preferred_element_type=F32).astype(BF)

    @pl.when(step == pl.num_programs(0) - 1)
    def _():
        keep.wait()


def make_grads(starts, rows, grads, matrices, state):
    nrel, width, _ = matrices.shape
    whole = pl.BlockSpec(grads.shape, lambda k, s: (0, 0))
    return pl.pallas_call(
        group_grads,
        out_shape=(
            jax.ShapeDtypeStruct(grads.shape, BF),
            jax.ShapeDtypeStruct((2, nrel // 2, width, width), BF),
            jax.ShapeDtypeStruct(state.shape, F32),
        ),
        grid_spec=pltpu.PrefetchScalarGridSpec(
            num_scalar_prefetch=1,
            grid=(nrel,),
            in_specs=[
                whole,
                whole,
                pl.BlockSpec((1, width, width), lambda k, s: (k, 0, 0)),
                pl.BlockSpec(memory_space=pl.ANY),
            ],
            out_specs=(
                whole,
                pl.BlockSpec((1, 1, width, width), lambda k, s: (lax.rem(k, 2), k // 2, 0, 0)),
                pl.BlockSpec(memory_space=pl.ANY),
            ),
            scratch_shapes=[pltpu.SemaphoreType.DMA],
        ),
        compiler_params=pltpu.CompilerParams(vmem_limit_bytes=16 << 20),
        name="make_grads",
    )(starts, rows, grads, matrices, state)


LOW = 64


def tally(stop, part, picks, pos, low, unit, packed):
    samples = 16
    rows = pos.shape[1]
    lanes = 128
    names = picks[pl.ds(pl.multiple_of(stop * samples, samples), samples), :]
    low[0:samples, :] = lax.bitwise_and(names, LOW - 1)
    unit[0:samples, :] = lax.shift_left(jnp.ones_like(names), 8 * lax.shift_right_logical(names, 6))
    place = pos[...] - stop * part
    inside = (place >= 0) & (place < part)
    place = jnp.where(inside, place, 0)
    low[samples : samples + 1, :] = lax.bitwise_and(place, LOW - 1)
    unit[samples : samples + 1, :] = jnp.where(
        inside, lax.shift_left(jnp.full_like(place, 33), 8 * lax.shift_right_logical(place, 6)), 0
    )

    def column(c, carry):
        here = pl.ds(pl.multiple_of(c * lanes, lanes), lanes)
        index = lax.broadcasted_iota(jnp.int32, (LOW, lanes), 0)
        total = jnp.zeros((LOW, lanes), jnp.int32)
        for k in range(samples + 1):
            match = jnp.broadcast_to(low[k : k + 1, here], (LOW, lanes)) == index
            total = total + jnp.where(match, jnp.broadcast_to(unit[k : k + 1, here], (LOW, lanes)), 0)
        packed[stop, :, here] = total
        return carry

    lax.fori_loop(0, rows // lanes, column, 0)


def gather_kernel(
    own_in, ids_in, rows_in, picks_in, target_in, out, rows_out, packed, place_out, starts_out,
    own, ids, rows_ref, picks, target,
    meta, sorted_picks, sorted_target, low, unit, local_sem, fetch_sem, send_sem, recv_sem,
):
    at = Spot()
    mail = Mail(send_sem, recv_sem)
    left, right = at.device(x=turn(at.x, 3)), at.device(x=turn(at.x, 1))
    down, up = at.device(y=turn(at.y, 3)), at.device(y=turn(at.y, 1))
    across = at.device(z=3 - at.z)
    partner = at.device(core=1 - at.core)
    fetch = [
        pltpu.make_async_copy(source, landing, fetch_sem.at[i])
        for i, (source, landing) in enumerate(
            ((own_in, own), (ids_in, ids), (target_in, target), (picks_in, picks), (rows_in, rows_ref))
        )
    ]
    for copy in fetch:
        copy.start()
    greet([left, right, down, up, across, partner])
    fetch[0].wait()
    half = own.shape[1] // 2
    share = half // 4

    def rows(start, size, step):
        return pl.ds(pl.multiple_of(start, step), size)

    start = at.core * half
    mine, first, second = rows(start, half, half), rows(start, half // 2, half), rows(start + half // 2, half // 2, half // 2)

    def quarter(y):
        return rows(start + y * share, share, share)

    def quarter_halves(y):
        return (
            rows(start + y * share, share // 2, share),
            rows(start + y * share + share // 2, share // 2, share // 2),
        )

    me, far = at.zh * 4, (1 - at.zh) * 4
    x0, x1, x2, x3 = at.x, turn(at.x, 1), turn(at.x, 2), turn(at.x, 3)
    y0, y1, y2, y3 = at.y, turn(at.y, 1), turn(at.y, 2), turn(at.y, 3)
    here = pltpu.make_async_copy(own, out.at[at.rel], local_sem)
    here.start()

    def same(ref, device):
        return mail.send(ref, ref, device)

    def a(base, x, rows):
        return out.at[base + x, 0, rows]

    def b(base, x, rows):
        return out.at[base + x, 1, rows]

    gifts = []

    class Quarter:
        def __init__(self, base, x):
            self.base, self.x = base, x
            self.sent = [same(b(base, x, quarter(y0)), device) for device in (up, down)]

        def on(self):
            self.sent[0].wait_recv()
            first = same(b(self.base, self.x, quarter_halves(y3)[0]), up)
            self.sent[1].wait_recv()
            self.sent = [first, same(b(self.base, self.x, quarter_halves(y1)[1]), down)]

        def done(self):
            for copy in self.sent:
                copy.wait_recv()
            gifts.append(same(b(self.base, self.x, mine), partner))

    own_a, own_b = own.at[0, mine], own.at[1, quarter(y0)]
    b_across = mail.send(own_b, b(me, x0, quarter(y0)), across)
    b_right = mail.send(own_b, b(me, x0, quarter(y0)), right)
    b_left = mail.send(own_b, b(me, x0, quarter(y0)), left)
    a_across = mail.send(own_a, a(me, x0, mine), across)
    a_right = mail.send(own_a, a(me, x0, mine), right)
    a_left = mail.send(own_a, a(me, x0, mine), left)

    stops, samples, total = picks.shape
    part = total // stops
    nrel = starts_out.shape[0]
    for copy in fetch[1:]:
        copy.wait()
    place, starts = sort_plan(ids[...], nrel)
    place = place.astype(jnp.int32)
    place_out[...] = place
    starts_out[...] = starts.astype(jnp.int32)
    for s in range(stops):
        meta[s * samples : (s + 1) * samples, :] = picks[s].astype(F32).astype(BF)
    goal = target[...]
    tail = lax.broadcasted_iota(jnp.int32, (16, total), 0)
    meta[stops * samples :, :] = jnp.where(
        tail == 0, jnp.broadcast_to(goal // part, (16, total)), jnp.broadcast_to(lax.rem(goal, part), (16, total))
    ).astype(F32).astype(BF)
    rows_out[total:, :] = jnp.zeros((rows_out.shape[0] - total, rows_out.shape[1]), BF)

    def work(b):
        sort_rows(b, place_out[...], rows_ref, meta, rows_out, sorted_picks, sorted_target, part)

    def count(s):
        tally(s, part, sorted_picks, sorted_target, low, unit, packed)

    h0, h1 = quarter_halves(y0)
    work(0)
    b_right.wait_recv()
    b_on_right = same(b(me, x3, h0), right)
    q_me3 = Quarter(me, x3)
    b_left.wait_recv()
    b_on_left = same(b(me, x1, h1), left)
    q_me1 = Quarter(me, x1)
    b_across.wait_recv()
    b_far_right = same(b(far, x0, quarter(y0)), right)
    b_far_left = same(b(far, x0, quarter(y0)), left)
    q_far0 = Quarter(far, x0)
    work(1)
    a_right.wait_recv()
    a_on_right = same(a(me, x3, first), right)
    gifts.append(same(a(me, x3, mine), partner))
    a_left.wait_recv()
    a_on_left = same(a(me, x1, second), left)
    gifts.append(same(a(me, x1, mine), partner))
    b_on_right.wait_recv()
    b_on_left.wait_recv()
    q_me2 = Quarter(me, x2)
    work(2)
    b_far_right.wait_recv()
    b_far_on_right = same(b(far, x3, h0), right)
    q_far3 = Quarter(far, x3)
    b_far_left.wait_recv()
    b_far_on_left = same(b(far, x1, h1), left)
    q_far1 = Quarter(far, x1)
    a_across.wait_recv()
    a_far_right = same(a(far, x0, mine), right)
    a_far_left = same(a(far, x0, mine), left)
    gifts.append(same(a(far, x0, mine), partner))
    work(3)
    q_me3.on()
    q_me1.on()
    work(4)
    q_far0.on()
    a_on_right.wait_recv()
    a_opposite = [same(a(me, x2, first), across)]
    a_on_left.wait_recv()
    a_opposite.append(same(a(me, x2, second), across))
    gifts.append(same(a(me, x2, mine), partner))
    b_far_on_right.wait_recv()
    b_far_on_left.wait_recv()
    q_far2 = Quarter(far, x2)
    work(5)
    q_me2.on()
    q_me3.done()
    work(6)
    q_far3.on()
    q_me1.done()
    work(7)
    q_far1.on()
    q_far0.done()
    count(0)
    q_far2.on()
    q_me2.done()
    count(1)
    a_far_right.wait_recv()
    gifts.append(same(a(far, x3, mine), partner))
    a_far_left.wait_recv()
    gifts.append(same(a(far, x1, mine), partner))
    q_far3.done()
    count(2)
    for copy in a_opposite:
        copy.wait_recv()
    gifts.append(same(a(far, x2, mine), partner))
    q_far1.done()
    q_far2.done()
    count(3)
    count(4)

    def later(s, carry):
        count(s)
        return carry

    lax.fori_loop(5, stops, later, 0)
    for copy in gifts:
        copy.wait_recv()
    mail.drain()
    here.wait()


def gather_relations(relations, ids, rows, picks, target):
    per, width, _ = relations.shape
    owners = lax.axis_size("rel")
    nrel = owners * per
    stops, samples, total = picks.shape
    vmem = pl.BlockSpec(memory_space=pltpu.VMEM)
    out = pl.pallas_call(
        gather_kernel,
        out_shape=(
            jax.ShapeDtypeStruct((owners, per, width, width), relations.dtype),
            jax.ShapeDtypeStruct((total + 256 + WINDOW_PAD, width), BF),
            jax.ShapeDtypeStruct((stops, LOW, total), jnp.int32),
            jax.ShapeDtypeStruct((1, total), jnp.int32),
            jax.ShapeDtypeStruct((nrel, 128), jnp.int32),
        ),
        in_specs=[pl.BlockSpec(memory_space=pltpu.HBM)] * 5,
        out_specs=(pl.BlockSpec(memory_space=pl.ANY), *[vmem] * 4),
        scratch_shapes=[
            *(pltpu.VMEM(a.shape, a.dtype) for a in (relations, ids, rows, picks, target)),
            pltpu.VMEM((stops * samples + 16, total), BF),
            pltpu.VMEM((stops * samples, total), jnp.int32),
            pltpu.VMEM((1, total), jnp.int32),
            pltpu.VMEM((24, total), jnp.int32),
            pltpu.VMEM((24, total), jnp.int32),
            pltpu.SemaphoreType.DMA,
            pltpu.SemaphoreType.DMA((5,)),
            pltpu.SemaphoreType.DMA((60,)),
            pltpu.SemaphoreType.DMA((60,)),
        ],
        compiler_params=pltpu.CompilerParams(
            collective_id=0, has_side_effects=True, vmem_limit_bytes=24 << 20
        ),
        name="gather_relations",
    )(*(pltpu.with_memory_space_constraint(v, pltpu.HBM) for v in (relations, ids, rows, picks, target)))
    matrices, rows, packed, place, starts = out
    starts = jnp.concatenate([starts[:, 0], jnp.full((1,), total, jnp.int32)])
    return matrices.reshape(nrel, width, width), rows, packed, place, starts


STOPS = 8
learn_rate = 0.005
LOG2E = 1.4426950408889634


def stops_kernel(
    q, packed, entities, state_out, grad_out, held, sent, held_short, sent_short, now, wide, turned_wide, weights, acc,
    local_sem, send_sem, recv_sem,
):
    cand, rel = lax.axis_index("cand"), lax.axis_index("rel")
    n = lax.axis_size("cand")
    ahead, behind = (lax.rem(cand + 1, n), rel), (lax.rem(cand + n - 1, n), rel)
    greet([ahead, behind])
    part, width = entities.shape
    rows = packed.shape[2]
    chunk = part // 2
    block = 256

    fetch = [
        pltpu.make_async_copy(entities.at[pl.ds(h * chunk, chunk)], held.at[h], local_sem.at[h])
        for h in range(2)
    ]
    for copy in fetch:
        copy.start()
    acc[...] = jnp.zeros_like(acc)
    for copy in fetch:
        copy.wait()

    def copier(kind, source, landing):
        return lambda t: pltpu.make_async_remote_copy(
            src_ref=source.at[t],
            dst_ref=landing.at[t + 2],
            send_sem=send_sem.at[kind, t],
            recv_sem=recv_sem.at[kind, t],
            device_id=ahead,
            device_id_type=MESH,
        )

    core = lax.rem(cand, 2)
    hop, hop_short = copier(0, sent, held), copier(1, sent_short, held_short)

    def step(t, carry):
        half = lax.rem(t, 2)
        stop = t // 2
        here_rows = pl.ds(pl.multiple_of(half * chunk, chunk), chunk)

        @pl.when(t < 2)
        def _():
            now[...] = held[t]

        @pl.when((t >= 2) & (core == 1))
        def _():
            hop(t - 2).wait_recv()
            now[...] = held[t]

        @pl.when((t >= 2) & (core == 0))
        def _():
            hop_short(t - 2).wait_recv()
            now[...] = held_short[t].astype(F32)

        rounded = now[...].astype(BF)
        wide[here_rows, :] = rounded
        pieces = []
        for i in range(rows // block):
            here = pl.ds(i * block, block)
            logits = lax.dot_general(
                rounded, q[here, :], (((1,), (1,)), ((), ())), preferred_element_type=F32
            )
            marks = packed[stop, :, here]
            marks = jnp.concatenate(
                [lax.shift_right_logical(marks, 16 * half + 8 * p) for p in range(chunk // LOW)], axis=0
            )
            named = lax.bitwise_and(marks, 31).astype(F32)
            chance = 1.0 / (1.0 + jnp.exp2(logits * -LOG2E))
            product = named * chance
            pieces.append(jnp.where(lax.bitwise_and(marks, 32) != 0, product - 1.0, product).astype(BF))
        weight = jnp.concatenate(pieces, axis=1)
        weights[here_rows, :] = weight
        change = jnp.dot(weight, q[0:rows, :], preferred_element_type=F32)
        moved = now[...] - learn_rate * change
        sent[t] = moved
        sent_short[t] = moved.astype(BF)

        @pl.when((t < 2 * STOPS - 2) & (core == 0))
        def _():
            hop(t).start()

        @pl.when((t < 2 * STOPS - 2) & (core == 1))
        def _():
            hop_short(t).start()

        @pl.when(half == 1)
        def _():
            turned_wide[...] = wide[...].astype(F32).T.astype(BF)
            big = 512

            def gather(c, carry):
                here = pl.ds(pl.multiple_of(c * big, big), big)
                acc[:, here] += jnp.dot(turned_wide[...], weights[:, here], preferred_element_type=F32)
                return carry

            lax.fori_loop(0, rows // big, gather, 0, unroll=True)

        return carry

    lax.fori_loop(0, 2 * STOPS, step, 0)
    for h in range(2):
        state_out[pl.ds(h * chunk, chunk), :] = sent[2 * STOPS - 2 + h]

    def turned(c, carry):
        here = pl.ds(pl.multiple_of(c * block, block), block)
        grad_out[here, :] = acc[:, here].T.astype(BF)
        return carry

    lax.fori_loop(0, rows // block, turned, 0)
    grad_out[rows:, :] = jnp.zeros((grad_out.shape[0] - rows, width), BF)

    def drained(t, carry):
        @pl.when(core == 0)
        def _():
            hop(t).wait_send()

        @pl.when(core == 1)
        def _():
            hop_short(t).wait_send()

        return carry

    lax.fori_loop(0, 2 * STOPS - 2, drained, 0)


def run_stops(queries, packed, entities):
    padded, width = queries.shape
    rows = packed.shape[2]
    part = entities.shape[0]
    chunk = part // 2
    vmem = pl.BlockSpec(memory_space=pltpu.VMEM)
    hops = 2 * STOPS
    return pl.pallas_call(
        stops_kernel,
        out_shape=(
            jax.ShapeDtypeStruct((part, width), F32),
            jax.ShapeDtypeStruct((padded, width), BF),
        ),
        in_specs=[vmem, vmem, pl.BlockSpec(memory_space=pltpu.HBM)],
        out_specs=(vmem, vmem),
        scratch_shapes=[
            pltpu.VMEM((hops, chunk, width), F32),
            pltpu.VMEM((hops, chunk, width), F32),
            pltpu.VMEM((hops, chunk, width), BF),
            pltpu.VMEM((hops, chunk, width), BF),
            pltpu.VMEM((chunk, width), F32),
            pltpu.VMEM((part, width), BF),
            pltpu.VMEM((width, part), BF),
            pltpu.VMEM((part, rows), BF),
            pltpu.VMEM((width, rows), F32),
            pltpu.SemaphoreType.DMA((2,)),
            pltpu.SemaphoreType.DMA((2, hops)),
            pltpu.SemaphoreType.DMA((2, hops)),
        ],
        compiler_params=pltpu.CompilerParams(
            collective_id=2, has_side_effects=True, vmem_limit_bytes=28 << 20
        ),
        name="run_stops",
    )(queries, packed, entities)


def add_into(dst, *others):
    lead, size = [], dst.size
    for n in dst.shape[:-2]:
        if size <= 1 << 15:
            break
        lead.append(n)
        size //= n
    total = 1
    for n in lead:
        total *= n

    def body(i, carry):
        index, rest = [], i
        for n in reversed(lead):
            index.insert(0, lax.rem(rest, n))
            rest = rest // n
        index = tuple(index) if index else ...
        value = dst[index].astype(F32)
        for other in others:
            value = value + other[index].astype(F32)
        dst[index] = value.astype(dst.dtype)
        return carry

    if total == 1:
        body(0, 0)
    else:
        lax.fori_loop(0, total, body, 0)


ORDERS = (("xyz", "yxz", "zxy", "xyz"), ("yxz", "xyz", "zyx", "yxz"))
SIZES = {"zh": 2, "x": 4, "zl": 2, "y": 4}
OF_AXIS = {"x": ("x",), "y": ("y",), "z": ("zh", "zl")}


def piece_shape(order, phase, rows, columns):
    gone = [name for axis in order[: phase + 1] for name in OF_AXIS[axis]]
    free = [n for name, n in SIZES.items() if name not in gone]
    if free:
        return (free[0] // 2, *free[1:], rows, columns), (*free, rows, columns)
    return (rows, columns // 2), (rows, columns)


def landing_shapes(order, rows, columns):
    shapes = []
    for phase in range(3):
        half, whole = piece_shape(order, phase, rows, columns)
        shapes += [(2, *half), (2, *whole)]
    return shapes


class Eighth:
    def __init__(self, mail, at, base, row, column, order, landings, ways):
        self.mail, self.at, self.base, self.order, self.landings, self.ways = mail, at, base, order, landings, ways
        self.row, self.column = row, column
        self.fixed, self.phase = {}, 0

    def view(self, fixed, cut=None):
        index = []
        free = [name for name in SIZES if name not in fixed]
        for name, n in SIZES.items():
            if name in fixed:
                index.append(fixed[name])
            elif cut is not None and name == free[0]:
                index.append(pl.ds(cut * (n // 2), n // 2))
            else:
                index.append(slice(None))
        start, size = self.column
        if cut is not None and not free:
            start, size = start + cut * (size // 2), size // 2
        return self.base.at[(*index, pl.ds(*self.row), pl.ds(start, size))]

    def spot(self, by):
        axis = self.order[self.phase]
        t = turn(getattr(self.at, axis), by)
        return {**self.fixed, **({"zh": t // 2, "zl": lax.rem(t, 2)} if axis == "z" else {axis: t})}

    def one(self):
        self.half, self.whole = self.landings[2 * self.phase : 2 * self.phase + 2]
        self.devices = self.ways[self.order[self.phase]]
        self.h = [
            self.mail.send(self.view(self.spot(2), d), self.half.at[d], device)
            for d, device in enumerate(self.devices)
        ]

    def two(self):
        self.f = []
        for d, device in enumerate(self.devices):
            self.h[d].wait_recv()
            target = self.spot((1, 3)[d])
            add_into(self.view(target, d), self.half.at[d])
            self.f.append(self.mail.send(self.view(target), self.whole.at[d], device))

    def three(self):
        for copy in self.f:
            copy.wait_recv()
        self.fixed = self.spot(0)
        self.phase += 1
        if self.phase < 3:
            add_into(self.view(self.fixed), self.whole.at[0], self.whole.at[1])
            self.one()

    def result(self):
        own = self.view(self.fixed)[...].astype(F32)
        return own + self.whole[0].astype(F32) + self.whole[1].astype(F32)


def scatter_kernel(place, terms, back, out, source_grad, got, *rest):
    swap_send, swap_recv, send_sem, recv_sem = rest[-4:]
    landings = rest[:-4]
    at = Spot()
    mail = Mail(send_sem, recv_sem)
    partner = at.device(core=1 - at.core)
    ways = {
        "x": (at.device(x=turn(at.x, 1)), at.device(x=turn(at.x, 3))),
        "y": (at.device(y=turn(at.y, 1)), at.device(y=turn(at.y, 3))),
        "z": (at.device(z=turn(at.z, 1)), at.device(z=turn(at.z, 3))),
    }
    greet([partner, *ways["x"], *ways["y"], *ways["z"]])

    def swap(j, r):
        zh, x = r // 4, lax.rem(r, 4)
        return pltpu.make_async_remote_copy(
            src_ref=terms.at[j, zh, x, :, :, 1 - at.core],
            dst_ref=got.at[j, zh, x],
            send_sem=swap_send.at[j, r],
            recv_sem=swap_recv.at[j, r],
            device_id=partner,
            device_id_type=MESH,
        )

    def offer(i, carry):
        swap(i // 8, lax.rem(i, 8)).start()
        return carry

    lax.fori_loop(0, 16, offer, 0)

    def joined(j):
        def one(r, carry):
            swap(j, r).wait_recv()
            zh, x = r // 4, lax.rem(r, 4)
            add_into(got.at[j, zh, x], terms.at[j, zh, x, :, :, at.core])
            return carry

        lax.fori_loop(0, 8, one, 0)

    def unsort(begin, end):
        lanes = 128
        total = place.shape[1]

        def one(b, carry):
            here = pl.ds(pl.multiple_of(b * lanes, lanes), lanes)
            mine = jnp.broadcast_to(place[:, here], (lanes, lanes)).T
            index = lax.broadcasted_iota(jnp.int32, (lanes, lanes), 1)
            choose = jnp.concatenate(
                [(mine == index + t * lanes).astype(F32).astype(BF) for t in range(total // lanes)], axis=1
            )
            source_grad[here, :] = jnp.dot(choose, back[0:total, :], preferred_element_type=F32).astype(BF)
            return carry

        lax.fori_loop(begin, end, one, 0)


    rows, columns = got.shape[-2] // 2, got.shape[-1] // 2
    units = [
        [
            Eighth(
                mail, at, got.at[j], (u // 2 * rows, rows), (u % 2 * columns, columns), ORDERS[j][u],
                landings[(4 * j + u) * 6 : (4 * j + u) * 6 + 6], ways,
            )
            for u in range(4)
        ]
        for j in range(2)
    ]
    every = [unit for group in units for unit in group]
    for j in range(2):
        joined(j)
        for unit in units[j]:
            unit.one()
    unsort(0, 4)
    for phase in range(3):
        for u, unit in enumerate(every):
            unit.two()
            if u % 4 == 3:
                unsort(4 + 4 * phase + u // 4, 5 + 4 * phase + u // 4)
        for u, unit in enumerate(every):
            unit.three()
            if u % 4 == 3:
                unsort(6 + 4 * phase + u // 4, 7 + 4 * phase + u // 4)
    for j in range(2):
        for u, unit in enumerate(units[j]):
            out[unit.row[0] : unit.row[0] + rows, j, unit.column[0] : unit.column[0] + columns] = unit.result()

    def sent(i, carry):
        swap(i // 8, lax.rem(i, 8)).wait_send()
        return carry

    lax.fori_loop(0, 16, sent, 0)
    mail.drain()


def scatter_grads(place, terms, back):
    width = back.shape[1]
    total = place.shape[1]
    rows = width // 16
    terms = terms.reshape(2, 2, 4, 2, 4, 2, rows, width)
    v = lambda *lead: pltpu.VMEM((*lead, rows, width), BF)
    vmem = pl.BlockSpec(memory_space=pltpu.VMEM)
    return pl.pallas_call(
        scatter_kernel,
        out_shape=(jax.ShapeDtypeStruct((rows, 2, width), F32), jax.ShapeDtypeStruct((total, width), BF)),
        in_specs=[vmem, vmem, vmem],
        out_specs=(vmem, vmem),
        scratch_shapes=[
            v(2, 2, 4, 2, 4),
            *(
                pltpu.VMEM(shape, BF)
                for group in ORDERS
                for order in group
                for shape in landing_shapes(order, rows // 2, width // 2)
            ),
            pltpu.SemaphoreType.DMA((2, 8)),
            pltpu.SemaphoreType.DMA((2, 8)),
            pltpu.SemaphoreType.DMA((96,)),
            pltpu.SemaphoreType.DMA((96,)),
        ],
        compiler_params=pltpu.CompilerParams(
            collective_id=1, has_side_effects=True, vmem_limit_bytes=30 << 20
        ),
        name="scatter_grads",
    )(place, terms, back)


def shards(source_rows, rel_ids, relations, entities, pos_slot, negatives):
    rows = source_rows.shape[0]
    matrices, sorted_rows, packed, place, starts = gather_relations(
        relations,
        rel_ids.reshape(1, rows),
        source_rows,
        jnp.transpose(negatives, (0, 2, 1)),
        pos_slot.reshape(1, rows),
    )
    queries = make_queries(starts, sorted_rows, matrices)
    state, query_grad = run_stops(queries, packed, entities)
    back, terms, state = make_grads(starts, sorted_rows, query_grad, matrices, state)
    relation_grad, source_grad = scatter_grads(place, terms, back)
    return (state, source_grad, relation_grad)


def solution(mesh):
    placed = (
        P(("cand", "rel"), None),
        P(("cand", "rel"), None),
        P("rel", None, None),
        P(("cand", "rel"), None),
        P(("cand", "rel")),
        P(None, ("cand", "rel"), None),
    )
    return jax.shard_map(
        shards,
        mesh=mesh,
        in_specs=placed,
        out_specs=(P(("cand", "rel"), None), P(("cand", "rel"), None), P("cand", "rel", None)),
        check_vma=False,
    )
```

```python
import functools

import jax
import jax.numpy as jnp
from jax import lax
from jax.experimental import pallas as pl
from jax.experimental.pallas import tpu as pltpu
from jax.sharding import PartitionSpec as P

MESH = pl.DeviceIdType.MESH
BF = jnp.bfloat16
F32 = jnp.float32


class Spot:
    def __init__(self):
        cand, rel = lax.axis_index("cand"), lax.axis_index("rel")
        self.core = lax.rem(cand, 2)
        self.y = lax.rem(cand // 2, 4)
        self.zl = cand // 8
        self.x = lax.rem(rel, 4)
        self.zh = rel // 4
        self.z = self.zh * 2 + self.zl
        self.rel = rel

    def device(self, x=None, y=None, z=None, core=None):
        x = self.x if x is None else x
        y = self.y if y is None else y
        z = self.z if z is None else z
        core = self.core if core is None else core
        return ((lax.rem(z, 2) * 4 + y) * 2 + core, (z // 2) * 4 + x)


def turn(i, by):
    return lax.rem(i + by, 4)


def greet(devices):
    barrier = pltpu.get_barrier_semaphore()
    for device in devices:
        pl.semaphore_signal(barrier, inc=1, device_id=device, device_id_type=MESH)
    pl.semaphore_wait(barrier, len(devices))


class Mail:
    def __init__(self, send_sem, recv_sem):
        self.send_sem, self.recv_sem, self.count, self.sent = send_sem, recv_sem, 0, []

    def send(self, src, dst, device):
        i = self.count
        self.count += 1
        copy = pltpu.make_async_remote_copy(
            src_ref=src,
            dst_ref=dst,
            send_sem=self.send_sem.at[i],
            recv_sem=self.recv_sem.at[i],
            device_id=device,
            device_id_type=MESH,
        )
        copy.start()
        self.sent.append(copy)
        return copy

    def drain(self):
        for copy in self.sent:
            copy.wait_send()


WINDOW_PAD = 16


def sort_plan(ids, nrel):
    rows = ids.shape[1]
    block = 256
    named = (jnp.broadcast_to(ids, (nrel, rows)) == lax.broadcasted_iota(jnp.int32, (nrel, rows), 0)).astype(F32)
    before = (
        lax.broadcasted_iota(jnp.int32, (block, block), 0) < lax.broadcasted_iota(jnp.int32, (block, block), 1)
    ).astype(BF)
    running = jnp.zeros((nrel, 1), F32)
    ranks = []
    for b in range(rows // block):
        part = named[:, b * block : (b + 1) * block]
        ranks.append(jnp.dot(part.astype(BF), before, preferred_element_type=F32) + running)
        running = running + jnp.sum(part, axis=1, keepdims=True)
    rank = jnp.concatenate(ranks, axis=1)
    lower = (
        lax.broadcasted_iota(jnp.int32, (nrel, nrel), 1) < lax.broadcasted_iota(jnp.int32, (nrel, nrel), 0)
    ).astype(BF)
    starts = jnp.dot(lower, jnp.broadcast_to(running, (nrel, 128)).astype(BF), preferred_element_type=F32)
    place = jnp.sum(named * (rank + starts[:, 0:1]), axis=0, keepdims=True)
    return place, starts


def sort_rows(b, place, rows_ref, meta_ref, rows_out, picks_out, pos_out, part):
    rows = place.shape[1]
    block = 256
    here = pl.ds(b * block, block)
    spot = lax.broadcasted_iota(jnp.int32, (block, rows), 0) + b * block
    choose = (jnp.broadcast_to(place, (block, rows)) == spot).astype(F32).astype(BF)
    rows_out[here, :] = jnp.dot(choose, rows_ref[...], preferred_element_type=F32).astype(BF)
    meta = lax.dot_general(
        meta_ref[...], choose, (((1,), (1,)), ((), ())), preferred_element_type=F32
    ).astype(jnp.int32)
    named = picks_out.shape[0]
    picks_out[:, here] = meta[0:named]
    pos_out[:, here] = meta[named : named + 1] * part + meta[named + 1 : named + 2]


TOGETHER = 4


def group_queries(starts, rows_ref, matrix, out):
    for r in range(TOGETHER):
        window, inside = out_window(starts, TOGETHER * pl.program_id(0) + r)
        new = jnp.dot(rows_ref[window, :], matrix[r], preferred_element_type=F32).astype(BF)
        out[window, :] = jnp.where(inside, new, out[window, :])


def out_window(starts, k):
    size = 256 + WINDOW_PAD
    start, end = starts[k], starts[k + 1]
    base = pl.multiple_of(start // WINDOW_PAD * WINDOW_PAD, WINDOW_PAD)
    row = lax.broadcasted_iota(jnp.int32, (size, 512), 0) + base
    return pl.ds(base, size), (row >= start) & (row < end)


def make_queries(starts, rows, matrices):
    nrel, width, _ = matrices.shape
    return pl.pallas_call(
        group_queries,
        out_shape=jax.ShapeDtypeStruct(rows.shape, BF),
        grid_spec=pltpu.PrefetchScalarGridSpec(
            num_scalar_prefetch=1,
            grid=(nrel // TOGETHER,),
            in_specs=[
                pl.BlockSpec(rows.shape, lambda k, s: (0, 0)),
                pl.BlockSpec((TOGETHER, width, width), lambda k, s: (k, 0, 0)),
            ],
            out_specs=pl.BlockSpec(rows.shape, lambda k, s: (0, 0)),
        ),
        compiler_params=pltpu.CompilerParams(vmem_limit_bytes=16 << 20),
        name="make_queries",
    )(starts, rows, matrices)


PAIR = 2


def group_grads(starts, rows_ref, grads, matrix, state, back, terms, state_out, sem):
    step = pl.program_id(0)
    keep = pltpu.make_async_copy(state, state_out, sem)

    @pl.when(step == 0)
    def _():
        keep.start()

    for r in range(PAIR):
        window, inside = out_window(starts, PAIR * step + r)
        grad = grads[window, :]
        rows = rows_ref[window, :]
        rows = jnp.where(inside, rows, jnp.zeros_like(rows))
        terms[r, 0] = lax.dot_general(rows, grad, (((0,), (0,)), ((), ())), preferred_element_type=F32).astype(BF)
        new = lax.dot_general(grad, matrix[r], (((1,), (1,)), ((), ())), preferred_element_type=F32).astype(BF)
        back[window, :] = jnp.where(inside, new, back[window, :])

    @pl.when(step == pl.num_programs(0) - 1)
    def _():
        keep.wait()


def make_grads(starts, rows, grads, matrices, state):
    nrel, width, _ = matrices.shape
    whole = pl.BlockSpec(grads.shape, lambda k, s: (0, 0))
    return pl.pallas_call(
        group_grads,
        out_shape=(
            jax.ShapeDtypeStruct(grads.shape, BF),
            jax.ShapeDtypeStruct((2, nrel // 2, width, width), BF),
            jax.ShapeDtypeStruct(state.shape, F32),
        ),
        grid_spec=pltpu.PrefetchScalarGridSpec(
            num_scalar_prefetch=1,
            grid=(nrel // PAIR,),
            in_specs=[
                whole,
                whole,
                pl.BlockSpec((PAIR, width, width), lambda k, s: (k, 0, 0)),
                pl.BlockSpec(memory_space=pl.ANY),
            ],
            out_specs=(
                whole,
                pl.BlockSpec((PAIR, 1, width, width), lambda k, s: (0, k, 0, 0)),
                pl.BlockSpec(memory_space=pl.ANY),
            ),
            scratch_shapes=[pltpu.SemaphoreType.DMA],
        ),
        compiler_params=pltpu.CompilerParams(vmem_limit_bytes=16 << 20),
        name="make_grads",
    )(starts, rows, grads, matrices, state)


LOW = 64


def tally(stop, part, picks, pos, low, unit, packed):
    samples = 16
    rows = pos.shape[1]
    lanes = 128
    names = picks[pl.ds(pl.multiple_of(stop * samples, samples), samples), :]
    low[0:samples, :] = lax.bitwise_and(names, LOW - 1)
    unit[0:samples, :] = lax.shift_left(jnp.ones_like(names), 8 * lax.shift_right_logical(names, 6))
    place = pos[...] - stop * part
    inside = (place >= 0) & (place < part)
    place = jnp.where(inside, place, 0)
    low[samples : samples + 1, :] = lax.bitwise_and(place, LOW - 1)
    unit[samples : samples + 1, :] = jnp.where(
        inside, lax.shift_left(jnp.full_like(place, 33), 8 * lax.shift_right_logical(place, 6)), 0
    )

    def column(c, carry):
        here = pl.ds(pl.multiple_of(c * lanes, lanes), lanes)
        index = lax.broadcasted_iota(jnp.int32, (LOW, lanes), 0)
        total = jnp.zeros((LOW, lanes), jnp.int32)
        for k in range(samples + 1):
            match = jnp.broadcast_to(low[k : k + 1, here], (LOW, lanes)) == index
            total = total + jnp.where(match, jnp.broadcast_to(unit[k : k + 1, here], (LOW, lanes)), 0)
        packed[stop, :, here] = total
        return carry

    lax.fori_loop(0, rows // lanes, column, 0)


def gather_kernel(
    own_in, ids_in, rows_in, picks_in, target_in, out, rows_out, packed, place_out, starts_out,
    own, ids, rows_ref, picks, target,
    meta, sorted_picks, sorted_target, low, unit, local_sem, fetch_sem, send_sem, recv_sem,
):
    at = Spot()
    mail = Mail(send_sem, recv_sem)
    left, right = at.device(x=turn(at.x, 3)), at.device(x=turn(at.x, 1))
    down, up = at.device(y=turn(at.y, 3)), at.device(y=turn(at.y, 1))
    across = at.device(z=3 - at.z)
    partner = at.device(core=1 - at.core)
    fetch = [
        pltpu.make_async_copy(source, landing, fetch_sem.at[i])
        for i, (source, landing) in enumerate(
            ((own_in, own), (ids_in, ids), (target_in, target), (picks_in, picks), (rows_in, rows_ref))
        )
    ]
    for copy in fetch:
        copy.start()
    greet([left, right, down, up, across, partner])
    fetch[0].wait()
    half = own.shape[1] // 2
    share = half // 4

    def rows(start, size, step):
        return pl.ds(pl.multiple_of(start, step), size)

    start = at.core * half
    mine, first, second = rows(start, half, half), rows(start, half // 2, half), rows(start + half // 2, half // 2, half // 2)

    def quarter(y):
        return rows(start + y * share, share, share)

    def quarter_halves(y):
        return (
            rows(start + y * share, share // 2, share),
            rows(start + y * share + share // 2, share // 2, share // 2),
        )

    me, far = at.zh * 4, (1 - at.zh) * 4
    x0, x1, x2, x3 = at.x, turn(at.x, 1), turn(at.x, 2), turn(at.x, 3)
    y0, y1, y2, y3 = at.y, turn(at.y, 1), turn(at.y, 2), turn(at.y, 3)
    here = pltpu.make_async_copy(own, out.at[at.rel], local_sem)
    here.start()

    def same(ref, device):
        return mail.send(ref, ref, device)

    def a(base, x, rows):
        return out.at[base + x, 0, rows]

    def b(base, x, rows):
        return out.at[base + x, 1, rows]

    gifts = []

    class Quarter:
        def __init__(self, base, x):
            self.base, self.x = base, x
            self.sent = [same(b(base, x, quarter(y0)), device) for device in (up, down)]

        def on(self):
            self.sent[0].wait_recv()
            first = same(b(self.base, self.x, quarter_halves(y3)[0]), up)
            self.sent[1].wait_recv()
            self.sent = [first, same(b(self.base, self.x, quarter_halves(y1)[1]), down)]

        def done(self):
            for copy in self.sent:
                copy.wait_recv()
            gifts.append(same(b(self.base, self.x, mine), partner))

    own_a, own_b = own.at[0, mine], own.at[1, quarter(y0)]
    b_across = mail.send(own_b, b(me, x0, quarter(y0)), across)
    b_right = mail.send(own_b, b(me, x0, quarter(y0)), right)
    b_left = mail.send(own_b, b(me, x0, quarter(y0)), left)
    a_across = mail.send(own_a, a(me, x0, mine), across)
    a_right = mail.send(own_a, a(me, x0, mine), right)
    a_left = mail.send(own_a, a(me, x0, mine), left)

    stops, samples, total = picks.shape
    part = total // stops
    nrel = starts_out.shape[0]
    for copy in fetch[1:]:
        copy.wait()
    place, starts = sort_plan(ids[...], nrel)
    place = place.astype(jnp.int32)
    place_out[...] = place
    starts_out[...] = starts.astype(jnp.int32)
    for s in range(stops):
        meta[s * samples : (s + 1) * samples, :] = picks[s].astype(F32).astype(BF)
    goal = target[...]
    tail = lax.broadcasted_iota(jnp.int32, (16, total), 0)
    meta[stops * samples :, :] = jnp.where(
        tail == 0, jnp.broadcast_to(goal // part, (16, total)), jnp.broadcast_to(lax.rem(goal, part), (16, total))
    ).astype(F32).astype(BF)
    rows_out[total:, :] = jnp.zeros((rows_out.shape[0] - total, rows_out.shape[1]), BF)

    def work(b):
        sort_rows(b, place_out[...], rows_ref, meta, rows_out, sorted_picks, sorted_target, part)

    def count(s):
        tally(s, part, sorted_picks, sorted_target, low, unit, packed)

    h0, h1 = quarter_halves(y0)
    work(0)
    b_right.wait_recv()
    b_on_right = same(b(me, x3, h0), right)
    q_me3 = Quarter(me, x3)
    b_left.wait_recv()
    b_on_left = same(b(me, x1, h1), left)
    q_me1 = Quarter(me, x1)
    b_across.wait_recv()
    b_far_right = same(b(far, x0, quarter(y0)), right)
    b_far_left = same(b(far, x0, quarter(y0)), left)
    q_far0 = Quarter(far, x0)
    work(1)
    a_right.wait_recv()
    a_on_right = same(a(me, x3, first), right)
    gifts.append(same(a(me, x3, mine), partner))
    a_left.wait_recv()
    a_on_left = same(a(me, x1, second), left)
    gifts.append(same(a(me, x1, mine), partner))
    b_on_right.wait_recv()
    b_on_left.wait_recv()
    q_me2 = Quarter(me, x2)
    work(2)
    b_far_right.wait_recv()
    b_far_on_right = same(b(far, x3, h0), right)
    q_far3 = Quarter(far, x3)
    b_far_left.wait_recv()
    b_far_on_left = same(b(far, x1, h1), left)
    q_far1 = Quarter(far, x1)
    a_across.wait_recv()
    a_far_right = same(a(far, x0, mine), right)
    a_far_left = same(a(far, x0, mine), left)
    gifts.append(same(a(far, x0, mine), partner))
    work(3)
    q_me3.on()
    q_me1.on()
    work(4)
    q_far0.on()
    a_on_right.wait_recv()
    a_opposite = [same(a(me, x2, first), across)]
    a_on_left.wait_recv()
    a_opposite.append(same(a(me, x2, second), across))
    gifts.append(same(a(me, x2, mine), partner))
    b_far_on_right.wait_recv()
    b_far_on_left.wait_recv()
    q_far2 = Quarter(far, x2)
    work(5)
    q_me2.on()
    q_me3.done()
    work(6)
    q_far3.on()
    q_me1.done()
    work(7)
    q_far1.on()
    q_far0.done()
    count(0)
    q_far2.on()
    q_me2.done()
    count(1)
    a_far_right.wait_recv()
    gifts.append(same(a(far, x3, mine), partner))
    a_far_left.wait_recv()
    gifts.append(same(a(far, x1, mine), partner))
    q_far3.done()
    count(2)
    for copy in a_opposite:
        copy.wait_recv()
    gifts.append(same(a(far, x2, mine), partner))
    q_far1.done()
    q_far2.done()
    count(3)
    count(4)

    def later(s, carry):
        count(s)
        return carry

    lax.fori_loop(5, stops, later, 0)
    for copy in gifts:
        copy.wait_recv()
    mail.drain()
    here.wait()


def gather_relations(relations, ids, rows, picks, target):
    per, width, _ = relations.shape
    owners = lax.axis_size("rel")
    nrel = owners * per
    stops, samples, total = picks.shape
    vmem = pl.BlockSpec(memory_space=pltpu.VMEM)
    out = pl.pallas_call(
        gather_kernel,
        out_shape=(
            jax.ShapeDtypeStruct((owners, per, width, width), relations.dtype),
            jax.ShapeDtypeStruct((total + 256 + WINDOW_PAD, width), BF),
            jax.ShapeDtypeStruct((stops, LOW, total), jnp.int32),
            jax.ShapeDtypeStruct((1, total), jnp.int32),
            jax.ShapeDtypeStruct((nrel, 128), jnp.int32),
        ),
        in_specs=[pl.BlockSpec(memory_space=pltpu.HBM)] * 5,
        out_specs=(pl.BlockSpec(memory_space=pl.ANY), *[vmem] * 4),
        scratch_shapes=[
            *(pltpu.VMEM(a.shape, a.dtype) for a in (relations, ids, rows, picks, target)),
            pltpu.VMEM((stops * samples + 16, total), BF),
            pltpu.VMEM((stops * samples, total), jnp.int32),
            pltpu.VMEM((1, total), jnp.int32),
            pltpu.VMEM((24, total), jnp.int32),
            pltpu.VMEM((24, total), jnp.int32),
            pltpu.SemaphoreType.DMA,
            pltpu.SemaphoreType.DMA((5,)),
            pltpu.SemaphoreType.DMA((60,)),
            pltpu.SemaphoreType.DMA((60,)),
        ],
        compiler_params=pltpu.CompilerParams(
            collective_id=0, has_side_effects=True, vmem_limit_bytes=24 << 20
        ),
        name="gather_relations",
    )(*(pltpu.with_memory_space_constraint(v, pltpu.HBM) for v in (relations, ids, rows, picks, target)))
    matrices, rows, packed, place, starts = out
    starts = jnp.concatenate([starts[:, 0], jnp.full((1,), total, jnp.int32)])
    return matrices.reshape(nrel, width, width), rows, packed, place, starts


STOPS = 8
learn_rate = 0.005
LOG2E = 1.4426950408889634


def stops_kernel(
    q, packed, entities, state_out, grad_out, held, sent, held_short, sent_short, now, wide, turned_wide, weights, acc,
    local_sem, send_sem, recv_sem,
):
    cand, rel = lax.axis_index("cand"), lax.axis_index("rel")
    n = lax.axis_size("cand")
    ahead, behind = (lax.rem(cand + 1, n), rel), (lax.rem(cand + n - 1, n), rel)
    greet([ahead, behind])
    part, width = entities.shape
    rows = packed.shape[2]
    chunk = part // 2
    block = 256

    fetch = [
        pltpu.make_async_copy(entities.at[pl.ds(h * chunk, chunk)], held.at[h], local_sem.at[h])
        for h in range(2)
    ]
    for copy in fetch:
        copy.start()
    acc[...] = jnp.zeros_like(acc)
    for copy in fetch:
        copy.wait()

    def copier(kind, source, landing):
        return lambda t: pltpu.make_async_remote_copy(
            src_ref=source.at[t],
            dst_ref=landing.at[t + 2],
            send_sem=send_sem.at[kind, t],
            recv_sem=recv_sem.at[kind, t],
            device_id=ahead,
            device_id_type=MESH,
        )

    core = lax.rem(cand, 2)
    hop, hop_short = copier(0, sent, held), copier(1, sent_short, held_short)

    def step(t, carry):
        half = lax.rem(t, 2)
        stop = t // 2
        here_rows = pl.ds(pl.multiple_of(half * chunk, chunk), chunk)

        @pl.when(t < 2)
        def _():
            now[...] = held[t]

        @pl.when((t >= 2) & (core == 1))
        def _():
            hop(t - 2).wait_recv()
            now[...] = held[t]

        @pl.when((t >= 2) & (core == 0))
        def _():
            hop_short(t - 2).wait_recv()
            now[...] = held_short[t].astype(F32)

        rounded = now[...].astype(BF)
        wide[here_rows, :] = rounded
        pieces = []
        for i in range(rows // block):
            here = pl.ds(i * block, block)
            logits = lax.dot_general(
                rounded, q[here, :], (((1,), (1,)), ((), ())), preferred_element_type=F32
            )
            marks = packed[stop, :, here]
            marks = jnp.concatenate(
                [lax.shift_right_logical(marks, 16 * half + 8 * p) for p in range(chunk // LOW)], axis=0
            )
            named = lax.bitwise_and(marks, 31).astype(F32)
            chance = 1.0 / (1.0 + jnp.exp2(logits * -LOG2E))
            product = named * chance
            pieces.append(jnp.where(lax.bitwise_and(marks, 32) != 0, product - 1.0, product).astype(BF))
        weight = jnp.concatenate(pieces, axis=1)
        weights[here_rows, :] = weight
        change = jnp.dot(weight, q[0:rows, :], preferred_element_type=F32)
        moved = now[...] - learn_rate * change
        sent[t] = moved
        sent_short[t] = moved.astype(BF)

        @pl.when((t < 2 * STOPS - 2) & (core == 0))
        def _():
            hop(t).start()

        @pl.when((t < 2 * STOPS - 2) & (core == 1))
        def _():
            hop_short(t).start()

        @pl.when(half == 1)
        def _():
            turned_wide[...] = wide[...].astype(F32).T.astype(BF)
            big = 512

            def gather(c, carry):
                here = pl.ds(pl.multiple_of(c * big, big), big)
                acc[:, here] += jnp.dot(turned_wide[...], weights[:, here], preferred_element_type=F32)
                return carry

            lax.fori_loop(0, rows // big, gather, 0, unroll=True)

        return carry

    lax.fori_loop(0, 2 * STOPS, step, 0)
    for h in range(2):
        state_out[pl.ds(h * chunk, chunk), :] = sent[2 * STOPS - 2 + h]

    def turned(c, carry):
        here = pl.ds(pl.multiple_of(c * block, block), block)
        grad_out[here, :] = acc[:, here].T.astype(BF)
        return carry

    lax.fori_loop(0, rows // block, turned, 0)
    grad_out[rows:, :] = jnp.zeros((grad_out.shape[0] - rows, width), BF)

    def drained(t, carry):
        @pl.when(core == 0)
        def _():
            hop(t).wait_send()

        @pl.when(core == 1)
        def _():
            hop_short(t).wait_send()

        return carry

    lax.fori_loop(0, 2 * STOPS - 2, drained, 0)


def run_stops(queries, packed, entities):
    padded, width = queries.shape
    rows = packed.shape[2]
    part = entities.shape[0]
    chunk = part // 2
    vmem = pl.BlockSpec(memory_space=pltpu.VMEM)
    hops = 2 * STOPS
    return pl.pallas_call(
        stops_kernel,
        out_shape=(
            jax.ShapeDtypeStruct((part, width), F32),
            jax.ShapeDtypeStruct((padded, width), BF),
        ),
        in_specs=[vmem, vmem, pl.BlockSpec(memory_space=pltpu.HBM)],
        out_specs=(vmem, vmem),
        scratch_shapes=[
            pltpu.VMEM((hops, chunk, width), F32),
            pltpu.VMEM((hops, chunk, width), F32),
            pltpu.VMEM((hops, chunk, width), BF),
            pltpu.VMEM((hops, chunk, width), BF),
            pltpu.VMEM((chunk, width), F32),
            pltpu.VMEM((part, width), BF),
            pltpu.VMEM((width, part), BF),
            pltpu.VMEM((part, rows), BF),
            pltpu.VMEM((width, rows), F32),
            pltpu.SemaphoreType.DMA((2,)),
            pltpu.SemaphoreType.DMA((2, hops)),
            pltpu.SemaphoreType.DMA((2, hops)),
        ],
        compiler_params=pltpu.CompilerParams(
            collective_id=2, has_side_effects=True, vmem_limit_bytes=28 << 20
        ),
        name="run_stops",
    )(queries, packed, entities)


def add_into(dst, *others):
    lead, size = [], dst.size
    for n in dst.shape[:-2]:
        if size <= 1 << 15:
            break
        lead.append(n)
        size //= n
    total = 1
    for n in lead:
        total *= n

    def body(i, carry):
        index, rest = [], i
        for n in reversed(lead):
            index.insert(0, lax.rem(rest, n))
            rest = rest // n
        index = tuple(index) if index else ...
        value = dst[index].astype(F32)
        for other in others:
            value = value + other[index].astype(F32)
        dst[index] = value.astype(dst.dtype)
        return carry

    if total == 1:
        body(0, 0)
    else:
        lax.fori_loop(0, total, body, 0)


ORDERS = (("xyz", "yxz", "zxy", "xyz"), ("yxz", "xyz", "zyx", "yxz"))
SIZES = {"zh": 2, "x": 4, "zl": 2, "y": 4}
OF_AXIS = {"x": ("x",), "y": ("y",), "z": ("zh", "zl")}


def piece_shape(order, phase, rows, columns):
    gone = [name for axis in order[: phase + 1] for name in OF_AXIS[axis]]
    free = [n for name, n in SIZES.items() if name not in gone]
    if free:
        return (free[0] // 2, *free[1:], rows, columns), (*free, rows, columns)
    return (rows, columns // 2), (rows, columns)


def landing_shapes(order, rows, columns):
    shapes = []
    for phase in range(3):
        half, whole = piece_shape(order, phase, rows, columns)
        shapes += [(2, *half), (2, *whole)]
    return shapes


class Eighth:
    def __init__(self, mail, at, base, row, column, order, landings, ways):
        self.mail, self.at, self.base, self.order, self.landings, self.ways = mail, at, base, order, landings, ways
        self.row, self.column = row, column
        self.fixed, self.phase = {}, 0

    def view(self, fixed, cut=None):
        index = []
        free = [name for name in SIZES if name not in fixed]
        for name, n in SIZES.items():
            if name in fixed:
                index.append(fixed[name])
            elif cut is not None and name == free[0]:
                index.append(pl.ds(cut * (n // 2), n // 2))
            else:
                index.append(slice(None))
        start, size = self.column
        if cut is not None and not free:
            start, size = start + cut * (size // 2), size // 2
        return self.base.at[(*index, pl.ds(*self.row), pl.ds(start, size))]

    def spot(self, by):
        axis = self.order[self.phase]
        t = turn(getattr(self.at, axis), by)
        return {**self.fixed, **({"zh": t // 2, "zl": lax.rem(t, 2)} if axis == "z" else {axis: t})}

    def one(self):
        self.half, self.whole = self.landings[2 * self.phase : 2 * self.phase + 2]
        self.devices = self.ways[self.order[self.phase]]
        self.h = [
            self.mail.send(self.view(self.spot(2), d), self.half.at[d], device)
            for d, device in enumerate(self.devices)
        ]

    def two(self):
        self.f = []
        for d, device in enumerate(self.devices):
            self.h[d].wait_recv()
            target = self.spot((1, 3)[d])
            add_into(self.view(target, d), self.half.at[d])
            self.f.append(self.mail.send(self.view(target), self.whole.at[d], device))

    def three(self):
        for copy in self.f:
            copy.wait_recv()
        self.fixed = self.spot(0)
        self.phase += 1
        if self.phase < 3:
            add_into(self.view(self.fixed), self.whole.at[0], self.whole.at[1])
            self.one()

    def result(self):
        own = self.view(self.fixed)[...].astype(F32)
        return own + self.whole[0].astype(F32) + self.whole[1].astype(F32)


def scatter_kernel(place, terms, back, out, source_grad, got, *rest):
    swap_send, swap_recv, send_sem, recv_sem = rest[-4:]
    landings = rest[:-4]
    at = Spot()
    mail = Mail(send_sem, recv_sem)
    partner = at.device(core=1 - at.core)
    ways = {
        "x": (at.device(x=turn(at.x, 1)), at.device(x=turn(at.x, 3))),
        "y": (at.device(y=turn(at.y, 1)), at.device(y=turn(at.y, 3))),
        "z": (at.device(z=turn(at.z, 1)), at.device(z=turn(at.z, 3))),
    }
    greet([partner, *ways["x"], *ways["y"], *ways["z"]])

    def swap(j, r):
        zh, x = r // 4, lax.rem(r, 4)
        return pltpu.make_async_remote_copy(
            src_ref=terms.at[j, zh, x, :, :, 1 - at.core],
            dst_ref=got.at[j, zh, x],
            send_sem=swap_send.at[j, r],
            recv_sem=swap_recv.at[j, r],
            device_id=partner,
            device_id_type=MESH,
        )

    def offer(i, carry):
        swap(i // 8, lax.rem(i, 8)).start()
        return carry

    lax.fori_loop(0, 16, offer, 0)

    def joined(j):
        def one(r, carry):
            swap(j, r).wait_recv()
            zh, x = r // 4, lax.rem(r, 4)
            add_into(got.at[j, zh, x], terms.at[j, zh, x, :, :, at.core])
            return carry

        lax.fori_loop(0, 8, one, 0)

    def unsort(begin, end):
        lanes = 128
        total = place.shape[1]

        def one(b, carry):
            here = pl.ds(pl.multiple_of(b * lanes, lanes), lanes)
            mine = jnp.broadcast_to(place[:, here], (lanes, lanes)).T
            index = lax.broadcasted_iota(jnp.int32, (lanes, lanes), 1)
            choose = jnp.concatenate(
                [(mine == index + t * lanes).astype(F32).astype(BF) for t in range(total // lanes)], axis=1
            )
            source_grad[here, :] = jnp.dot(choose, back[0:total, :], preferred_element_type=F32).astype(BF)
            return carry

        lax.fori_loop(begin, end, one, 0)


    rows, columns = got.shape[-2] // 2, got.shape[-1] // 2
    units = [
        [
            Eighth(
                mail, at, got.at[j], (u // 2 * rows, rows), (u % 2 * columns, columns), ORDERS[j][u],
                landings[(4 * j + u) * 6 : (4 * j + u) * 6 + 6], ways,
            )
            for u in range(4)
        ]
        for j in range(2)
    ]
    every = [unit for group in units for unit in group]
    for j in range(2):
        joined(j)
        for unit in units[j]:
            unit.one()
    unsort(0, 4)
    for phase in range(3):
        for u, unit in enumerate(every):
            unit.two()
            if u % 4 == 3:
                unsort(4 + 4 * phase + u // 4, 5 + 4 * phase + u // 4)
        for u, unit in enumerate(every):
            unit.three()
            if u % 4 == 3:
                unsort(6 + 4 * phase + u // 4, 7 + 4 * phase + u // 4)
    for j in range(2):
        for u, unit in enumerate(units[j]):
            out[unit.row[0] : unit.row[0] + rows, j, unit.column[0] : unit.column[0] + columns] = unit.result()

    def sent(i, carry):
        swap(i // 8, lax.rem(i, 8)).wait_send()
        return carry

    lax.fori_loop(0, 16, sent, 0)
    mail.drain()


def scatter_grads(place, terms, back):
    width = back.shape[1]
    total = place.shape[1]
    rows = width // 16
    terms = terms.reshape(2, 2, 4, 2, 4, 2, rows, width)
    v = lambda *lead: pltpu.VMEM((*lead, rows, width), BF)
    vmem = pl.BlockSpec(memory_space=pltpu.VMEM)
    return pl.pallas_call(
        scatter_kernel,
        out_shape=(jax.ShapeDtypeStruct((rows, 2, width), F32), jax.ShapeDtypeStruct((total, width), BF)),
        in_specs=[vmem, vmem, vmem],
        out_specs=(vmem, vmem),
        scratch_shapes=[
            v(2, 2, 4, 2, 4),
            *(
                pltpu.VMEM(shape, BF)
                for group in ORDERS
                for order in group
                for shape in landing_shapes(order, rows // 2, width // 2)
            ),
            pltpu.SemaphoreType.DMA((2, 8)),
            pltpu.SemaphoreType.DMA((2, 8)),
            pltpu.SemaphoreType.DMA((96,)),
            pltpu.SemaphoreType.DMA((96,)),
        ],
        compiler_params=pltpu.CompilerParams(
            collective_id=1, has_side_effects=True, vmem_limit_bytes=30 << 20
        ),
        name="scatter_grads",
    )(place, terms, back)


def shards(source_rows, rel_ids, relations, entities, pos_slot, negatives):
    rows = source_rows.shape[0]
    matrices, sorted_rows, packed, place, starts = gather_relations(
        relations,
        rel_ids.reshape(1, rows),
        source_rows,
        jnp.transpose(negatives, (0, 2, 1)),
        pos_slot.reshape(1, rows),
    )
    queries = make_queries(starts, sorted_rows, matrices)
    state, query_grad = run_stops(queries, packed, entities)
    back, terms, state = make_grads(starts, sorted_rows, query_grad, matrices, state)
    relation_grad, source_grad = scatter_grads(place, terms, back)
    return (state, source_grad, relation_grad)


def solution(mesh):
    placed = (
        P(("cand", "rel"), None),
        P(("cand", "rel"), None),
        P("rel", None, None),
        P(("cand", "rel"), None),
        P(("cand", "rel")),
        P(None, ("cand", "rel"), None),
    )
    return jax.shard_map(
        shards,
        mesh=mesh,
        in_specs=placed,
        out_specs=(P(("cand", "rel"), None), P(("cand", "rel"), None), P("cand", "rel", None)),
        check_vma=False,
    )
```

```python
import functools

import jax
import jax.numpy as jnp
from jax import lax
from jax.experimental import pallas as pl
from jax.experimental.pallas import tpu as pltpu
from jax.sharding import PartitionSpec as P

MESH = pl.DeviceIdType.MESH
BF = jnp.bfloat16
F32 = jnp.float32


class Spot:
    def __init__(self):
        cand, rel = lax.axis_index("cand"), lax.axis_index("rel")
        self.core = lax.rem(cand, 2)
        self.y = lax.rem(cand // 2, 4)
        self.zl = cand // 8
        self.x = lax.rem(rel, 4)
        self.zh = rel // 4
        self.z = self.zh * 2 + self.zl
        self.rel = rel

    def device(self, x=None, y=None, z=None, core=None):
        x = self.x if x is None else x
        y = self.y if y is None else y
        z = self.z if z is None else z
        core = self.core if core is None else core
        return ((lax.rem(z, 2) * 4 + y) * 2 + core, (z // 2) * 4 + x)


def turn(i, by):
    return lax.rem(i + by, 4)


def greet(devices):
    barrier = pltpu.get_barrier_semaphore()
    for device in devices:
        pl.semaphore_signal(barrier, inc=1, device_id=device, device_id_type=MESH)
    pl.semaphore_wait(barrier, len(devices))


class Mail:
    def __init__(self, send_sem, recv_sem):
        self.send_sem, self.recv_sem, self.count, self.sent = send_sem, recv_sem, 0, []

    def send(self, src, dst, device):
        i = self.count
        self.count += 1
        copy = pltpu.make_async_remote_copy(
            src_ref=src,
            dst_ref=dst,
            send_sem=self.send_sem.at[i],
            recv_sem=self.recv_sem.at[i],
            device_id=device,
            device_id_type=MESH,
        )
        copy.start()
        self.sent.append(copy)
        return copy

    def drain(self):
        for copy in self.sent:
            copy.wait_send()


WINDOW_PAD = 16


def sort_plan(ids, nrel):
    rows = ids.shape[1]
    block = 256
    named = (jnp.broadcast_to(ids, (nrel, rows)) == lax.broadcasted_iota(jnp.int32, (nrel, rows), 0)).astype(F32)
    before = (
        lax.broadcasted_iota(jnp.int32, (block, block), 0) < lax.broadcasted_iota(jnp.int32, (block, block), 1)
    ).astype(BF)
    running = jnp.zeros((nrel, 1), F32)
    ranks = []
    for b in range(rows // block):
        part = named[:, b * block : (b + 1) * block]
        ranks.append(jnp.dot(part.astype(BF), before, preferred_element_type=F32) + running)
        running = running + jnp.sum(part, axis=1, keepdims=True)
    rank = jnp.concatenate(ranks, axis=1)
    lower = (
        lax.broadcasted_iota(jnp.int32, (nrel, nrel), 1) < lax.broadcasted_iota(jnp.int32, (nrel, nrel), 0)
    ).astype(BF)
    starts = jnp.dot(lower, jnp.broadcast_to(running, (nrel, 128)).astype(BF), preferred_element_type=F32)
    place = jnp.sum(named * (rank + starts[:, 0:1]), axis=0, keepdims=True)
    return place, starts


def sort_rows(b, place, rows_ref, meta_ref, rows_out, picks_out, pos_out, part):
    rows = place.shape[1]
    block = 256
    here = pl.ds(b * block, block)
    spot = lax.broadcasted_iota(jnp.int32, (block, rows), 0) + b * block
    choose = (jnp.broadcast_to(place, (block, rows)) == spot).astype(F32).astype(BF)
    rows_out[here, :] = jnp.dot(choose, rows_ref[...], preferred_element_type=F32).astype(BF)
    meta = lax.dot_general(
        meta_ref[...], choose, (((1,), (1,)), ((), ())), preferred_element_type=F32
    ).astype(jnp.int32)
    named = picks_out.shape[0]
    picks_out[:, here] = meta[0:named]
    pos_out[:, here] = meta[named : named + 1] * part + meta[named + 1 : named + 2]


TOGETHER = 4


def group_queries(starts, rows_ref, matrix, out):
    for r in range(TOGETHER):
        window, inside = out_window(starts, TOGETHER * pl.program_id(0) + r)
        new = jnp.dot(rows_ref[window, :], matrix[r], preferred_element_type=F32).astype(BF)
        out[window, :] = jnp.where(inside, new, out[window, :])


def out_window(starts, k):
    size = 256 + WINDOW_PAD
    start, end = starts[k], starts[k + 1]
    base = pl.multiple_of(start // WINDOW_PAD * WINDOW_PAD, WINDOW_PAD)
    row = lax.broadcasted_iota(jnp.int32, (size, 512), 0) + base
    return pl.ds(base, size), (row >= start) & (row < end)


def make_queries(starts, rows, matrices):
    nrel, width, _ = matrices.shape
    return pl.pallas_call(
        group_queries,
        out_shape=jax.ShapeDtypeStruct(rows.shape, BF),
        grid_spec=pltpu.PrefetchScalarGridSpec(
            num_scalar_prefetch=1,
            grid=(nrel // TOGETHER,),
            in_specs=[
                pl.BlockSpec(rows.shape, lambda k, s: (0, 0)),
                pl.BlockSpec((TOGETHER, width, width), lambda k, s: (k, 0, 0)),
            ],
            out_specs=pl.BlockSpec(rows.shape, lambda k, s: (0, 0)),
        ),
        compiler_params=pltpu.CompilerParams(vmem_limit_bytes=16 << 20),
        name="make_queries",
    )(starts, rows, matrices)


PAIR = 2


def group_grads(starts, rows_ref, grads, matrix, state, back, terms, state_out, sem):
    step = pl.program_id(0)
    keep = pltpu.make_async_copy(state, state_out, sem)

    @pl.when(step == 0)
    def _():
        keep.start()

    for r in range(PAIR):
        window, inside = out_window(starts, PAIR * step + r)
        grad = grads[window, :]
        rows = rows_ref[window, :]
        rows = jnp.where(inside, rows, jnp.zeros_like(rows))
        terms[r, 0] = lax.dot_general(rows, grad, (((0,), (0,)), ((), ())), preferred_element_type=F32).astype(BF)
        new = lax.dot_general(grad, matrix[r], (((1,), (1,)), ((), ())), preferred_element_type=F32).astype(BF)
        back[window, :] = jnp.where(inside, new, back[window, :])

    @pl.when(step == pl.num_programs(0) - 1)
    def _():
        keep.wait()


def make_grads(starts, rows, grads, matrices, state):
    nrel, width, _ = matrices.shape
    whole = pl.BlockSpec(grads.shape, lambda k, s: (0, 0))
    return pl.pallas_call(
        group_grads,
        out_shape=(
            jax.ShapeDtypeStruct(grads.shape, BF),
            jax.ShapeDtypeStruct((2, nrel // 2, width, width), BF),
            jax.ShapeDtypeStruct(state.shape, F32),
        ),
        grid_spec=pltpu.PrefetchScalarGridSpec(
            num_scalar_prefetch=1,
            grid=(nrel // PAIR,),
            in_specs=[
                whole,
                whole,
                pl.BlockSpec((PAIR, width, width), lambda k, s: (k, 0, 0)),
                pl.BlockSpec(memory_space=pl.ANY),
            ],
            out_specs=(
                whole,
                pl.BlockSpec((PAIR, 1, width, width), lambda k, s: (0, k, 0, 0)),
                pl.BlockSpec(memory_space=pl.ANY),
            ),
            scratch_shapes=[pltpu.SemaphoreType.DMA],
        ),
        compiler_params=pltpu.CompilerParams(vmem_limit_bytes=16 << 20),
        name="make_grads",
    )(starts, rows, grads, matrices, state)


LOW = 64


def tally(stop, part, picks, pos, low, unit, packed):
    samples = 16
    rows = pos.shape[1]
    lanes = 128
    names = picks[pl.ds(pl.multiple_of(stop * samples, samples), samples), :]
    low[0:samples, :] = lax.bitwise_and(names, LOW - 1)
    unit[0:samples, :] = lax.shift_left(jnp.ones_like(names), 8 * lax.shift_right_logical(names, 6))
    place = pos[...] - stop * part
    inside = (place >= 0) & (place < part)
    place = jnp.where(inside, place, 0)
    low[samples : samples + 1, :] = lax.bitwise_and(place, LOW - 1)
    unit[samples : samples + 1, :] = jnp.where(
        inside, lax.shift_left(jnp.full_like(place, 33), 8 * lax.shift_right_logical(place, 6)), 0
    )

    def column(c, carry):
        here = pl.ds(pl.multiple_of(c * lanes, lanes), lanes)
        index = lax.broadcasted_iota(jnp.int32, (LOW, lanes), 0)
        total = jnp.zeros((LOW, lanes), jnp.int32)
        for k in range(samples + 1):
            match = jnp.broadcast_to(low[k : k + 1, here], (LOW, lanes)) == index
            total = total + jnp.where(match, jnp.broadcast_to(unit[k : k + 1, here], (LOW, lanes)), 0)
        packed[stop, :, here] = total
        return carry

    lax.fori_loop(0, rows // lanes, column, 0)


def gather_kernel(
    own_in, ids_in, rows_in, picks_in, target_in, out, rows_out, packed, place_out, starts_out,
    own, ids, rows_ref, picks, target,
    meta, sorted_picks, sorted_target, low, unit, local_sem, fetch_sem, send_sem, recv_sem,
):
    at = Spot()
    mail = Mail(send_sem, recv_sem)
    left, right = at.device(x=turn(at.x, 3)), at.device(x=turn(at.x, 1))
    down, up = at.device(y=turn(at.y, 3)), at.device(y=turn(at.y, 1))
    across = at.device(z=3 - at.z)
    partner = at.device(core=1 - at.core)
    fetch = [
        pltpu.make_async_copy(source, landing, fetch_sem.at[i])
        for i, (source, landing) in enumerate(
            ((own_in, own), (ids_in, ids), (target_in, target), (picks_in, picks), (rows_in, rows_ref))
        )
    ]
    for copy in fetch:
        copy.start()
    greet([left, right, down, up, across, partner])
    fetch[0].wait()
    half = own.shape[1] // 2
    share = half // 4

    def rows(start, size, step):
        return pl.ds(pl.multiple_of(start, step), size)

    start = at.core * half
    mine, first, second = rows(start, half, half), rows(start, half // 2, half), rows(start + half // 2, half // 2, half // 2)

    def quarter(y):
        return rows(start + y * share, share, share)

    def quarter_halves(y):
        return (
            rows(start + y * share, share // 2, share),
            rows(start + y * share + share // 2, share // 2, share // 2),
        )

    me, far = at.zh * 4, (1 - at.zh) * 4
    x0, x1, x2, x3 = at.x, turn(at.x, 1), turn(at.x, 2), turn(at.x, 3)
    y0, y1, y2, y3 = at.y, turn(at.y, 1), turn(at.y, 2), turn(at.y, 3)
    here = pltpu.make_async_copy(own, out.at[at.rel], local_sem)
    here.start()

    def same(ref, device):
        return mail.send(ref, ref, device)

    def a(base, x, rows):
        return out.at[base + x, 0, rows]

    def b(base, x, rows):
        return out.at[base + x, 1, rows]

    gifts = []

    class Quarter:
        def __init__(self, base, x):
            self.base, self.x = base, x
            self.sent = [same(b(base, x, quarter(y0)), device) for device in (up, down)]

        def on(self):
            self.sent[0].wait_recv()
            first = same(b(self.base, self.x, quarter_halves(y3)[0]), up)
            self.sent[1].wait_recv()
            self.sent = [first, same(b(self.base, self.x, quarter_halves(y1)[1]), down)]

        def done(self):
            for copy in self.sent:
                copy.wait_recv()
            gifts.append(same(b(self.base, self.x, mine), partner))

    own_a, own_b = own.at[0, mine], own.at[1, quarter(y0)]
    b_across = mail.send(own_b, b(me, x0, quarter(y0)), across)
    b_right = mail.send(own_b, b(me, x0, quarter(y0)), right)
    b_left = mail.send(own_b, b(me, x0, quarter(y0)), left)
    a_across = mail.send(own_a, a(me, x0, mine), across)
    a_right = mail.send(own_a, a(me, x0, mine), right)
    a_left = mail.send(own_a, a(me, x0, mine), left)

    stops, samples, total = picks.shape
    part = total // stops
    nrel = starts_out.shape[0]
    for copy in fetch[1:]:
        copy.wait()
    place, starts = sort_plan(ids[...], nrel)
    place = place.astype(jnp.int32)
    place_out[...] = place
    starts_out[...] = starts.astype(jnp.int32)
    for s in range(stops):
        meta[s * samples : (s + 1) * samples, :] = picks[s].astype(F32).astype(BF)
    goal = target[...]
    tail = lax.broadcasted_iota(jnp.int32, (16, total), 0)
    meta[stops * samples :, :] = jnp.where(
        tail == 0, jnp.broadcast_to(goal // part, (16, total)), jnp.broadcast_to(lax.rem(goal, part), (16, total))
    ).astype(F32).astype(BF)
    rows_out[total:, :] = jnp.zeros((rows_out.shape[0] - total, rows_out.shape[1]), BF)

    def work(b):
        sort_rows(b, place_out[...], rows_ref, meta, rows_out, sorted_picks, sorted_target, part)

    def count(s):
        tally(s, part, sorted_picks, sorted_target, low, unit, packed)

    h0, h1 = quarter_halves(y0)
    work(0)
    b_right.wait_recv()
    b_on_right = same(b(me, x3, h0), right)
    q_me3 = Quarter(me, x3)
    b_left.wait_recv()
    b_on_left = same(b(me, x1, h1), left)
    q_me1 = Quarter(me, x1)
    b_across.wait_recv()
    b_far_right = same(b(far, x0, quarter(y0)), right)
    b_far_left = same(b(far, x0, quarter(y0)), left)
    q_far0 = Quarter(far, x0)
    work(1)
    a_right.wait_recv()
    a_on_right = same(a(me, x3, first), right)
    gifts.append(same(a(me, x3, mine), partner))
    a_left.wait_recv()
    a_on_left = same(a(me, x1, second), left)
    gifts.append(same(a(me, x1, mine), partner))
    b_on_right.wait_recv()
    b_on_left.wait_recv()
    q_me2 = Quarter(me, x2)
    work(2)
    b_far_right.wait_recv()
    b_far_on_right = same(b(far, x3, h0), right)
    q_far3 = Quarter(far, x3)
    b_far_left.wait_recv()
    b_far_on_left = same(b(far, x1, h1), left)
    q_far1 = Quarter(far, x1)
    a_across.wait_recv()
    a_far_right = same(a(far, x0, mine), right)
    a_far_left = same(a(far, x0, mine), left)
    gifts.append(same(a(far, x0, mine), partner))
    work(3)
    q_me3.on()
    q_me1.on()
    work(4)
    q_far0.on()
    a_on_right.wait_recv()
    a_opposite = [same(a(me, x2, first), across)]
    a_on_left.wait_recv()
    a_opposite.append(same(a(me, x2, second), across))
    gifts.append(same(a(me, x2, mine), partner))
    b_far_on_right.wait_recv()
    b_far_on_left.wait_recv()
    q_far2 = Quarter(far, x2)
    work(5)
    q_me2.on()
    q_me3.done()
    work(6)
    q_far3.on()
    q_me1.done()
    work(7)
    q_far1.on()
    q_far0.done()
    count(0)
    q_far2.on()
    q_me2.done()
    count(1)
    a_far_right.wait_recv()
    gifts.append(same(a(far, x3, mine), partner))
    a_far_left.wait_recv()
    gifts.append(same(a(far, x1, mine), partner))
    q_far3.done()
    count(2)
    for copy in a_opposite:
        copy.wait_recv()
    gifts.append(same(a(far, x2, mine), partner))
    q_far1.done()
    q_far2.done()
    count(3)
    count(4)

    def later(s, carry):
        count(s)
        return carry

    lax.fori_loop(5, stops, later, 0)
    for copy in gifts:
        copy.wait_recv()
    mail.drain()
    here.wait()


def gather_relations(relations, ids, rows, picks, target):
    per, width, _ = relations.shape
    owners = lax.axis_size("rel")
    nrel = owners * per
    stops, samples, total = picks.shape
    vmem = pl.BlockSpec(memory_space=pltpu.VMEM)
    out = pl.pallas_call(
        gather_kernel,
        out_shape=(
            jax.ShapeDtypeStruct((owners, per, width, width), relations.dtype),
            jax.ShapeDtypeStruct((total + 256 + WINDOW_PAD, width), BF),
            jax.ShapeDtypeStruct((stops, LOW, total), jnp.int32),
            jax.ShapeDtypeStruct((1, total), jnp.int32),
            jax.ShapeDtypeStruct((nrel, 128), jnp.int32),
        ),
        in_specs=[pl.BlockSpec(memory_space=pltpu.HBM)] * 5,
        out_specs=(pl.BlockSpec(memory_space=pl.ANY), *[vmem] * 4),
        scratch_shapes=[
            *(pltpu.VMEM(a.shape, a.dtype) for a in (relations, ids, rows, picks, target)),
            pltpu.VMEM((stops * samples + 16, total), BF),
            pltpu.VMEM((stops * samples, total), jnp.int32),
            pltpu.VMEM((1, total), jnp.int32),
            pltpu.VMEM((24, total), jnp.int32),
            pltpu.VMEM((24, total), jnp.int32),
            pltpu.SemaphoreType.DMA,
            pltpu.SemaphoreType.DMA((5,)),
            pltpu.SemaphoreType.DMA((60,)),
            pltpu.SemaphoreType.DMA((60,)),
        ],
        compiler_params=pltpu.CompilerParams(
            collective_id=0, has_side_effects=True, vmem_limit_bytes=24 << 20
        ),
        name="gather_relations",
    )(*(pltpu.with_memory_space_constraint(v, pltpu.HBM) for v in (relations, ids, rows, picks, target)))
    matrices, rows, packed, place, starts = out
    starts = jnp.concatenate([starts[:, 0], jnp.full((1,), total, jnp.int32)])
    return matrices.reshape(nrel, width, width), rows, packed, place, starts


STOPS = 8
learn_rate = 0.005
LOG2E = 1.4426950408889634


def stops_kernel(
    q, packed, entities, state_out, grad_out, held, sent, held_short, sent_short, now, wide, turned_wide, weights, acc,
    local_sem, send_sem, recv_sem,
):
    cand, rel = lax.axis_index("cand"), lax.axis_index("rel")
    n = lax.axis_size("cand")
    ahead, behind = (lax.rem(cand + 1, n), rel), (lax.rem(cand + n - 1, n), rel)
    greet([ahead, behind])
    part, width = entities.shape
    rows = packed.shape[2]
    chunk = part // 2
    block = 256

    fetch = [
        pltpu.make_async_copy(entities.at[pl.ds(h * chunk, chunk)], held.at[h], local_sem.at[h])
        for h in range(2)
    ]
    for copy in fetch:
        copy.start()
    acc[...] = jnp.zeros_like(acc)
    for copy in fetch:
        copy.wait()

    def copier(kind, source, landing):
        return lambda t: pltpu.make_async_remote_copy(
            src_ref=source.at[t],
            dst_ref=landing.at[t + 2],
            send_sem=send_sem.at[kind, t],
            recv_sem=recv_sem.at[kind, t],
            device_id=ahead,
            device_id_type=MESH,
        )

    core = lax.rem(cand, 2)
    hop, hop_short = copier(0, sent, held), copier(1, sent_short, held_short)

    def step(t, carry):
        half = lax.rem(t, 2)
        stop = t // 2
        here_rows = pl.ds(pl.multiple_of(half * chunk, chunk), chunk)

        @pl.when(t < 2)
        def _():
            now[...] = held[t]

        @pl.when((t >= 2) & (core == 1))
        def _():
            hop(t - 2).wait_recv()
            now[...] = held[t]

        @pl.when((t >= 2) & (core == 0))
        def _():
            hop_short(t - 2).wait_recv()
            now[...] = held_short[t].astype(F32)

        rounded = now[...].astype(BF)
        wide[here_rows, :] = rounded
        pieces = []
        for i in range(rows // block):
            here = pl.ds(i * block, block)
            logits = lax.dot_general(
                rounded, q[here, :], (((1,), (1,)), ((), ())), preferred_element_type=F32
            )
            marks = packed[stop, :, here]
            marks = jnp.concatenate(
                [lax.shift_right_logical(marks, 16 * half + 8 * p) for p in range(chunk // LOW)], axis=0
            )
            named = lax.bitwise_and(marks, 31).astype(F32)
            chance = 1.0 / (1.0 + jnp.exp2(logits * -LOG2E))
            product = named * chance
            pieces.append(jnp.where(lax.bitwise_and(marks, 32) != 0, product - 1.0, product).astype(BF))
        weight = jnp.concatenate(pieces, axis=1)
        weights[here_rows, :] = weight
        change = jnp.dot(weight, q[0:rows, :], preferred_element_type=F32)
        moved = now[...] - learn_rate * change
        sent[t] = moved
        sent_short[t] = moved.astype(BF)

        @pl.when((t < 2 * STOPS - 2) & (core == 0))
        def _():
            hop(t).start()

        @pl.when((t < 2 * STOPS - 2) & (core == 1))
        def _():
            hop_short(t).start()

        @pl.when(half == 1)
        def _():
            turned_wide[...] = wide[...].astype(F32).T.astype(BF)
            big = 512

            def gather(c, carry):
                here = pl.ds(pl.multiple_of(c * big, big), big)
                acc[:, here] += jnp.dot(turned_wide[...], weights[:, here], preferred_element_type=F32)
                return carry

            lax.fori_loop(0, rows // big, gather, 0, unroll=True)

        return carry

    lax.fori_loop(0, 2 * STOPS, step, 0)
    for h in range(2):
        state_out[pl.ds(h * chunk, chunk), :] = sent[2 * STOPS - 2 + h]

    def turned(c, carry):
        here = pl.ds(pl.multiple_of(c * block, block), block)
        grad_out[here, :] = acc[:, here].T.astype(BF)
        return carry

    lax.fori_loop(0, rows // block, turned, 0)
    grad_out[rows:, :] = jnp.zeros((grad_out.shape[0] - rows, width), BF)

    def drained(t, carry):
        @pl.when(core == 0)
        def _():
            hop(t).wait_send()

        @pl.when(core == 1)
        def _():
            hop_short(t).wait_send()

        return carry

    lax.fori_loop(0, 2 * STOPS - 2, drained, 0)


def run_stops(queries, packed, entities):
    padded, width = queries.shape
    rows = packed.shape[2]
    part = entities.shape[0]
    chunk = part // 2
    vmem = pl.BlockSpec(memory_space=pltpu.VMEM)
    hops = 2 * STOPS
    return pl.pallas_call(
        stops_kernel,
        out_shape=(
            jax.ShapeDtypeStruct((part, width), F32),
            jax.ShapeDtypeStruct((padded, width), BF),
        ),
        in_specs=[vmem, vmem, pl.BlockSpec(memory_space=pltpu.HBM)],
        out_specs=(vmem, vmem),
        scratch_shapes=[
            pltpu.VMEM((hops, chunk, width), F32),
            pltpu.VMEM((hops, chunk, width), F32),
            pltpu.VMEM((hops, chunk, width), BF),
            pltpu.VMEM((hops, chunk, width), BF),
            pltpu.VMEM((chunk, width), F32),
            pltpu.VMEM((part, width), BF),
            pltpu.VMEM((width, part), BF),
            pltpu.VMEM((part, rows), BF),
            pltpu.VMEM((width, rows), F32),
            pltpu.SemaphoreType.DMA((2,)),
            pltpu.SemaphoreType.DMA((2, hops)),
            pltpu.SemaphoreType.DMA((2, hops)),
        ],
        compiler_params=pltpu.CompilerParams(
            collective_id=2, has_side_effects=True, vmem_limit_bytes=28 << 20
        ),
        name="run_stops",
    )(queries, packed, entities)


def add_into(dst, *others):
    lead, size = [], dst.size
    for n in dst.shape[:-2]:
        if size <= 1 << 15:
            break
        lead.append(n)
        size //= n
    total = 1
    for n in lead:
        total *= n

    def body(i, carry):
        index, rest = [], i
        for n in reversed(lead):
            index.insert(0, lax.rem(rest, n))
            rest = rest // n
        index = tuple(index) if index else ...
        value = dst[index].astype(F32)
        for other in others:
            value = value + other[index].astype(F32)
        dst[index] = value.astype(dst.dtype)
        return carry

    if total == 1:
        body(0, 0)
    else:
        lax.fori_loop(0, total, body, 0)


ORDERS = (("xyz", "yxz", "zxy", "xyz"), ("yxz", "xyz", "zyx", "yxz"))
SIZES = {"zh": 2, "x": 4, "zl": 2, "y": 4}
OF_AXIS = {"x": ("x",), "y": ("y",), "z": ("zh", "zl")}


def piece_shape(order, phase, rows, columns):
    gone = [name for axis in order[: phase + 1] for name in OF_AXIS[axis]]
    free = [n for name, n in SIZES.items() if name not in gone]
    if free:
        return (free[0] // 2, *free[1:], rows, columns), (*free, rows, columns)
    return (rows, columns // 2), (rows, columns)


def landing_shapes(order, rows, columns):
    shapes = []
    for phase in range(3):
        half, whole = piece_shape(order, phase, rows, columns)
        shapes += [(2, *half), (2, *whole)] if phase < 2 else [(3, *whole)]
    return shapes


class Eighth:
    def __init__(self, mail, at, base, row, column, order, landings, ways):
        self.mail, self.at, self.base, self.order, self.landings, self.ways = mail, at, base, order, landings, ways
        self.row, self.column = row, column
        self.fixed, self.phase = {}, 0

    def view(self, fixed, cut=None):
        index = []
        free = [name for name in SIZES if name not in fixed]
        for name, n in SIZES.items():
            if name in fixed:
                index.append(fixed[name])
            elif cut is not None and name == free[0]:
                index.append(pl.ds(cut * (n // 2), n // 2))
            else:
                index.append(slice(None))
        start, size = self.column
        if cut is not None and not free:
            start, size = start + cut * (size // 2), size // 2
        return self.base.at[(*index, pl.ds(*self.row), pl.ds(start, size))]

    def spot(self, by):
        axis = self.order[self.phase]
        t = turn(getattr(self.at, axis), by)
        return {**self.fixed, **({"zh": t // 2, "zl": lax.rem(t, 2)} if axis == "z" else {axis: t})}

    def straight(self):
        self.whole = self.landings[-1]
        self.f = [
            self.mail.send(self.view(self.spot(by)), self.whole.at[i], device)
            for i, (by, device) in enumerate(zip((1, 3, 2), self.ways[self.order[2]]))
        ]

    def one(self):
        if self.phase == 2:
            return self.straight()
        self.half, self.whole = self.landings[2 * self.phase : 2 * self.phase + 2]
        self.devices = self.ways[self.order[self.phase]][:2]
        self.h = [
            self.mail.send(self.view(self.spot(2), d), self.half.at[d], device)
            for d, device in enumerate(self.devices)
        ]

    def two(self):
        if self.phase == 2:
            return
        self.f = []
        for d, device in enumerate(self.devices):
            self.h[d].wait_recv()
            target = self.spot((1, 3)[d])
            add_into(self.view(target, d), self.half.at[d])
            self.f.append(self.mail.send(self.view(target), self.whole.at[d], device))

    def three(self):
        for copy in self.f:
            copy.wait_recv()
        self.fixed = self.spot(0)
        self.phase += 1
        if self.phase < 3:
            add_into(self.view(self.fixed), self.whole.at[0], self.whole.at[1])
            self.one()

    def result(self):
        own = self.view(self.fixed)[...].astype(F32)
        return own + self.whole[0].astype(F32) + self.whole[1].astype(F32) + self.whole[2].astype(F32)


def scatter_kernel(place, terms, back, out, source_grad, got, *rest):
    swap_send, swap_recv, send_sem, recv_sem = rest[-4:]
    landings = rest[:-4]
    at = Spot()
    mail = Mail(send_sem, recv_sem)
    partner = at.device(core=1 - at.core)
    ways = {
        "x": tuple(at.device(x=turn(at.x, by)) for by in (1, 3, 2)),
        "y": tuple(at.device(y=turn(at.y, by)) for by in (1, 3, 2)),
        "z": tuple(at.device(z=turn(at.z, by)) for by in (1, 3, 2)),
    }
    greet([partner, *ways["x"], *ways["y"], *ways["z"]])

    def swap(j, r):
        zh, x = r // 4, lax.rem(r, 4)
        return pltpu.make_async_remote_copy(
            src_ref=terms.at[j, zh, x, :, :, 1 - at.core],
            dst_ref=got.at[j, zh, x],
            send_sem=swap_send.at[j, r],
            recv_sem=swap_recv.at[j, r],
            device_id=partner,
            device_id_type=MESH,
        )

    def offer(i, carry):
        swap(i // 8, lax.rem(i, 8)).start()
        return carry

    lax.fori_loop(0, 16, offer, 0)

    def joined(j):
        def one(r, carry):
            swap(j, r).wait_recv()
            zh, x = r // 4, lax.rem(r, 4)
            add_into(got.at[j, zh, x], terms.at[j, zh, x, :, :, at.core])
            return carry

        lax.fori_loop(0, 8, one, 0)

    def unsort(begin, end):
        lanes = 128
        total = place.shape[1]

        def one(b, carry):
            here = pl.ds(pl.multiple_of(b * lanes, lanes), lanes)
            mine = jnp.broadcast_to(place[:, here], (lanes, lanes)).T
            index = lax.broadcasted_iota(jnp.int32, (lanes, lanes), 1)
            choose = jnp.concatenate(
                [(mine == index + t * lanes).astype(F32).astype(BF) for t in range(total // lanes)], axis=1
            )
            source_grad[here, :] = jnp.dot(choose, back[0:total, :], preferred_element_type=F32).astype(BF)
            return carry

        lax.fori_loop(begin, end, one, 0)


    rows, columns = got.shape[-2] // 2, got.shape[-1] // 2
    units = [
        [
            Eighth(
                mail, at, got.at[j], (u // 2 * rows, rows), (u % 2 * columns, columns), ORDERS[j][u],
                landings[(4 * j + u) * 5 : (4 * j + u) * 5 + 5], ways,
            )
            for u in range(4)
        ]
        for j in range(2)
    ]
    every = [unit for group in units for unit in group]
    for j in range(2):
        joined(j)
        for unit in units[j]:
            unit.one()
    unsort(0, 4)
    for phase in range(3):
        for u, unit in enumerate(every):
            unit.two()
            if u % 4 == 3:
                unsort(4 + 4 * phase + u // 4, 5 + 4 * phase + u // 4)
        for u, unit in enumerate(every):
            unit.three()
            if u % 4 == 3:
                unsort(6 + 4 * phase + u // 4, 7 + 4 * phase + u // 4)
    for j in range(2):
        for u, unit in enumerate(units[j]):
            out[unit.row[0] : unit.row[0] + rows, j, unit.column[0] : unit.column[0] + columns] = unit.result()

    def sent(i, carry):
        swap(i // 8, lax.rem(i, 8)).wait_send()
        return carry

    lax.fori_loop(0, 16, sent, 0)
    mail.drain()


def scatter_grads(place, terms, back):
    width = back.shape[1]
    total = place.shape[1]
    rows = width // 16
    terms = terms.reshape(2, 2, 4, 2, 4, 2, rows, width)
    v = lambda *lead: pltpu.VMEM((*lead, rows, width), BF)
    vmem = pl.BlockSpec(memory_space=pltpu.VMEM)
    return pl.pallas_call(
        scatter_kernel,
        out_shape=(jax.ShapeDtypeStruct((rows, 2, width), F32), jax.ShapeDtypeStruct((total, width), BF)),
        in_specs=[vmem, vmem, vmem],
        out_specs=(vmem, vmem),
        scratch_shapes=[
            v(2, 2, 4, 2, 4),
            *(
                pltpu.VMEM(shape, BF)
                for group in ORDERS
                for order in group
                for shape in landing_shapes(order, rows // 2, width // 2)
            ),
            pltpu.SemaphoreType.DMA((2, 8)),
            pltpu.SemaphoreType.DMA((2, 8)),
            pltpu.SemaphoreType.DMA((88,)),
            pltpu.SemaphoreType.DMA((88,)),
        ],
        compiler_params=pltpu.CompilerParams(
            collective_id=1, has_side_effects=True, vmem_limit_bytes=30 << 20
        ),
        name="scatter_grads",
    )(place, terms, back)


def shards(source_rows, rel_ids, relations, entities, pos_slot, negatives):
    rows = source_rows.shape[0]
    matrices, sorted_rows, packed, place, starts = gather_relations(
        relations,
        rel_ids.reshape(1, rows),
        source_rows,
        jnp.transpose(negatives, (0, 2, 1)),
        pos_slot.reshape(1, rows),
    )
    queries = make_queries(starts, sorted_rows, matrices)
    state, query_grad = run_stops(queries, packed, entities)
    back, terms, state = make_grads(starts, sorted_rows, query_grad, matrices, state)
    relation_grad, source_grad = scatter_grads(place, terms, back)
    return (state, source_grad, relation_grad)


def solution(mesh):
    placed = (
        P(("cand", "rel"), None),
        P(("cand", "rel"), None),
        P("rel", None, None),
        P(("cand", "rel"), None),
        P(("cand", "rel")),
        P(None, ("cand", "rel"), None),
    )
    return jax.shard_map(
        shards,
        mesh=mesh,
        in_specs=placed,
        out_specs=(P(("cand", "rel"), None), P(("cand", "rel"), None), P("cand", "rel", None)),
        check_vma=False,
    )
```
